256 devices in a mesh: tm: 32 (over x, z), freq: 2 (over core), rec: 4 (over y).
Axes of the slice: x: 4, y: 4, z: 8, core: 2. Of those that a mesh axis runs over, the one named last changes fastest.
Arguments:
- tokens: bfloat16 [10240, 768], P(('rec', 'tm', 'freq')), parts along dimension 0, may hold values from -6 to 6
- placement: int32 [2, 10240], P(None, ('rec', 'tm', 'freq')), parts along dimension 1, may hold values from 0 to 1599, as said below
- patch_mask: int32 [6400, 8], P(('rec', 'tm'), 'freq'), parts along dimension 0, may hold values from 0 to 1, as said below
- targets: bfloat16 [6400, 8, 256], P(('rec', 'tm'), 'freq'), parts along dimension 0, may hold values from -6 to 6
- in_weight: bfloat16 [768, 384], replicated, may hold values from -0.21875 to 0.21875
- mask_token: bfloat16 [384], replicated, may hold values from -5 to 5
- conv_weight: bfloat16 [2, 3456, 384], replicated, may hold values from -0.109375 to 0.109375
- head_weight: bfloat16 [384, 256], replicated, may hold values from -0.3125 to 0.3125
Outputs:
- prediction: bfloat16 [6400, 8, 256], P(('rec', 'tm'), 'freq'), parts along dimension 0
- token_grad: float32 [10240, 768], P(('rec', 'tm', 'freq')), parts along dimension 0
- conv_grad: float32 [8, 3456, 384], P('rec', ('tm', 'freq')), parts along dimension 0
The draws below stay inside these ranges and needn't reach their ends.
There are 4 independent parts, one for each index of `rec`. The reference program is written for one: setup_inputs(seed, part) draws one part's arguments, and reference() takes and returns one part's arrays. A program takes and returns all parts, laid end to end along the dimension named above; an argument that names none is the same for every part. Nothing has to cross between parts.
Inputs may be any that keep to these rules, and one draw needn't show every extreme that they name: `patch_mask`: exactly 2560 patches are visible; each tile of 50 x 4 patches (tile index = time tile times 2 plus frequency tile) holds at most 80 visible ones, a bound reached in every draw. `placement`: every visible patch is named by exactly one token, no masked patch by any; the first row stays below 1600 and the second below 8; the 40 tokens of one shard name at most 2 patches of any one tile, a bound reached in every draw.
All inputs are finite; a program needn't handle non-finite values.
Results may differ from the reference program's by a relative error of at most 0.0085.
Values may be sent and summed in bfloat16 or wider, within the bound.
No kernel may reach another device: no remote copies, remote signals or barrier semaphores. Data moves between devices by JAX's collectives and lax.ppermute only.
A program may use at most 64 MiB of HBM per device.

```python
import jax
import jax.numpy as jnp
from jax import lax

D_ENC = 768
CHANNELS = 384
PIX = 256
FREQS = 8
LAYERS = 2
TIME_PATCHES = 50
TIME = 1600
FREQ_PATCHES = 4
TILE_COUNT = 64
VIS_DEV = 40
VIS_TOTAL = 2560
N_TM = 32
N_FREQ = 2


def tile_layout(key):
    base_offset = jax.random.fold_in(key, 4099)
    key_ranking, key_surplus, key_reward, key_equality = jax.random.split(base_offset, 4)
    grid_cells = TIME_PATCHES * FREQ_PATCHES
    pairing = jax.random.permutation(key_ranking, TILE_COUNT)
    excess = jax.random.randint(key_surplus, (TILE_COUNT // 2,), 0, VIS_DEV + 1)
    excess = excess.at[0].set(VIS_DEV)
    counts = jnp.zeros((TILE_COUNT,), jnp.int32)
    counts = counts.at[pairing[0::2]].set(VIS_DEV + excess).at[pairing[1::2]].set(VIS_DEV - excess)
    block_reward = jax.random.randint(key_reward, (TILE_COUNT, TIME_PATCHES // 5, 1, FREQ_PATCHES // 2, 1), 0, 5)
    block_reward = jnp.broadcast_to(block_reward, (TILE_COUNT, TIME_PATCHES // 5, 5, FREQ_PATCHES // 2, 2)).reshape(TILE_COUNT, grid_cells)
    equality_breaker = jax.vmap(lambda sub_key: jax.random.permutation(sub_key, grid_cells))(jax.random.split(key_equality, TILE_COUNT))
    score_values = block_reward * grid_cells + equality_breaker
    cell_rank = jnp.argsort(jnp.argsort(-score_values, axis=1, stable=True), axis=1, stable=True)
    visible = (cell_rank < counts[:, None]).astype(jnp.int32)
    position = jnp.cumsum(visible, axis=1) - visible
    offset = jnp.cumsum(counts) - counts
    serial = offset[:, None] + position
    column = serial % TILE_COUNT * VIS_DEV + serial // TILE_COUNT
    column = jnp.where(visible == 1, column, VIS_TOTAL)
    tile_ids = jnp.arange(TILE_COUNT)[:, None]
    cell_ids = jnp.arange(grid_cells)[None, :]
    grid_rows = tile_ids // N_FREQ * TIME_PATCHES + cell_ids // FREQ_PATCHES
    grid_cols = tile_ids % N_FREQ * FREQ_PATCHES + cell_ids % FREQ_PATCHES
    return (visible, column, grid_rows, grid_cols)


def draw_placement(key, part):
    visible, column, grid_rows, grid_cols = tile_layout(key)
    flat = column.reshape(-1)
    row_values = jnp.broadcast_to(grid_rows, column.shape).reshape(-1).astype(jnp.int32)
    col_values = jnp.broadcast_to(grid_cols, column.shape).reshape(-1).astype(jnp.int32)
    row_out = jnp.zeros((VIS_TOTAL + 1,), jnp.int32).at[flat].set(row_values)
    col_out = jnp.zeros((VIS_TOTAL + 1,), jnp.int32).at[flat].set(col_values)
    return jnp.stack([row_out[:VIS_TOTAL], col_out[:VIS_TOTAL]])


def draw_patch_mask(key, part):
    visible, column, grid_rows, grid_cols = tile_layout(key)
    hidden_grid = (1 - visible).reshape(N_TM, N_FREQ, TIME_PATCHES, FREQ_PATCHES)
    return hidden_grid.transpose(0, 2, 1, 3).reshape(TIME, FREQS).astype(jnp.int32)


def draw_mask_token(key, part):
    token_key = jax.random.fold_in(key, 7331)
    values = jnp.clip(jax.random.normal(token_key, (CHANNELS,), jnp.float32), -5.0, 5.0)
    return values.astype(jnp.bfloat16)


def block_levels(key, shape, shards, low, top_value):
    loudness, own = 1.0, jax.random.fold_in(key, 6)
    for dim, blocks in shards:
        heights = jnp.exp(jax.random.uniform(jax.random.fold_in(own, dim), (blocks,), jnp.float32, low / len(shards), top_value / len(shards)))
        loudness = loudness * jnp.repeat(heights, shape[dim] // blocks).reshape([-1 if axis == dim else 1 for axis in range(len(shape))])
    return loudness


def noise(key, extent, scale, limit, shards=(), kind=jnp.bfloat16):
    values = scale * jax.random.normal(key, extent, jnp.float32)
    if shards:
        values = values * block_levels(key, extent, shards, -0.22, 0.18)
    return jnp.clip(values, -limit, limit).astype(kind)


def setup_inputs(seed: int = 0, part: int = 0) -> dict:
    splits = jax.random.split(jax.random.key(seed), 9)
    part_splits = jax.random.split(jax.random.fold_in(splits[8], part), 9)
    return {
        "tokens": noise(part_splits[0], (VIS_TOTAL, D_ENC), 1.0, 6.0, ((0, 64),)),
        "placement": draw_placement(jax.random.fold_in(jax.random.fold_in(splits[8], part), 71), part),
        "patch_mask": draw_patch_mask(jax.random.fold_in(jax.random.fold_in(splits[8], part), 71), part),
        "targets": noise(part_splits[3], (TIME, FREQS, PIX), 1.0, 6.0, ((0, 32), (1, 2))),
        "in_weight": noise(splits[4], (D_ENC, CHANNELS), D_ENC ** -0.5, 0.21875),
        "mask_token": draw_mask_token(jax.random.fold_in(splits[8], 71), part),
        "conv_weight": noise(splits[6], (LAYERS, 9 * CHANNELS, CHANNELS), (9 * CHANNELS) ** -0.5, 0.109375),
        "head_weight": noise(splits[7], (CHANNELS, PIX), CHANNELS ** -0.5, 0.3125),
    }


def norm_gelu(conv_out):
    center = conv_out - lax.optimization_barrier(jnp.mean(conv_out, axis=-1, keepdims=True))
    spread = lax.optimization_barrier(jnp.mean(center * center, axis=-1, keepdims=True))
    return jax.nn.gelu(center * lax.rsqrt(spread + 1e-05), approximate=False)

def contract_rows(left, right):
    return lax.dot_general(left, right, (((0,), (0,)), ((), ())), preferred_element_type=jnp.float32)

def contract_cols(left, right):
    return lax.dot_general(left, right, (((1,), (1,)), ((), ())), preferred_element_type=jnp.float32)

def conv_taps(padded, weight):
    time_rows = padded.shape[0] - 2
    freq_cols = padded.shape[1] - 2
    channels = padded.shape[2]
    summed = jnp.zeros((time_rows * freq_cols, weight.shape[1]), jnp.float32)
    for tap_idx in range(9):
        row_off, col_off = (tap_idx // 3, tap_idx % 3)
        window = padded[row_off:row_off + time_rows, col_off:col_off + freq_cols].reshape(-1, channels)
        summed = summed + jnp.dot(window, weight[tap_idx * channels:(tap_idx + 1) * channels], preferred_element_type=jnp.float32)
    return summed

def conv_back(grad_pad, weight):
    time_rows = grad_pad.shape[0] - 2
    freq_cols = grad_pad.shape[1] - 2
    channels = weight.shape[1]
    summed = jnp.zeros((time_rows * freq_cols, channels), jnp.float32)
    for tap_idx in range(9):
        row_off, col_off = (tap_idx // 3, tap_idx % 3)
        window = grad_pad[2 - row_off:2 - row_off + time_rows, 2 - col_off:2 - col_off + freq_cols].reshape(-1, channels)
        summed = summed + contract_cols(window, weight[tap_idx * channels:(tap_idx + 1) * channels])
    return summed

def weight_term(padded, grad_conv):
    time_rows = padded.shape[0] - 2
    freq_cols = padded.shape[1] - 2
    channels = padded.shape[2]
    blocks = []
    for tap_idx in range(9):
        row_off, col_off = (tap_idx // 3, tap_idx % 3)
        window = padded[row_off:row_off + time_rows, col_off:col_off + freq_cols].reshape(-1, channels)
        blocks.append(contract_rows(window, grad_conv))
    return jnp.concatenate(blocks, axis=0)

def pad_grid(values):
    return jnp.pad(values, ((1, 1), (1, 1), (0, 0)))

def reference(tokens, placement, patch_mask, targets, in_weight, mask_token, conv_weight, head_weight):
    channels = in_weight.shape[1]
    grid_rows = placement[0]
    grid_cols = placement[1]
    proj = jnp.dot(tokens, in_weight, preferred_element_type=jnp.float32).astype(jnp.bfloat16)
    placed = jnp.zeros((TIME, FREQS, channels), jnp.bfloat16).at[grid_rows, grid_cols].set(proj)
    masked = (patch_mask == 1).reshape(-1, 1)
    current = jnp.where(masked, mask_token.astype(jnp.float32)[None, :], placed.reshape(-1, channels).astype(jnp.float32)).astype(jnp.bfloat16)
    stored = []
    for layer_idx in range(LAYERS):
        padded = pad_grid(current.reshape(TIME, FREQS, channels))
        conv_out = conv_taps(padded, conv_weight[layer_idx])
        stored.append((padded, conv_out))
        current = (current.astype(jnp.float32) + norm_gelu(conv_out)).astype(jnp.bfloat16)
    predicted = jnp.dot(current, head_weight, preferred_element_type=jnp.float32)
    prediction = predicted.astype(jnp.bfloat16).reshape(TIME, FREQS, -1)
    misfit = jnp.where(masked, (predicted - targets.reshape(TIME * FREQS, -1).astype(jnp.float32)) / 16.0, 0.0)
    gradient = contract_cols(misfit.astype(jnp.bfloat16), head_weight)
    grad_terms = [None] * LAYERS
    for layer_idx in reversed(range(LAYERS)):
        padded, conv_out = stored[layer_idx]
        _, pull_back = jax.vjp(norm_gelu, conv_out)
        grad_conv = pull_back(gradient)[0].astype(jnp.bfloat16)
        grad_terms[layer_idx] = weight_term(padded, grad_conv)
        grad_pad = pad_grid(grad_conv.reshape(TIME, FREQS, channels))
        gradient = gradient + conv_back(grad_pad, conv_weight[layer_idx])
    grad_grid = gradient.astype(jnp.bfloat16).reshape(TIME, FREQS, channels)
    grad_proj = grad_grid[grid_rows, grid_cols]
    token_grad = contract_cols(grad_proj, in_weight)
    return (prediction, token_grad, jnp.stack(grad_terms))
```

```python
import jax
import jax.numpy as jnp
from jax import lax
from jax.experimental import pallas as pl
from jax.experimental.pallas import tpu as pltpu
from jax.sharding import Mesh
from jax.sharding import PartitionSpec as P

TM = ("tm_0", "tm_1")
TM_FREQ = ("tm_0", "tm_1", "freq")
REC_TM_FREQ = ("rec", "tm_0", "tm_1", "freq")
REC_TM = ("rec", "tm_0", "tm_1")

F32 = jnp.float32
BF16 = jnp.bfloat16
ROWS = 50
COLS = 8
CELLS = ROWS * COLS
CHANNELS = 384
DEPTH = 3 * CHANNELS
PIX = 256
SLOTS = 4
ERF_SCALE = 0.7071067811865476
PDF_SCALE = 0.3989422804014327
ERF_TOP = (
    0.00022905065861350646,
    0.0034082910107109506,
    0.050955695062380861,
    0.18520832239976145,
    1.128379143519084,
)
ERF_BOTTOM = (
    -1.1791602954361697e-7,
    0.000023547966471313185,
    0.0010179625278914885,
    0.014070470171167667,
    0.11098505178285362,
    0.49746925110067538,
    1.0,
)


def horner(value, factors):
    total = jnp.full_like(value, factors[0])
    for factor in factors[1:]:
        total = total * value + factor
    return total


def erf(value):
    bounded = jnp.clip(value, -3.7439211627767994, 3.7439211627767994)
    square = bounded * bounded
    return bounded * horner(square, ERF_TOP) / horner(square, ERF_BOTTOM)


def half_erf(unit):
    return 0.5 * (1.0 + erf(unit * ERF_SCALE))


def column_shifted(value):
    cells, channels = value.shape
    grid = value.reshape(cells // 8, 8, channels)
    column = lax.broadcasted_iota(jnp.int32, grid.shape, 1)
    lower = jnp.where(column == 0, 0.0, pltpu.roll(grid, 1, axis=1))
    upper = jnp.where(column == 7, 0.0, pltpu.roll(grid, 7, axis=1))
    return lower.reshape(value.shape), value, upper.reshape(value.shape)


def store_columns(value, even, odd):
    cells, channels = value.shape
    for part, shifted in enumerate(column_shifted(value)):
        lanes = slice(part * channels, (part + 1) * channels)
        even[0:cells, lanes] = shifted.astype(BF16)
        odd[0 : cells - 8, lanes] = shifted[8:].astype(BF16)


def conv_taps(even, odd, weight, cells):
    summed = jnp.dot(even[0:cells], weight[0, 0:DEPTH], preferred_element_type=F32)
    summed += jnp.dot(odd[0:cells], weight[0, DEPTH : 2 * DEPTH], preferred_element_type=F32)
    summed += jnp.dot(
        even[16 : 16 + cells], weight[0, 2 * DEPTH : 3 * DEPTH], preferred_element_type=F32
    )
    return summed


def conv_back(grad, weight, cells):
    summed = None
    for row_off in range(3):
        term = lax.dot_general(
            grad,
            weight[0, row_off * DEPTH : (row_off + 1) * DEPTH],
            (((1,), (1,)), ((), ())),
            preferred_element_type=F32,
        )
        term = term[8 * (2 - row_off) : 8 * (2 - row_off) + cells]
        summed = term if summed is None else summed + term
    grid = (cells // 8, 8, CHANNELS)
    column = lax.broadcasted_iota(jnp.int32, grid, 1)
    first = summed[:, 0:CHANNELS].reshape(grid)
    last = summed[:, 2 * CHANNELS :].reshape(grid)
    total = jnp.where(column == 7, 0.0, pltpu.roll(first, 7, axis=1))
    total += jnp.where(column == 0, 0.0, pltpu.roll(last, 1, axis=1))
    return summed[:, CHANNELS : 2 * CHANNELS] + total.reshape(cells, CHANNELS)


def normed(conv_out):
    center = conv_out - jnp.mean(conv_out, axis=-1, keepdims=True)
    scale = lax.rsqrt(jnp.mean(center * center, axis=-1, keepdims=True) + 1e-05)
    return center * scale, scale


def pull_back(unit, scale, gradient):
    slope = half_erf(unit) + unit * (PDF_SCALE * jnp.exp(-0.5 * unit * unit))
    grad = gradient * slope
    mean = jnp.mean(grad, axis=-1, keepdims=True)
    along = jnp.mean(grad * unit, axis=-1, keepdims=True)
    return scale * (grad - mean - unit * along)


def rows_valid(place_ref, cells, before):
    row = lax.shift_right_logical(lax.broadcasted_iota(jnp.int32, (cells, 1), 0), 3)
    row = row + place_ref[0] * ROWS - before
    return (row >= 0) & (row < place_ref[2] * ROWS)


def place_kernel(arrived, aim, token, x_out, chosen_out):
    notes = arrived[:, CHANNELS : CHANNELS + 128].astype(F32)
    cell = notes[:, 0:1] * 8.0 + notes[:, 1:2]
    cell = jnp.where(notes[:, 2:3] == 1.0, cell, -1.0).astype(jnp.int32)
    slots = arrived.shape[0]
    chosen = jnp.where(lax.broadcasted_iota(jnp.int32, (slots, CELLS), 1) == cell, 1.0, 0.0)
    chosen = chosen.astype(BF16)
    chosen_out[...] = chosen
    placed = lax.dot_general(
        chosen, arrived[:, 0:CHANNELS], (((0,), (0,)), ((), ())), preferred_element_type=F32
    )
    masked = aim[16 : 16 + CELLS, PIX : PIX + 1] == 1.0
    x_out[...] = jnp.where(masked, token[...].astype(F32), placed).astype(BF16)


def first_kernel(
    place_ref, above, own, below, weight, active_out, unit_out, scale_out, share_out, even, odd
):
    source = jnp.concatenate(
        [above[...].astype(F32), own[...].astype(F32), below[...].astype(F32)], axis=0
    )
    store_columns(source, even, odd)
    unit, scale = normed(conv_taps(even, odd, weight, 448))
    unit_out[...] = unit[16:432]
    scale_out[...] = jnp.broadcast_to(scale[16:432], (416, 128))
    active = source[8:456] + unit * half_erf(unit)
    active = jnp.where(rows_valid(place_ref, 448, 3), active, 0.0)
    active_out[...] = active.astype(BF16)
    share_out[...] = jnp.where(place_ref[1] == 1, active[16:432], source[24:440]).astype(BF16)


def second_kernel(
    place_ref, active_ref, unit_ref, scale_ref, weight, head, aim,
    pred, share_out, mid_out, grad_out, even, odd,
):
    active = active_ref[...].astype(F32)
    store_columns(active, even, odd)
    unit, scale = normed(conv_taps(even, odd, weight, 432))
    top = (active[8:440] + unit * half_erf(unit)).astype(BF16)
    guess = jnp.dot(top, head[...], preferred_element_type=F32)
    pred[...] = guess[16:416].astype(BF16)
    misfit = jnp.where(
        aim[:, PIX : PIX + 1] == 1.0, (guess - aim[:, 0:PIX].astype(F32)) * 0.0625, 0.0
    ).astype(BF16)
    grad_top = lax.dot_general(
        misfit, head[...], (((1,), (1,)), ((), ())), preferred_element_type=F32
    )
    grad_two = pull_back(unit, scale, grad_top).astype(BF16)
    grad_mid = grad_top[8:424] + conv_back(grad_two, weight, 416)
    grad_one = pull_back(unit_ref[...], scale_ref[:, 0:1], grad_mid)
    grad_one = jnp.where(rows_valid(place_ref, 416, 1), grad_one, 0.0)
    grad_out[...] = grad_one.astype(BF16)
    mid_out[...] = grad_mid[8:408]
    share_out[...] = jnp.where(
        place_ref[1] == 1, grad_two.astype(F32)[16:416], grad_one[8:408]
    ).astype(BF16)


def tail_kernel(grad_ref, mid_ref, weight, chosen, out):
    grad_cells = mid_ref[...] + conv_back(grad_ref[...], weight, CELLS)
    out[...] = jnp.dot(chosen[...], grad_cells.astype(BF16), preferred_element_type=F32).astype(
        BF16
    )


def weight_kernel(place_ref, *refs):
    inner, outer = refs[0:4], refs[4:8]
    out, turned, moved, total = refs[8:]
    first_tap = place_ref[3] * 2
    for part in range(4):
        turned[part] = inner[part][...].astype(F32).T.astype(BF16)
    moved[...] = jnp.zeros_like(moved)
    for step in range(3):
        tap = first_tap + step
        row_off = jnp.where(tap >= 6, 2, jnp.where(tap >= 3, 1, 0))
        col_off = tap - 3 * row_off
        start = pl.multiple_of(row_off * 8, 8)
        summed = None
        for part in range(4):
            low, middle, high = column_shifted(outer[part][...].astype(F32))
            piece = jnp.where(col_off == 0, high, jnp.where(col_off == 1, middle, low))
            slot = 4 * step + part
            moved[slot, pl.ds(start, CELLS), :] = piece
            term = jnp.dot(
                turned[part], moved[slot].astype(BF16), preferred_element_type=F32
            )
            summed = term if summed is None else summed + term
        total[step * CHANNELS : (step + 1) * CHANNELS] = summed
    base = pl.multiple_of(place_ref[3] * 96, 8)
    kept = total[pl.ds(base, 864), :]
    for block in range(16):
        out[block] = kept[54 * block : 54 * (block + 1)].astype(BF16)


VMEM = pl.BlockSpec(memory_space=pltpu.VMEM)
SMEM = pl.BlockSpec(memory_space=pltpu.SMEM)


def call(kernel, name, shapes, scratch, cost, *operands, scalars=True, specs=None):
    in_specs = [SMEM] + [VMEM] * (len(operands) - 1) if scalars else [VMEM] * len(operands)
    return pl.pallas_call(
        kernel,
        out_shape=shapes,
        in_specs=specs or in_specs,
        out_specs=jax.tree.map(lambda _: VMEM, shapes),
        scratch_shapes=scratch,
        compiler_params=pltpu.CompilerParams(vmem_limit_bytes=56 << 20),
        cost_estimate=pl.CostEstimate(
            flops=cost, bytes_accessed=cost // 400, transcendentals=0
        ),
        name=name,
    )(*operands)


def shape(dims, dtype=BF16):
    return jax.ShapeDtypeStruct(dims, dtype)


def send(value, axis, step, wrap):
    count = lax.axis_size(axis)
    pairs = [(i, (i + step) % count) for i in range(count)]
    if not wrap:
        pairs = [(i, i + step) for i in range(count) if 0 <= i + step < count]
    return lax.ppermute(value, axis, pairs)


def per_device(
    tokens, placement, patch_mask, targets, in_weight, mask_token, conv_weight, head_weight
):
    time_tiles = lax.axis_size(TM)
    shards = time_tiles * lax.axis_size("freq")
    core = lax.axis_index("freq")
    place = jnp.stack(
        [lax.axis_index(TM), core, jnp.int32(time_tiles), lax.axis_index("tm_0")]
    ).astype(jnp.int32)
    half = patch_mask.shape[1]

    grid_rows, grid_cols = placement[0], placement[1]
    target = grid_rows // ROWS * 2 + grid_cols // half
    same = target[:, None] == target[None, :]
    order = jnp.arange(target.shape[0])
    slot = jnp.sum(same & (order[None, :] < order[:, None]), axis=1)
    where_to = target * 2 + slot
    proj = jnp.dot(tokens, in_weight, preferred_element_type=F32).astype(BF16)
    lane = jnp.arange(128)[None, :]
    notes = jnp.where(
        lane == 0,
        (grid_rows % ROWS)[:, None],
        jnp.where(lane == 1, grid_cols[:, None], jnp.where(lane == 2, 1, 0)),
    ).astype(BF16)
    payload = jnp.concatenate([proj, notes], axis=1)
    index = jnp.arange(shards * SLOTS)
    wanted = index // (2 * SLOTS) * SLOTS + index % SLOTS
    sender = (wanted[:, None] == where_to[None, :]).astype(BF16)
    packed = jnp.dot(sender, payload, preferred_element_type=F32).astype(BF16)
    arrived = lax.all_to_all(
        packed.reshape(shards, SLOTS, -1), TM_FREQ, split_axis=0, concat_axis=0, tiled=True
    ).reshape(shards * SLOTS, -1)

    flags = jnp.broadcast_to((patch_mask == 1)[:, :, None], (*patch_mask.shape, 128))
    aim = jnp.concatenate([targets, flags.astype(BF16)], axis=2)
    other = send(aim, "freq", 1, True)
    aim = jnp.where(
        core == 0, jnp.concatenate([aim, other], axis=1), jnp.concatenate([other, aim], axis=1)
    )
    aim = jnp.concatenate(
        [send(aim[-2:], TM, 1, False), aim, send(aim[:2], TM, -1, False)], axis=0
    ).reshape(-1, PIX + 128)

    own, chosen = call(
        place_kernel,
        "place",
        (shape((CELLS, CHANNELS)), shape((shards * SLOTS, CELLS))),
        [],
        80_000_000,
        arrived,
        aim,
        mask_token[None, :],
        scalars=False,
    )
    above = send(own[-32:], TM, 1, False)
    below = send(own[:32], TM, -1, False)
    weights = [conv_weight[layer : layer + 1] for layer in range(2)]
    columns = [pltpu.VMEM((464, DEPTH), BF16), pltpu.VMEM((464, DEPTH), BF16)]
    active, unit, scale, inner = call(
        first_kernel,
        "first",
        (shape((448, CHANNELS)), shape((416, CHANNELS), F32), shape((416, 128), F32), shape((416, CHANNELS))),
        columns,
        1_500_000_000,
        place,
        above,
        own,
        below,
        weights[0],
    )
    inners = [inner] + [send(inner, "tm_0", step, True) for step in (1, 2, 3)]
    pred, outer, mid, grad = call(
        second_kernel,
        "second",
        (shape((CELLS, PIX)), shape((CELLS, CHANNELS)), shape((CELLS, CHANNELS), F32), shape((416, CHANNELS))),
        columns,
        3_500_000_000,
        place,
        active,
        unit,
        scale,
        weights[1],
        head_weight,
        aim,
    )
    outers = [outer] + [send(outer, "tm_0", step, True) for step in (1, 2, 3)]

    outgoing = call(
        tail_kernel,
        "tail",
        shape((shards * SLOTS, CHANNELS)),
        [],
        1_200_000_000,
        grad,
        mid,
        weights[0],
        chosen,
        scalars=False,
    )
    outgoing = lax.dynamic_index_in_dim(
        outgoing.reshape(shards, 2, 2, CHANNELS), core, axis=1, keepdims=False
    )
    returned = lax.all_to_all(outgoing, TM_FREQ, split_axis=0, concat_axis=0, tiled=True)
    taken = (jnp.arange(shards * 2)[None, :] == where_to[:, None]).astype(BF16)
    grad_proj = jnp.dot(
        taken, returned.reshape(shards * 2, -1), preferred_element_type=F32
    ).astype(BF16)
    token_grad = lax.dot_general(
        grad_proj, in_weight, (((1,), (1,)), ((), ())), preferred_element_type=F32
    )

    terms = call(
        weight_kernel,
        "weight",
        shape((16, 54, CHANNELS)),
        [
            pltpu.VMEM((4, CHANNELS, 416), BF16),
            pltpu.VMEM((12, 416, CHANNELS), F32),
            pltpu.VMEM((DEPTH, CHANNELS), F32),
        ],
        1_500_000_000,
        place,
        *inners,
        *outers,
    )
    terms = lax.all_to_all(terms, ("tm_1", "freq"), split_axis=0, concat_axis=0, tiled=True)
    conv_grad = terms.reshape(-1, 2, 54, CHANNELS).astype(F32).sum(axis=0)
    pred = lax.dynamic_slice_in_dim(pred.reshape(ROWS, COLS, PIX), core * half, half, axis=1)
    return (pred, token_grad, conv_grad)


def solution(mesh):
    split = Mesh(
        mesh.devices.reshape(4, 8, mesh.shape["freq"], mesh.shape["rec"]),
        ("tm_0", "tm_1", "freq", "rec"),
    )
    placed = (
        P(REC_TM_FREQ, None),
        P(None, REC_TM_FREQ),
        P(REC_TM, "freq"),
        P(REC_TM, "freq", None),
        P(),
        P(),
        P(),
        P(),
    )
    return jax.shard_map(
        per_device,
        mesh=split,
        in_specs=placed,
        out_specs=(P(REC_TM, "freq", None), P(REC_TM_FREQ, None), P("rec", TM_FREQ, None)),
        check_vma=False,
    )
```

```python
import jax
import jax.numpy as jnp
from jax import lax
from jax.experimental import pallas as pl
from jax.experimental.pallas import tpu as pltpu
from jax.sharding import Mesh
from jax.sharding import PartitionSpec as P


TM = ("tm_0", "tm_1")
TM_FREQ = ("tm_0", "tm_1", "freq")
REC_TM_FREQ = ("rec", "tm_0", "tm_1", "freq")
REC_TM = ("rec", "tm_0", "tm_1")

F32 = jnp.float32
BF16 = jnp.bfloat16
ROWS = 50
COLS = 8
CELLS = ROWS * COLS
CHANNELS = 384
DEPTH = 3 * CHANNELS
PIX = 256
ERF_SCALE = 0.7071067811865476
PDF_SCALE = 0.3989422804014327
ERF_TOP = (
    0.00022905065861350646,
    0.0034082910107109506,
    0.050955695062380861,
    0.18520832239976145,
    1.128379143519084,
)
ERF_BOTTOM = (
    -1.1791602954361697e-7,
    0.000023547966471313185,
    0.0010179625278914885,
    0.014070470171167667,
    0.11098505178285362,
    0.49746925110067538,
    1.0,
)


def horner(value, factors):
    total = jnp.full_like(value, factors[0])
    for factor in factors[1:]:
        total = total * value + factor
    return total


def erf(value):
    bounded = jnp.clip(value, -3.7439211627767994, 3.7439211627767994)
    square = bounded * bounded
    return bounded * horner(square, ERF_TOP) / horner(square, ERF_BOTTOM)


def half_erf(unit):
    return 0.5 * (1.0 + erf(unit * ERF_SCALE))


def column_shifted(value):
    cells, channels = value.shape
    grid = value.reshape(cells // 8, 8, channels)
    column = lax.broadcasted_iota(jnp.int32, grid.shape, 1)
    lower = jnp.where(column == 0, 0.0, pltpu.roll(grid, 1, axis=1))
    upper = jnp.where(column == 7, 0.0, pltpu.roll(grid, 7, axis=1))
    return lower.reshape(value.shape), value, upper.reshape(value.shape)


def store_columns(value, even, odd):
    cells, channels = value.shape
    for part, shifted in enumerate(column_shifted(value)):
        lanes = slice(part * channels, (part + 1) * channels)
        even[0:cells, lanes] = shifted.astype(BF16)
        odd[0 : cells - 8, lanes] = shifted[8:].astype(BF16)


def conv_taps(even, odd, weight, cells):
    summed = jnp.dot(even[0:cells], weight[0, 0:DEPTH], preferred_element_type=F32)
    summed += jnp.dot(odd[0:cells], weight[0, DEPTH : 2 * DEPTH], preferred_element_type=F32)
    summed += jnp.dot(
        even[16 : 16 + cells], weight[0, 2 * DEPTH : 3 * DEPTH], preferred_element_type=F32
    )
    return summed


def conv_back(grad, weight, cells):
    summed = None
    for row_off in range(3):
        term = lax.dot_general(
            grad,
            weight[0, row_off * DEPTH : (row_off + 1) * DEPTH],
            (((1,), (1,)), ((), ())),
            preferred_element_type=F32,
        )
        term = term[8 * (2 - row_off) : 8 * (2 - row_off) + cells]
        summed = term if summed is None else summed + term
    grid = (cells // 8, 8, CHANNELS)
    column = lax.broadcasted_iota(jnp.int32, grid, 1)
    first = summed[:, 0:CHANNELS].reshape(grid)
    last = summed[:, 2 * CHANNELS :].reshape(grid)
    total = jnp.where(column == 7, 0.0, pltpu.roll(first, 7, axis=1))
    total += jnp.where(column == 0, 0.0, pltpu.roll(last, 1, axis=1))
    return summed[:, CHANNELS : 2 * CHANNELS] + total.reshape(cells, CHANNELS)


def normed(conv_out):
    center = conv_out - jnp.mean(conv_out, axis=-1, keepdims=True)
    scale = lax.rsqrt(jnp.mean(center * center, axis=-1, keepdims=True) + 1e-05)
    return center * scale, scale


def pull_back(unit, scale, gradient):
    slope = half_erf(unit) + unit * (PDF_SCALE * jnp.exp(-0.5 * unit * unit))
    grad = gradient * slope
    mean = jnp.mean(grad, axis=-1, keepdims=True)
    along = jnp.mean(grad * unit, axis=-1, keepdims=True)
    return scale * (grad - mean - unit * along)


def rows_valid(cells, before):
    row = lax.shift_right_logical(lax.broadcasted_iota(jnp.int32, (cells, 1), 0), 3)
    row = row + lax.axis_index(TM) * ROWS - before
    return (row >= 0) & (row < lax.axis_size(TM) * ROWS)


def pack_kernel(tokens, placement, in_weight, packed, where_out):
    count = tokens.shape[0]
    rows = placement[0:1, :].astype(F32)
    cols = placement[1:2, :].astype(F32)
    tile_row = jnp.floor((rows + 0.5) * (1.0 / ROWS))
    tile = tile_row * 2.0 + jnp.where(cols >= 4.0, 1.0, 0.0)
    down = lax.broadcasted_iota(jnp.int32, (count, count), 0)
    across = lax.broadcasted_iota(jnp.int32, (count, count), 1)

    def column(value):
        return jnp.sum(jnp.where(down == across, value, 0.0), axis=1, keepdims=True)

    earlier = jnp.where((column(tile) == tile) & (down < across), 1.0, 0.0)
    where_to = tile * 2.0 + jnp.sum(earlier, axis=0, keepdims=True)
    where_out[...] = jnp.broadcast_to(column(where_to), where_out.shape)
    index = lax.broadcasted_iota(jnp.int32, (packed.shape[0], 1), 0)
    wanted = lax.shift_right_logical(index, 4) * 4 + (index & 3)
    match = jnp.where(wanted.astype(F32) == where_to, 1.0, 0.0).astype(BF16)
    proj = jnp.dot(tokens[...], in_weight[...], preferred_element_type=F32).astype(BF16)
    lane = lax.broadcasted_iota(jnp.int32, (count, 128), 1)
    notes = jnp.where(lane == 1, column(cols), jnp.where(lane == 2, 1.0, 0.0))
    notes = jnp.where(lane == 0, column(rows - tile_row * ROWS), notes).astype(BF16)
    low = jnp.dot(match, proj[:, 0:256], preferred_element_type=F32)
    rest = jnp.concatenate([proj[:, 256:384], notes], axis=1)
    high = jnp.dot(match, rest, preferred_element_type=F32)
    packed[...] = jnp.where((index & 4) == 0, low, high).astype(BF16)


def place_kernel(arrived, own_aim, other_aim, token, x_out, aim_out, down_out, up_out, chosen_out):
    core = lax.axis_index("freq")
    slots = arrived.shape[0]
    notes = arrived[:, 128:256].astype(F32).reshape(slots // 8, 8, 128)
    within = lax.broadcasted_iota(jnp.int32, notes.shape, 1)
    notes = jnp.where(within >= 4, notes, pltpu.roll(notes, 4, axis=1)).reshape(slots, 128)
    cell = jnp.where(notes[:, 2:3] == 1.0, notes[:, 0:1] * 8.0 + notes[:, 1:2], -1.0)
    lane = lax.broadcasted_iota(jnp.int32, (slots, CELLS), 1)
    index = lax.broadcasted_iota(jnp.int32, (slots, CELLS), 0)
    hit = lane == cell.astype(jnp.int32)

    def pick(flag):
        return lax.dot_general(
            jnp.where(hit & flag, 1.0, 0.0).astype(BF16),
            arrived[...],
            (((0,), (0,)), ((), ())),
            preferred_element_type=F32,
        )

    placed = jnp.concatenate([pick((index & 4) == 0), pick((index & 4) == 4)[:, 0:128]], axis=1)
    number = lax.broadcasted_iota(jnp.int32, (CELLS, 1), 0)
    far = (lax.shift_right_logical(number, 2) & 1) != core
    source = lax.shift_right_logical(number, 3) * 4 + (number & 3) + jnp.where(far, CELLS // 2, 0)
    order = lax.broadcasted_iota(jnp.int32, (CELLS, CELLS), 1) == source
    aim = jnp.dot(
        jnp.where(order, 1.0, 0.0).astype(BF16),
        jnp.concatenate([own_aim[...].astype(F32), other_aim[...].astype(F32)], axis=0).astype(BF16),
        preferred_element_type=F32,
    )
    x = jnp.where(aim[:, PIX : PIX + 1] == 1.0, token[...].astype(F32), placed)
    x_out[...] = x.astype(BF16)
    aim_out[...] = aim.astype(BF16)
    down_out[...] = jnp.concatenate([x[CELLS - 32 :], aim[CELLS - 16 :]], axis=0).astype(BF16)
    up_out[...] = jnp.concatenate([x[0:32], aim[0:16]], axis=0).astype(BF16)
    spread = jnp.broadcast_to(cell, (slots, 128)).reshape(slots // 8, 8, 128)
    first = jnp.sum(jnp.where(within == 4 + 2 * core, spread, 0.0), axis=1, keepdims=True)
    second = jnp.sum(jnp.where(within == 5 + 2 * core, spread, 0.0), axis=1, keepdims=True)
    spread = jnp.where((within & 1) == 0, first, second)
    spread = jnp.where(within < 6, spread, -1.0).reshape(slots, 128)
    chosen_out[...] = jnp.where(lane == spread[:, 0:1].astype(jnp.int32), 1.0, 0.0).astype(BF16)


def first_kernel(
    above, own, below, weight, active_out, unit_out, scale_out, share_out, even, odd
):
    source = jnp.concatenate(
        [above[0:32].astype(F32), own[...].astype(F32), below[0:32].astype(F32)], axis=0
    )
    store_columns(source, even, odd)
    unit, scale = normed(conv_taps(even, odd, weight, 448))
    unit_out[...] = unit[16:432]
    scale_out[...] = jnp.broadcast_to(scale[16:432], (416, 128))
    active = source[8:456] + unit * half_erf(unit)
    active = jnp.where(rows_valid(448, 3), active, 0.0)
    active_out[...] = active.astype(BF16)
    share_out[...] = jnp.where(lax.axis_index("freq") == 1, active[16:432], source[24:440]).astype(BF16)


def second_kernel(
    active_ref, unit_ref, scale_ref, weight, head, above, aim_ref, below,
    pred, share_out, mid_out, grad_out, even, odd,
):
    active = active_ref[...].astype(F32)
    store_columns(active, even, odd)
    unit, scale = normed(conv_taps(even, odd, weight, 432))
    top = (active[8:440] + unit * half_erf(unit)).astype(BF16)
    guess = jnp.dot(top, head[...], preferred_element_type=F32)
    pred[...] = guess[16:416].astype(BF16)
    aim = jnp.concatenate([above[32:48], aim_ref[...], below[32:48]], axis=0)
    misfit = jnp.where(
        aim[:, PIX : PIX + 1] == 1.0, (guess - aim[:, 0:PIX].astype(F32)) * 0.0625, 0.0
    ).astype(BF16)
    grad_top = lax.dot_general(
        misfit, head[...], (((1,), (1,)), ((), ())), preferred_element_type=F32
    )
    grad_two = pull_back(unit, scale, grad_top).astype(BF16)
    grad_mid = grad_top[8:424] + conv_back(grad_two, weight, 416)
    grad_one = pull_back(unit_ref[...], scale_ref[:, 0:1], grad_mid)
    grad_one = jnp.where(rows_valid(416, 1), grad_one, 0.0)
    grad_out[...] = grad_one.astype(BF16)
    mid_out[...] = grad_mid[8:408]
    share_out[...] = jnp.where(
        lax.axis_index("freq") == 1, grad_two.astype(F32)[16:416], grad_one[8:408]
    ).astype(BF16)


def tail_kernel(grad_ref, mid_ref, weight, chosen, out):
    grad_cells = mid_ref[...] + conv_back(grad_ref[...], weight, CELLS)
    picked = jnp.dot(chosen[...], grad_cells.astype(BF16), preferred_element_type=F32)
    part = lax.broadcasted_iota(jnp.int32, out.shape, 0) & 6
    picked = jnp.where(
        part == 0, picked[:, 0:128], jnp.where(part == 2, picked[:, 128:256], picked[:, 256:384])
    )
    out[...] = picked.astype(BF16)


def finish_kernel(returned, where_ref, in_weight, out):
    count = where_ref.shape[0]
    slots = returned.shape[0]
    index = lax.broadcasted_iota(jnp.int32, (count, slots), 1)
    slot = lax.shift_right_logical(index, 3) * 2 + (index & 1)
    hit = where_ref[:, 0:1].astype(jnp.int32) == slot
    parts = []
    for part in range(3):
        taken = jnp.where(hit & ((index & 6) == 2 * part), 1.0, 0.0).astype(BF16)
        parts.append(jnp.dot(taken, returned[...], preferred_element_type=F32))
    grad_proj = jnp.concatenate(parts, axis=1).astype(BF16)
    out[...] = lax.dot_general(
        grad_proj, in_weight[...], (((1,), (1,)), ((), ())), preferred_element_type=F32
    )


def weight_kernel(*refs):
    inner, outer = refs[0:4], refs[4:8]
    out, turned, moved, total = refs[8:]
    first_tap = lax.axis_index("tm_0") * 2
    for part in range(4):
        turned[part] = inner[part][...].astype(F32).T.astype(BF16)
    moved[...] = jnp.zeros_like(moved)
    for step in range(3):
        tap = first_tap + step
        row_off = jnp.where(tap >= 6, 2, jnp.where(tap >= 3, 1, 0))
        col_off = tap - 3 * row_off
        start = pl.multiple_of(row_off * 8, 8)
        summed = None
        for part in range(4):
            low, middle, high = column_shifted(outer[part][...].astype(F32))
            piece = jnp.where(col_off == 0, high, jnp.where(col_off == 1, middle, low))
            slot = 4 * step + part
            moved[slot, pl.ds(start, CELLS), :] = piece
            term = jnp.dot(
                turned[part], moved[slot].astype(BF16), preferred_element_type=F32
            )
            summed = term if summed is None else summed + term
        total[step * CHANNELS : (step + 1) * CHANNELS] = summed
    base = pl.multiple_of(lax.axis_index("tm_0") * 96, 8)
    kept = total[pl.ds(base, 864), :]
    for block in range(16):
        out[block] = kept[54 * block : 54 * (block + 1)].astype(BF16)


VMEM = pl.BlockSpec(memory_space=pltpu.VMEM)


def call(kernel, shapes, scratch, cost, limit, *operands):
    return pl.pallas_call(
        kernel,
        out_shape=shapes,
        in_specs=[VMEM] * len(operands),
        out_specs=jax.tree.map(lambda _: VMEM, shapes),
        scratch_shapes=scratch,
        compiler_params=pltpu.CompilerParams(vmem_limit_bytes=limit << 20),
        cost_estimate=pl.CostEstimate(
            flops=cost, bytes_accessed=cost // 400, transcendentals=0
        ),
    )(*operands)


def shape(dims, dtype=BF16):
    return jax.ShapeDtypeStruct(dims, dtype)


def send(value, axis, step, wrap):
    count = lax.axis_size(axis)
    pairs = [(i, (i + step) % count) for i in range(count)]
    if not wrap:
        pairs = [(i, i + step) for i in range(count) if 0 <= i + step < count]
    return lax.ppermute(value, axis, pairs)


def per_device(
    tokens, placement, patch_mask, targets, in_weight, mask_token, conv_weight, head_weight
):
    shards = lax.axis_size(TM_FREQ)
    core = lax.axis_index("freq")
    visible = tokens.shape[0]
    half = patch_mask.shape[1]

    packed, where_to = call(
        pack_kernel,
        (shape((shards * 8, 256)), shape((visible, 128), F32)),
        [],
        80_000_000,
        4,
        tokens,
        placement,
        in_weight,
    )
    arrived = lax.all_to_all(packed, TM_FREQ, split_axis=0, concat_axis=0, tiled=True)

    flags = jnp.broadcast_to((patch_mask == 1)[:, :, None], (*patch_mask.shape, 128))
    aim = jnp.concatenate([targets, flags.astype(BF16)], axis=2).reshape(-1, PIX + 128)
    other = send(aim, "freq", 1, True)

    own, aim, down, up, chosen = call(
        place_kernel,
        (
            shape((CELLS, CHANNELS)),
            shape((CELLS, PIX + 128)),
            shape((48, CHANNELS)),
            shape((48, CHANNELS)),
            shape((shards * 8, CELLS)),
        ),
        [],
        300_000_000,
        8,
        arrived,
        aim,
        other,
        mask_token[None, :],
    )
    above = send(down, TM, 1, False)
    below = send(up, TM, -1, False)
    weights = [conv_weight[layer : layer + 1] for layer in range(2)]
    columns = [pltpu.VMEM((464, DEPTH), BF16), pltpu.VMEM((464, DEPTH), BF16)]
    active, unit, scale, inner = call(
        first_kernel,
        (
            shape((448, CHANNELS)),
            shape((416, CHANNELS), F32),
            shape((416, 128), F32),
            shape((416, CHANNELS)),
        ),
        columns,
        1_500_000_000,
        16,
        above,
        own,
        below,
        weights[0],
    )
    inners = [inner] + [send(inner, "tm_0", step, True) for step in (1, 2, 3)]
    pred, outer, mid, grad = call(
        second_kernel,
        (
            shape((CELLS, PIX)),
            shape((CELLS, CHANNELS)),
            shape((CELLS, CHANNELS), F32),
            shape((416, CHANNELS)),
        ),
        columns,
        3_500_000_000,
24,
        active,
        unit,
        scale,
        weights[1],
        head_weight,
        above,
        aim,
        below,
    )
    outers = [outer] + [send(outer, "tm_0", step, True) for step in (1, 2, 3)]

    outgoing = call(
        tail_kernel, shape((shards * 8, 128)), [], 1_200_000_000, 16, grad, mid, weights[0], chosen
    )
    returned = lax.all_to_all(
        outgoing, TM_FREQ, split_axis=0, concat_axis=0, tiled=True
    )
    terms = call(
        weight_kernel,
        shape((16, 54, CHANNELS)),
        [
            pltpu.VMEM((4, CHANNELS, 416), BF16),
            pltpu.VMEM((12, 416, CHANNELS), F32),
            pltpu.VMEM((DEPTH, CHANNELS), F32),
        ],
        1_500_000_000,
        24,
        *inners,
        *outers,
    )
    terms = lax.all_to_all(terms, ("tm_1", "freq"), split_axis=0, concat_axis=0, tiled=True)
    token_grad = call(
        finish_kernel,
        shape((visible, in_weight.shape[0]), F32),
        [],
        80_000_000,
        4,
        returned,
        where_to,
        in_weight,
    )
    conv_grad = terms.reshape(-1, 2, 54, CHANNELS).astype(F32).sum(axis=0)
    pred = lax.dynamic_slice_in_dim(pred.reshape(ROWS, COLS, PIX), core * half, half, axis=1)
    return (pred, token_grad, conv_grad)


def solution(mesh):
    split = Mesh(
        mesh.devices.reshape(4, 8, mesh.shape["freq"], mesh.shape["rec"]),
        ("tm_0", "tm_1", "freq", "rec"),
    )
    placed = (
        P(REC_TM_FREQ, None),
        P(None, REC_TM_FREQ),
        P(REC_TM, "freq"),
        P(REC_TM, "freq", None),
        P(),
        P(),
        P(),
        P(),
    )
    return jax.shard_map(
        per_device,
        mesh=split,
        in_specs=placed,
        out_specs=(P(REC_TM, "freq", None), P(REC_TM_FREQ, None), P("rec", TM_FREQ, None)),
        check_vma=False,
    )
```

```python
import jax
import jax.numpy as jnp
from jax import lax
from jax.experimental import pallas as pl
from jax.experimental.pallas import tpu as pltpu
from jax.sharding import Mesh
from jax.sharding import PartitionSpec as P


TM = ("tm_0", "tm_1")
TM_FREQ = ("tm_0", "tm_1", "freq")
REC_TM_FREQ = ("rec", "tm_0", "tm_1", "freq")
REC_TM = ("rec", "tm_0", "tm_1")

F32 = jnp.float32
BF16 = jnp.bfloat16
ROWS = 50
COLS = 8
CELLS = ROWS * COLS
CHANNELS = 384
DEPTH = 3 * CHANNELS
PIX = 256
ERF_SCALE = 0.7071067811865476
PDF_SCALE = 0.3989422804014327
ERF_TOP = (
    0.00022905065861350646,
    0.0034082910107109506,
    0.050955695062380861,
    0.18520832239976145,
    1.128379143519084,
)
ERF_BOTTOM = (
    -1.1791602954361697e-7,
    0.000023547966471313185,
    0.0010179625278914885,
    0.014070470171167667,
    0.11098505178285362,
    0.49746925110067538,
    1.0,
)


def horner(value, factors):
    total = jnp.full_like(value, factors[0])
    for factor in factors[1:]:
        total = total * value + factor
    return total


def erf(value):
    bounded = jnp.clip(value, -3.7439211627767994, 3.7439211627767994)
    square = bounded * bounded
    return bounded * horner(square, ERF_TOP) / horner(square, ERF_BOTTOM)


def half_erf(unit):
    return 0.5 * (1.0 + erf(unit * ERF_SCALE))


def column_shifted(value):
    cells, channels = value.shape
    grid = value.reshape(cells // 8, 8, channels)
    column = lax.broadcasted_iota(jnp.int32, grid.shape, 1)
    lower = jnp.where(column == 0, 0.0, pltpu.roll(grid, 1, axis=1))
    upper = jnp.where(column == 7, 0.0, pltpu.roll(grid, 7, axis=1))
    return lower.reshape(value.shape), value, upper.reshape(value.shape)


def store_columns(value, even, odd):
    cells, channels = value.shape
    for part, shifted in enumerate(column_shifted(value)):
        lanes = slice(part * channels, (part + 1) * channels)
        even[0:cells, lanes] = shifted.astype(BF16)
        odd[0 : cells - 8, lanes] = shifted[8:].astype(BF16)


def fetch(weight, layer, taps, arrivals):
    copies = []
    for part in range(3):
        rows = pl.ds(part * DEPTH, DEPTH)
        copies.append(
            pltpu.make_async_copy(weight.at[layer, rows], taps.at[rows], arrivals.at[part])
        )
    for copy in copies:
        copy.start()
    return copies


def conv_taps(even, odd, taps, copies, cells):
    summed = None
    for part, window in enumerate((even[0:cells], odd[0:cells], even[16 : 16 + cells])):
        copies[part].wait()
        term = jnp.dot(
            window, taps[part * DEPTH : (part + 1) * DEPTH], preferred_element_type=F32
        )
        summed = term if summed is None else summed + term
    return summed


def conv_back(grad, taps, cells, copies=None):
    summed = None
    for row_off in range(3):
        if copies:
            copies[row_off].wait()
        term = lax.dot_general(
            grad,
            taps[row_off * DEPTH : (row_off + 1) * DEPTH],
            (((1,), (1,)), ((), ())),
            preferred_element_type=F32,
        )
        term = term[8 * (2 - row_off) : 8 * (2 - row_off) + cells]
        summed = term if summed is None else summed + term
    grid = (cells // 8, 8, CHANNELS)
    column = lax.broadcasted_iota(jnp.int32, grid, 1)
    first = summed[:, 0:CHANNELS].reshape(grid)
    last = summed[:, 2 * CHANNELS :].reshape(grid)
    total = jnp.where(column == 7, 0.0, pltpu.roll(first, 7, axis=1))
    total += jnp.where(column == 0, 0.0, pltpu.roll(last, 1, axis=1))
    return summed[:, CHANNELS : 2 * CHANNELS] + total.reshape(cells, CHANNELS)


def normed(conv_out):
    center = conv_out - jnp.mean(conv_out, axis=-1, keepdims=True)
    scale = lax.rsqrt(jnp.mean(center * center, axis=-1, keepdims=True) + 1e-05)
    return center * scale, scale


def pull_back(unit, scale, gradient):
    slope = half_erf(unit) + unit * (PDF_SCALE * jnp.exp(-0.5 * unit * unit))
    grad = gradient * slope
    mean = jnp.mean(grad, axis=-1, keepdims=True)
    along = jnp.mean(grad * unit, axis=-1, keepdims=True)
    return scale * (grad - mean - unit * along)


def rows_valid(cells, before):
    row = lax.shift_right_logical(lax.broadcasted_iota(jnp.int32, (cells, 1), 0), 3)
    row = row + lax.axis_index(TM) * ROWS - before
    return (row >= 0) & (row < lax.axis_size(TM) * ROWS)


def pack_kernel(tokens, placement, in_weight, packed, where_out):
    count = tokens.shape[0]
    rows = placement[0:1, :].astype(F32)
    cols = placement[1:2, :].astype(F32)
    tile_row = jnp.floor((rows + 0.5) * (1.0 / ROWS))
    tile = tile_row * 2.0 + jnp.where(cols >= 4.0, 1.0, 0.0)
    down = lax.broadcasted_iota(jnp.int32, (count, count), 0)
    across = lax.broadcasted_iota(jnp.int32, (count, count), 1)

    def column(value):
        return jnp.sum(jnp.where(down == across, value, 0.0), axis=1, keepdims=True)

    earlier = jnp.where((column(tile) == tile) & (down < across), 1.0, 0.0)
    where_to = tile * 2.0 + jnp.sum(earlier, axis=0, keepdims=True)
    where_out[...] = jnp.broadcast_to(column(where_to), where_out.shape)
    index = lax.broadcasted_iota(jnp.int32, (packed.shape[0], 1), 0)
    wanted = lax.shift_right_logical(index, 4) * 4 + (index & 3)
    match = jnp.where(wanted.astype(F32) == where_to, 1.0, 0.0).astype(BF16)
    proj = jnp.dot(tokens[...], in_weight[...], preferred_element_type=F32).astype(BF16)
    lane = lax.broadcasted_iota(jnp.int32, (count, 128), 1)
    notes = jnp.where(lane == 1, column(cols), jnp.where(lane == 2, 1.0, 0.0))
    notes = jnp.where(lane == 0, column(rows - tile_row * ROWS), notes).astype(BF16)
    low = jnp.dot(match, proj[:, 0:256], preferred_element_type=F32)
    rest = jnp.concatenate([proj[:, 256:384], notes], axis=1)
    high = jnp.dot(match, rest, preferred_element_type=F32)
    packed[...] = jnp.where((index & 4) == 0, low, high).astype(BF16)


def place_kernel(arrived, own_aim, other_aim, token, x_out, aim_out, down_out, up_out, chosen_out):
    core = lax.axis_index("freq")
    slots = arrived.shape[0]
    notes = arrived[:, 128:256].astype(F32).reshape(slots // 8, 8, 128)
    within = lax.broadcasted_iota(jnp.int32, notes.shape, 1)
    notes = jnp.where(within >= 4, notes, pltpu.roll(notes, 4, axis=1)).reshape(slots, 128)
    cell = jnp.where(notes[:, 2:3] == 1.0, notes[:, 0:1] * 8.0 + notes[:, 1:2], -1.0)
    lane = lax.broadcasted_iota(jnp.int32, (slots, CELLS), 1)
    index = lax.broadcasted_iota(jnp.int32, (slots, CELLS), 0)
    hit = lane == cell.astype(jnp.int32)

    def pick(flag):
        return lax.dot_general(
            jnp.where(hit & flag, 1.0, 0.0).astype(BF16),
            arrived[...],
            (((0,), (0,)), ((), ())),
            preferred_element_type=F32,
        )

    placed = jnp.concatenate([pick((index & 4) == 0), pick((index & 4) == 4)[:, 0:128]], axis=1)
    number = lax.broadcasted_iota(jnp.int32, (CELLS, 1), 0)
    far = (lax.shift_right_logical(number, 2) & 1) != core
    source = lax.shift_right_logical(number, 3) * 4 + (number & 3) + jnp.where(far, CELLS // 2, 0)
    order = lax.broadcasted_iota(jnp.int32, (CELLS, CELLS), 1) == source
    aim = jnp.dot(
        jnp.where(order, 1.0, 0.0).astype(BF16),
        jnp.concatenate([own_aim[...].astype(F32), other_aim[...].astype(F32)], axis=0).astype(BF16),
        preferred_element_type=F32,
    )
    x = jnp.where(aim[:, PIX : PIX + 1] == 1.0, token[...].astype(F32), placed)
    x_out[...] = x.astype(BF16)
    aim_out[...] = aim.astype(BF16)
    down_out[...] = jnp.concatenate([x[CELLS - 32 :], aim[CELLS - 16 :]], axis=0).astype(BF16)
    up_out[...] = jnp.concatenate([x[0:32], aim[0:16]], axis=0).astype(BF16)
    spread = jnp.broadcast_to(cell, (slots, 128)).reshape(slots // 8, 8, 128)
    first = jnp.sum(jnp.where(within == 4 + 2 * core, spread, 0.0), axis=1, keepdims=True)
    second = jnp.sum(jnp.where(within == 5 + 2 * core, spread, 0.0), axis=1, keepdims=True)
    spread = jnp.where((within & 1) == 0, first, second)
    spread = jnp.where(within < 6, spread, -1.0).reshape(slots, 128)
    chosen_out[...] = jnp.where(lane == spread[:, 0:1].astype(jnp.int32), 1.0, 0.0).astype(BF16)


def first_kernel(
    above, own, below, weight, active_out, unit_out, scale_out, share_out,
    even, odd, taps, arrivals,
):
    copies = fetch(weight, 0, taps, arrivals)
    source = jnp.concatenate(
        [above[0:32].astype(F32), own[...].astype(F32), below[0:32].astype(F32)], axis=0
    )
    store_columns(source, even, odd)
    unit, scale = normed(conv_taps(even, odd, taps, copies, 448))
    unit_out[...] = unit[16:432]
    scale_out[...] = jnp.broadcast_to(scale[16:432], (416, 128))
    active = source[8:456] + unit * half_erf(unit)
    active = jnp.where(rows_valid(448, 3), active, 0.0)
    active_out[...] = active.astype(BF16)
    share = jnp.where(lax.axis_index("freq") == 1, active[16:432], source[24:440]).astype(BF16)
    for peer in range(4):
        share_out[peer] = share


def second_kernel(
    active_ref, unit_ref, scale_ref, weight, head, above, aim_ref, below,
    pred, share_out, mid_out, grad_out, even, odd, taps, arrivals,
):
    copies = fetch(weight, 1, taps, arrivals)
    active = active_ref[...].astype(F32)
    store_columns(active, even, odd)
    unit, scale = normed(conv_taps(even, odd, taps, copies, 432))
    top = (active[8:440] + unit * half_erf(unit)).astype(BF16)
    guess = jnp.dot(top, head[...], preferred_element_type=F32)
    pred[...] = guess[16:416].astype(BF16)
    aim = jnp.concatenate([above[32:48], aim_ref[...], below[32:48]], axis=0)
    misfit = jnp.where(
        aim[:, PIX : PIX + 1] == 1.0, (guess - aim[:, 0:PIX].astype(F32)) * 0.0625, 0.0
    ).astype(BF16)
    grad_top = lax.dot_general(
        misfit, head[...], (((1,), (1,)), ((), ())), preferred_element_type=F32
    )
    grad_two = pull_back(unit, scale, grad_top).astype(BF16)
    grad_mid = grad_top[8:424] + conv_back(grad_two, taps, 416)
    grad_one = pull_back(unit_ref[...], scale_ref[:, 0:1], grad_mid)
    grad_one = jnp.where(rows_valid(416, 1), grad_one, 0.0)
    grad_out[...] = grad_one.astype(BF16)
    mid_out[...] = grad_mid[8:408]
    share_out[...] = jnp.where(
        lax.axis_index("freq") == 1, grad_two.astype(F32)[16:416], grad_one[8:408]
    ).astype(BF16)


def tail_kernel(grad_ref, mid_ref, weight, chosen, out, taps, arrivals):
    copies = fetch(weight, 0, taps, arrivals)
    grad_cells = mid_ref[...] + conv_back(grad_ref[...], taps, CELLS, copies)
    picked = jnp.dot(chosen[...], grad_cells.astype(BF16), preferred_element_type=F32)
    part = lax.broadcasted_iota(jnp.int32, out.shape, 0) & 6
    picked = jnp.where(
        part == 0, picked[:, 0:128], jnp.where(part == 2, picked[:, 128:256], picked[:, 256:384])
    )
    out[...] = picked.astype(BF16)


def finish_kernel(returned, where_ref, in_weight, out):
    count = where_ref.shape[0]
    slots = returned.shape[0]
    index = lax.broadcasted_iota(jnp.int32, (count, slots), 1)
    slot = lax.shift_right_logical(index, 3) * 2 + (index & 1)
    hit = where_ref[:, 0:1].astype(jnp.int32) == slot
    parts = []
    for part in range(3):
        taken = jnp.where(hit & ((index & 6) == 2 * part), 1.0, 0.0).astype(BF16)
        parts.append(jnp.dot(taken, returned[...], preferred_element_type=F32))
    grad_proj = jnp.concatenate(parts, axis=1).astype(BF16)
    out[...] = lax.dot_general(
        grad_proj, in_weight[...], (((1,), (1,)), ((), ())), preferred_element_type=F32
    )


def weight_kernel(inner, own, back, early, late, front, out, turned, moved, total):
    place = lax.axis_index("tm_0")
    for part in range(4):
        turned[part] = inner[(place - part) & 3].astype(F32).T.astype(BF16)
    moved[:, 0:16] = jnp.zeros((12, 16, CHANNELS), F32)
    moved[:, CELLS : CELLS + 16] = jnp.zeros((12, 16, CHANNELS), F32)
    outers = (
        own[...].astype(F32),
        back[...].astype(F32),
        jnp.concatenate([early[...].astype(F32), late[...].astype(F32)], axis=0),
        front[...].astype(F32),
    )
    column = lax.broadcasted_iota(jnp.int32, (ROWS, COLS, CHANNELS), 1)
    for step in range(3):
        tap = place * 2 + step
        row_off = jnp.where(tap >= 6, 2, jnp.where(tap >= 3, 1, 0))
        shift = tap - 3 * row_off - 1
        start = pl.multiple_of(row_off * 8, 8)
        inside = (column >= shift) & (column < COLS + shift)
        summed = None
        for part in range(4):
            piece = pltpu.roll(outers[part].reshape(ROWS, COLS, CHANNELS), shift & 7, axis=1)
            piece = jnp.where(inside, piece, 0.0).reshape(CELLS, CHANNELS)
            slot = 4 * step + part
            moved[slot, pl.ds(start, CELLS), :] = piece
            term = jnp.dot(turned[part], moved[slot].astype(BF16), preferred_element_type=F32)
            summed = term if summed is None else summed + term
        total[step * CHANNELS : (step + 1) * CHANNELS] = summed
    base = pl.multiple_of(place * 96, 8)
    kept = total[pl.ds(base, 864), :]
    for block in range(16):
        out[block] = kept[54 * block : 54 * (block + 1)].astype(BF16)


VMEM = pl.BlockSpec(memory_space=pltpu.VMEM)
HBM = pl.BlockSpec(memory_space=pltpu.HBM)


def call(kernel, shapes, scratch, cost, limit, *operands, far=-1):
    return pl.pallas_call(
        kernel,
        out_shape=shapes,
        in_specs=[HBM if i == far else VMEM for i in range(len(operands))],
        out_specs=jax.tree.map(lambda _: VMEM, shapes),
        scratch_shapes=scratch,
        compiler_params=pltpu.CompilerParams(vmem_limit_bytes=limit << 20),
        cost_estimate=pl.CostEstimate(
            flops=cost, bytes_accessed=cost // 400, transcendentals=0
        ),
    )(*operands)


def shape(dims, dtype=BF16):
    return jax.ShapeDtypeStruct(dims, dtype)


def send(value, axis, step, wrap):
    count = lax.axis_size(axis)
    pairs = [(i, (i + step) % count) for i in range(count)]
    if not wrap:
        pairs = [(i, i + step) for i in range(count) if 0 <= i + step < count]
    return lax.ppermute(value, axis, pairs)


def per_device(
    tokens, placement, patch_mask, targets, in_weight, mask_token, conv_weight, head_weight
):
    shards = lax.axis_size(TM_FREQ)
    conv_weight = pltpu.with_memory_space_constraint(conv_weight, pltpu.HBM)
    core = lax.axis_index("freq")
    visible = tokens.shape[0]
    half = patch_mask.shape[1]

    packed, where_to = call(
        pack_kernel,
        (shape((shards * 8, 256)), shape((visible, 128), F32)),
        [],
        80_000_000,
        62,
        tokens,
        placement,
        in_weight,
    )
    arrived = lax.all_to_all(packed, TM_FREQ, split_axis=0, concat_axis=0, tiled=True)

    flags = jnp.broadcast_to((patch_mask == 1)[:, :, None], (*patch_mask.shape, 128))
    aim = jnp.concatenate([targets, flags.astype(BF16)], axis=2).reshape(-1, PIX + 128)
    other = send(aim, "freq", 1, True)

    own, aim, down, up, chosen = call(
        place_kernel,
        (
            shape((CELLS, CHANNELS)),
            shape((CELLS, PIX + 128)),
            shape((48, CHANNELS)),
            shape((48, CHANNELS)),
            shape((shards * 8, CELLS)),
        ),
        [],
        300_000_000,
        8,
        arrived,
        aim,
        other,
        mask_token[None, :],
    )
    above = send(down, TM, 1, False)
    below = send(up, TM, -1, False)
    loaded = [pltpu.VMEM((9 * CHANNELS, CHANNELS), BF16), pltpu.SemaphoreType.DMA((3,))]
    columns = [pltpu.VMEM((464, DEPTH), BF16), pltpu.VMEM((464, DEPTH), BF16), *loaded]
    active, unit, scale, inner = call(
        first_kernel,
        (
            shape((448, CHANNELS)),
            shape((416, CHANNELS), F32),
            shape((416, 128), F32),
            shape((4, 416, CHANNELS)),
        ),
        columns,
        1_500_000_000,
        16,
        above,
        own,
        below,
        conv_weight,
        far=3,
    )
    inners = lax.all_to_all(inner, "tm_0", split_axis=0, concat_axis=0, tiled=True)
    pred, outer, mid, grad = call(
        second_kernel,
        (
            shape((CELLS, PIX)),
            shape((CELLS, CHANNELS)),
            shape((CELLS, CHANNELS), F32),
            shape((416, CHANNELS)),
        ),
        columns,
        3_500_000_000,
24,
        active,
        unit,
        scale,
        conv_weight,
        head_weight,
        above,
        aim,
        below,
        far=3,
    )
    back = send(outer, "tm_0", 1, True)
    front = send(outer, "tm_0", -1, True)
    early = send(back[: CELLS // 2], "tm_0", 1, True)
    late = send(front[CELLS // 2 :], "tm_0", -1, True)
    outgoing = call(
        tail_kernel,
        shape((shards * 8, 128)),
        loaded,
        1_200_000_000,
        16,
        grad,
        mid,
        conv_weight,
        chosen,
        far=2,
    )
    returned = lax.all_to_all(
        outgoing, TM_FREQ, split_axis=0, concat_axis=0, tiled=True
    )
    terms = call(
        weight_kernel,
        shape((16, 54, CHANNELS)),
        [
            pltpu.VMEM((4, CHANNELS, 416), BF16),
            pltpu.VMEM((12, 416, CHANNELS), F32),
            pltpu.VMEM((DEPTH, CHANNELS), F32),
        ],
        1_500_000_000,
        24,
        inners,
        outer,
        back,
        early,
        late,
        front,
    )
    terms = lax.all_to_all(terms, ("tm_1", "freq"), split_axis=0, concat_axis=0, tiled=True)
    token_grad = call(
        finish_kernel,
        shape((visible, in_weight.shape[0]), F32),
        [],
        80_000_000,
        4,
        returned,
        where_to,
        in_weight,
    )
    conv_grad = terms.reshape(-1, 2, 54, CHANNELS).astype(F32).sum(axis=0)
    pred = lax.dynamic_slice_in_dim(pred.reshape(ROWS, COLS, PIX), core * half, half, axis=1)
    return (pred, token_grad, conv_grad)


def solution(mesh):
    split = Mesh(
        mesh.devices.reshape(4, 8, mesh.shape["freq"], mesh.shape["rec"]),
        ("tm_0", "tm_1", "freq", "rec"),
    )
    placed = (
        P(REC_TM_FREQ, None),
        P(None, REC_TM_FREQ),
        P(REC_TM, "freq"),
        P(REC_TM, "freq", None),
        P(),
        P(),
        P(),
        P(),
    )
    return jax.shard_map(
        per_device,
        mesh=split,
        in_specs=placed,
        out_specs=(P(REC_TM, "freq", None), P(REC_TM_FREQ, None), P("rec", TM_FREQ, None)),
        check_vma=False,
    )
```

```python
import jax
import jax.numpy as jnp
from jax import lax
from jax.experimental import pallas as pl
from jax.experimental.pallas import tpu as pltpu
from jax.sharding import Mesh
from jax.sharding import PartitionSpec as P


TM = ("tm_0", "tm_1")
TM_FREQ = ("tm_0", "tm_1", "freq")
REC_TM_FREQ = ("rec", "tm_0", "tm_1", "freq")
REC_TM = ("rec", "tm_0", "tm_1")

F32 = jnp.float32
BF16 = jnp.bfloat16
ROWS = 50
COLS = 8
CELLS = ROWS * COLS
CHANNELS = 384
DEPTH = 3 * CHANNELS
PIX = 256
ERF_SCALE = 0.7071067811865476
PDF_SCALE = 0.3989422804014327
ERF_TOP = (
    0.00022905065861350646,
    0.0034082910107109506,
    0.050955695062380861,
    0.18520832239976145,
    1.128379143519084,
)
ERF_BOTTOM = (
    -1.1791602954361697e-7,
    0.000023547966471313185,
    0.0010179625278914885,
    0.014070470171167667,
    0.11098505178285362,
    0.49746925110067538,
    1.0,
)


def horner(value, factors):
    total = jnp.full_like(value, factors[0])
    for factor in factors[1:]:
        total = total * value + factor
    return total


def erf(value):
    bounded = jnp.clip(value, -3.7439211627767994, 3.7439211627767994)
    square = bounded * bounded
    return bounded * horner(square, ERF_TOP) / horner(square, ERF_BOTTOM)


def half_erf(unit):
    return 0.5 * (1.0 + erf(unit * ERF_SCALE))


def column_shifted(value):
    cells, channels = value.shape
    grid = value.reshape(cells // 8, 8, channels)
    column = lax.broadcasted_iota(jnp.int32, grid.shape, 1)
    lower = jnp.where(column == 0, 0.0, pltpu.roll(grid, 1, axis=1))
    upper = jnp.where(column == 7, 0.0, pltpu.roll(grid, 7, axis=1))
    return lower.reshape(value.shape), value, upper.reshape(value.shape)


def store_columns(value, even, odd):
    cells, channels = value.shape
    for part, shifted in enumerate(column_shifted(value)):
        lanes = slice(part * channels, (part + 1) * channels)
        even[0:cells, lanes] = shifted.astype(BF16)
        odd[0 : cells - 8, lanes] = shifted[8:].astype(BF16)


def conv_taps(even, odd, taps, cells):
    summed = None
    for part, window in enumerate((even[0:cells], odd[0:cells], even[16 : 16 + cells])):
        term = jnp.dot(
            window, taps[0, part * DEPTH : (part + 1) * DEPTH], preferred_element_type=F32
        )
        summed = term if summed is None else summed + term
    return summed


def conv_back(grad, taps, cells):
    summed = None
    for row_off in range(3):
        term = lax.dot_general(
            grad,
            taps[0, row_off * DEPTH : (row_off + 1) * DEPTH],
            (((1,), (1,)), ((), ())),
            preferred_element_type=F32,
        )
        term = term[8 * (2 - row_off) : 8 * (2 - row_off) + cells]
        summed = term if summed is None else summed + term
    grid = (cells // 8, 8, CHANNELS)
    column = lax.broadcasted_iota(jnp.int32, grid, 1)
    first = summed[:, 0:CHANNELS].reshape(grid)
    last = summed[:, 2 * CHANNELS :].reshape(grid)
    total = jnp.where(column == 7, 0.0, pltpu.roll(first, 7, axis=1))
    total += jnp.where(column == 0, 0.0, pltpu.roll(last, 1, axis=1))
    return summed[:, CHANNELS : 2 * CHANNELS] + total.reshape(cells, CHANNELS)


def normed(conv_out):
    center = conv_out - jnp.mean(conv_out, axis=-1, keepdims=True)
    scale = lax.rsqrt(jnp.mean(center * center, axis=-1, keepdims=True) + 1e-05)
    return center * scale, scale


def pull_back(unit, scale, gradient):
    slope = half_erf(unit) + unit * (PDF_SCALE * jnp.exp(-0.5 * unit * unit))
    grad = gradient * slope
    mean = jnp.mean(grad, axis=-1, keepdims=True)
    along = jnp.mean(grad * unit, axis=-1, keepdims=True)
    return scale * (grad - mean - unit * along)


def rows_valid(cells, before):
    row = lax.shift_right_logical(lax.broadcasted_iota(jnp.int32, (cells, 1), 0), 3)
    row = row + lax.axis_index(TM) * ROWS - before
    return (row >= 0) & (row < lax.axis_size(TM) * ROWS)


def pack_kernel(tokens, placement, in_weight, packed, where_out):
    count = tokens.shape[0]
    rows = placement[0:1, :].astype(F32)
    cols = placement[1:2, :].astype(F32)
    tile_row = jnp.floor((rows + 0.5) * (1.0 / ROWS))
    tile = tile_row * 2.0 + jnp.where(cols >= 4.0, 1.0, 0.0)
    down = lax.broadcasted_iota(jnp.int32, (count, count), 0)
    across = lax.broadcasted_iota(jnp.int32, (count, count), 1)

    def column(value):
        return jnp.sum(jnp.where(down == across, value, 0.0), axis=1, keepdims=True)

    earlier = jnp.where((column(tile) == tile) & (down < across), 1.0, 0.0)
    where_to = tile * 2.0 + jnp.sum(earlier, axis=0, keepdims=True)
    where_out[...] = jnp.broadcast_to(column(where_to), where_out.shape)
    index = lax.broadcasted_iota(jnp.int32, (packed.shape[0], 1), 0)
    wanted = lax.shift_right_logical(index, 4) * 4 + (index & 3)
    match = jnp.where(wanted.astype(F32) == where_to, 1.0, 0.0).astype(BF16)
    proj = jnp.dot(tokens[...], in_weight[...], preferred_element_type=F32).astype(BF16)
    lane = lax.broadcasted_iota(jnp.int32, (count, 128), 1)
    notes = jnp.where(lane == 1, column(cols), jnp.where(lane == 2, 1.0, 0.0))
    notes = jnp.where(lane == 0, column(rows - tile_row * ROWS), notes).astype(BF16)
    low = jnp.dot(match, proj[:, 0:256], preferred_element_type=F32)
    rest = jnp.concatenate([proj[:, 256:384], notes], axis=1)
    high = jnp.dot(match, rest, preferred_element_type=F32)
    packed[...] = jnp.where((index & 4) == 0, low, high).astype(BF16)


def place_kernel(arrived, own_aim, other_aim, token, x_out, aim_out, down_out, up_out, chosen_out):
    core = lax.axis_index("freq")
    slots = arrived.shape[0]
    notes = arrived[:, 128:256].astype(F32).reshape(slots // 8, 8, 128)
    within = lax.broadcasted_iota(jnp.int32, notes.shape, 1)
    notes = jnp.where(within >= 4, notes, pltpu.roll(notes, 4, axis=1)).reshape(slots, 128)
    cell = jnp.where(notes[:, 2:3] == 1.0, notes[:, 0:1] * 8.0 + notes[:, 1:2], -1.0)
    lane = lax.broadcasted_iota(jnp.int32, (slots, CELLS), 1)
    index = lax.broadcasted_iota(jnp.int32, (slots, CELLS), 0)
    hit = lane == cell.astype(jnp.int32)

    def pick(flag):
        return lax.dot_general(
            jnp.where(hit & flag, 1.0, 0.0).astype(BF16),
            arrived[...],
            (((0,), (0,)), ((), ())),
            preferred_element_type=F32,
        )

    placed = jnp.concatenate([pick((index & 4) == 0), pick((index & 4) == 4)[:, 0:128]], axis=1)
    number = lax.broadcasted_iota(jnp.int32, (CELLS, 1), 0)
    far = (lax.shift_right_logical(number, 2) & 1) != core
    source = lax.shift_right_logical(number, 3) * 4 + (number & 3) + jnp.where(far, CELLS // 2, 0)
    order = lax.broadcasted_iota(jnp.int32, (CELLS, CELLS), 1) == source
    aim = jnp.dot(
        jnp.where(order, 1.0, 0.0).astype(BF16),
        jnp.concatenate([own_aim[...].astype(F32), other_aim[...].astype(F32)], axis=0).astype(BF16),
        preferred_element_type=F32,
    )
    x = jnp.where(aim[:, PIX : PIX + 1] == 1.0, token[...].astype(F32), placed)
    x_out[...] = x.astype(BF16)
    aim_out[...] = aim.astype(BF16)
    down_out[...] = jnp.concatenate([x[CELLS - 32 :], aim[CELLS - 16 :]], axis=0).astype(BF16)
    up_out[...] = jnp.concatenate([x[0:32], aim[0:16]], axis=0).astype(BF16)
    spread = jnp.broadcast_to(cell, (slots, 128)).reshape(slots // 8, 8, 128)
    first = jnp.sum(jnp.where(within == 4 + 2 * core, spread, 0.0), axis=1, keepdims=True)
    second = jnp.sum(jnp.where(within == 5 + 2 * core, spread, 0.0), axis=1, keepdims=True)
    spread = jnp.where((within & 1) == 0, first, second)
    spread = jnp.where(within < 6, spread, -1.0).reshape(slots, 128)
    chosen_out[...] = jnp.where(lane == spread[:, 0:1].astype(jnp.int32), 1.0, 0.0).astype(BF16)


def first_kernel(
    above, own, below, weight, active_out, unit_out, scale_out, share_out, even, odd
):
    source = jnp.concatenate(
        [above[0:32].astype(F32), own[...].astype(F32), below[0:32].astype(F32)], axis=0
    )
    store_columns(source, even, odd)
    unit, scale = normed(conv_taps(even, odd, weight, 448))
    unit_out[...] = unit[16:432]
    scale_out[...] = jnp.broadcast_to(scale[16:432], (416, 128))
    active = source[8:456] + unit * half_erf(unit)
    active = jnp.where(rows_valid(448, 3), active, 0.0)
    active_out[...] = active.astype(BF16)
    share_out[...] = jnp.where(
        lax.axis_index("freq") == 1, active[16:432], source[24:440]
    ).astype(BF16)


def second_kernel(
    active_ref, unit_ref, scale_ref, weight, head, above, aim_ref, below,
    pred, share_out, mid_out, grad_out, even, odd,
):
    active = active_ref[...].astype(F32)
    store_columns(active, even, odd)
    unit, scale = normed(conv_taps(even, odd, weight, 432))
    top = (active[8:440] + unit * half_erf(unit)).astype(BF16)
    guess = jnp.dot(top, head[...], preferred_element_type=F32)
    pred[...] = guess[16:416].astype(BF16)
    aim = jnp.concatenate([above[32:48], aim_ref[...], below[32:48]], axis=0)
    misfit = jnp.where(
        aim[:, PIX : PIX + 1] == 1.0, (guess - aim[:, 0:PIX].astype(F32)) * 0.0625, 0.0
    ).astype(BF16)
    grad_top = lax.dot_general(
        misfit, head[...], (((1,), (1,)), ((), ())), preferred_element_type=F32
    )
    grad_two = pull_back(unit, scale, grad_top).astype(BF16)
    grad_mid = grad_top[8:424] + conv_back(grad_two, weight, 416)
    grad_one = pull_back(unit_ref[...], scale_ref[:, 0:1], grad_mid)
    grad_one = jnp.where(rows_valid(416, 1), grad_one, 0.0)
    grad_out[...] = grad_one.astype(BF16)
    mid_out[...] = grad_mid[8:408]
    share_out[...] = jnp.where(
        lax.axis_index("freq") == 1, grad_two.astype(F32)[16:416], grad_one[8:408]
    ).astype(BF16)


def tail_kernel(grad_ref, mid_ref, weight, chosen, out):
    grad_cells = mid_ref[...] + conv_back(grad_ref[...], weight, CELLS)
    picked = jnp.dot(chosen[...], grad_cells.astype(BF16), preferred_element_type=F32)
    part = lax.broadcasted_iota(jnp.int32, out.shape, 0) & 6
    picked = jnp.where(
        part == 0, picked[:, 0:128], jnp.where(part == 2, picked[:, 128:256], picked[:, 256:384])
    )
    out[...] = picked.astype(BF16)


def finish_kernel(returned, where_ref, in_weight, out):
    count = where_ref.shape[0]
    slots = returned.shape[0]
    index = lax.broadcasted_iota(jnp.int32, (count, slots), 1)
    slot = lax.shift_right_logical(index, 3) * 2 + (index & 1)
    hit = where_ref[:, 0:1].astype(jnp.int32) == slot
    parts = []
    for part in range(3):
        taken = jnp.where(hit & ((index & 6) == 2 * part), 1.0, 0.0).astype(BF16)
        parts.append(jnp.dot(taken, returned[...], preferred_element_type=F32))
    grad_proj = jnp.concatenate(parts, axis=1).astype(BF16)
    out[...] = lax.dot_general(
        grad_proj, in_weight[...], (((1,), (1,)), ((), ())), preferred_element_type=F32
    )


def weight_kernel(*refs):
    inners, outers = refs[0:4], [ref[...].astype(F32) for ref in refs[4:8]]
    out, turned, moved, total = refs[8:]
    place = lax.axis_index("tm_0")
    for part in range(4):
        turned[part] = inners[part][...].astype(F32).T.astype(BF16)
    column = lax.broadcasted_iota(jnp.int32, (ROWS, COLS, CHANNELS), 1)
    for step in range(3):
        tap = place * 2 + step
        row_off = jnp.where(tap >= 6, 2, jnp.where(tap >= 3, 1, 0))
        shift = tap - 3 * row_off - 1
        start = pl.multiple_of(row_off * 8, 8)
        inside = (column >= shift) & (column < COLS + shift)
        summed = None
        for part in range(4):
            piece = pltpu.roll(outers[part].reshape(ROWS, COLS, CHANNELS), shift & 7, axis=1)
            piece = jnp.where(inside, piece, 0.0).reshape(CELLS, CHANNELS)
            moved[part, 0:16] = jnp.zeros((16, CHANNELS), F32)
            moved[part, CELLS : CELLS + 16] = jnp.zeros((16, CHANNELS), F32)
            moved[part, pl.ds(start, CELLS), :] = piece
            term = jnp.dot(turned[part], moved[part].astype(BF16), preferred_element_type=F32)
            summed = term if summed is None else summed + term
        total[step * CHANNELS : (step + 1) * CHANNELS] = summed
    base = pl.multiple_of(place * 96, 8)
    kept = total[pl.ds(base, 864), :]
    for block in range(16):
        out[block] = kept[54 * block : 54 * (block + 1)].astype(BF16)


VMEM = pl.BlockSpec(memory_space=pltpu.VMEM)


def call(kernel, shapes, scratch, cost, limit, *operands):
    return pl.pallas_call(
        kernel,
        out_shape=shapes,
        in_specs=[VMEM] * len(operands),
        out_specs=jax.tree.map(lambda _: VMEM, shapes),
        scratch_shapes=scratch,
        compiler_params=pltpu.CompilerParams(vmem_limit_bytes=limit << 20),
        cost_estimate=pl.CostEstimate(
            flops=cost, bytes_accessed=cost // 400, transcendentals=0
        ),
    )(*operands)


def shape(dims, dtype=BF16):
    return jax.ShapeDtypeStruct(dims, dtype)


def send(value, axis, step, wrap):
    count = lax.axis_size(axis)
    pairs = [(i, (i + step) % count) for i in range(count)]
    if not wrap:
        pairs = [(i, i + step) for i in range(count) if 0 <= i + step < count]
    return lax.ppermute(value, axis, pairs)


def per_device(
    tokens, placement, patch_mask, targets, in_weight, mask_token, conv_weight, head_weight
):
    shards = lax.axis_size(TM_FREQ)
    core = lax.axis_index("freq")
    visible = tokens.shape[0]
    half = patch_mask.shape[1]

    packed, where_to = call(
        pack_kernel,
        (shape((shards * 8, 256)), shape((visible, 128), F32)),
        [],
        80_000_000,
        62,
        tokens,
        placement,
        in_weight,
    )
    arrived = lax.all_to_all(packed, TM_FREQ, split_axis=0, concat_axis=0, tiled=True)
    flags = jnp.broadcast_to((patch_mask == 1)[:, :, None], (*patch_mask.shape, 128))
    aim = jnp.concatenate([targets, flags.astype(BF16)], axis=2).reshape(-1, PIX + 128)

    other = send(aim, "freq", 1, True)
    weights = [conv_weight[layer : layer + 1] for layer in range(2)]

    own, aim, down, up, chosen = call(
        place_kernel,
        (
            shape((CELLS, CHANNELS)),
            shape((CELLS, PIX + 128)),
            shape((48, CHANNELS)),
            shape((48, CHANNELS)),
            shape((shards * 8, CELLS)),
        ),
        [],
        300_000_000,
        8,
        arrived,
        aim,
        other,
        mask_token[None, :],
    )
    above = send(down, TM, 1, False)
    below = send(up, TM, -1, False)
    columns = [pltpu.VMEM((464, DEPTH), BF16), pltpu.VMEM((464, DEPTH), BF16)]
    active, unit, scale, inner = call(
        first_kernel,
        (
            shape((448, CHANNELS)),
            shape((416, CHANNELS), F32),
            shape((416, 128), F32),
            shape((416, CHANNELS)),
        ),
        columns,
        1_500_000_000,
        12,
        above,
        own,
        below,
        weights[0],
    )
    inners = [inner] + [send(inner, "tm_0", step, True) for step in (1, 2, 3)]
    pred, outer, mid, grad = call(
        second_kernel,
        (
            shape((CELLS, PIX)),
            shape((CELLS, CHANNELS)),
            shape((CELLS, CHANNELS), F32),
            shape((416, CHANNELS)),
        ),
        columns,
        3_500_000_000,
18,
        active,
        unit,
        scale,
        weights[1],
        head_weight,
        above,
        aim,
        below,
    )
    outers = [outer] + [send(outer, "tm_0", step, True) for step in (1, 2, 3)]
    outgoing = call(
        tail_kernel, shape((shards * 8, 128)), [], 1_200_000_000, 12, grad, mid, weights[0], chosen
    )
    returned = lax.all_to_all(
        outgoing, TM_FREQ, split_axis=0, concat_axis=0, tiled=True
    )
    terms = call(
        weight_kernel,
        shape((16, 54, CHANNELS)),
        [
            pltpu.VMEM((4, CHANNELS, 416), BF16),
            pltpu.VMEM((4, 416, CHANNELS), F32),
            pltpu.VMEM((DEPTH, CHANNELS), F32),
        ],
        1_500_000_000,
        16,
        *inners,
        *outers,
    )
    terms = lax.all_to_all(terms, ("tm_1", "freq"), split_axis=0, concat_axis=0, tiled=True)
    token_grad = call(
        finish_kernel,
        shape((visible, in_weight.shape[0]), F32),
        [],
        80_000_000,
        4,
        returned,
        where_to,
        in_weight,
    )
    conv_grad = terms.reshape(-1, 2, 54, CHANNELS).astype(F32).sum(axis=0)
    pred = lax.dynamic_slice_in_dim(pred.reshape(ROWS, COLS, PIX), core * half, half, axis=1)
    return (pred, token_grad, conv_grad)


def solution(mesh):
    split = Mesh(
        mesh.devices.reshape(4, 8, mesh.shape["freq"], mesh.shape["rec"]),
        ("tm_0", "tm_1", "freq", "rec"),
    )
    placed = (
        P(REC_TM_FREQ, None),
        P(None, REC_TM_FREQ),
        P(REC_TM, "freq"),
        P(REC_TM, "freq", None),
        P(),
        P(),
        P(),
        P(),
    )
    return jax.shard_map(
        per_device,
        mesh=split,
        in_specs=placed,
        out_specs=(P(REC_TM, "freq", None), P(REC_TM_FREQ, None), P("rec", TM_FREQ, None)),
        check_vma=False,
    )
```

```python
import jax
import jax.numpy as jnp
from jax import lax
from jax.experimental import pallas as pl
from jax.experimental.pallas import tpu as pltpu
from jax.sharding import Mesh
from jax.sharding import PartitionSpec as P


TM = ("tm_0", "tm_1")
TM_FREQ = ("tm_0", "tm_1", "freq")
REC_TM_FREQ = ("rec", "tm_0", "tm_1", "freq")
REC_TM = ("rec", "tm_0", "tm_1")

F32 = jnp.float32
BF16 = jnp.bfloat16
ROWS = 50
COLS = 8
CELLS = ROWS * COLS
CHANNELS = 384
DEPTH = 3 * CHANNELS
PIX = 256
ERF_SCALE = 0.7071067811865476
PDF_SCALE = 0.3989422804014327
ERF_TOP = (
    0.00022905065861350646,
    0.0034082910107109506,
    0.050955695062380861,
    0.18520832239976145,
    1.128379143519084,
)
ERF_BOTTOM = (
    -1.1791602954361697e-7,
    0.000023547966471313185,
    0.0010179625278914885,
    0.014070470171167667,
    0.11098505178285362,
    0.49746925110067538,
    1.0,
)


def horner(value, factors):
    total = jnp.full_like(value, factors[0])
    for factor in factors[1:]:
        total = total * value + factor
    return total


def erf(value):
    bounded = jnp.clip(value, -3.7439211627767994, 3.7439211627767994)
    square = bounded * bounded
    return bounded * horner(square, ERF_TOP) / horner(square, ERF_BOTTOM)


def half_erf(unit):
    return 0.5 * (1.0 + erf(unit * ERF_SCALE))


def column_shifted(value):
    cells, channels = value.shape
    grid = value.reshape(cells // 8, 8, channels)
    column = lax.broadcasted_iota(jnp.int32, grid.shape, 1)
    lower = jnp.where(column == 0, 0.0, pltpu.roll(grid, 1, axis=1))
    upper = jnp.where(column == 7, 0.0, pltpu.roll(grid, 7, axis=1))
    return lower.reshape(value.shape), value, upper.reshape(value.shape)


def store_columns(value, even, odd):
    cells, channels = value.shape
    for part, shifted in enumerate(column_shifted(value)):
        lanes = slice(part * channels, (part + 1) * channels)
        even[0:cells, lanes] = shifted.astype(BF16)
        odd[0 : cells - 8, lanes] = shifted[8:].astype(BF16)


def conv_taps(even, odd, taps, cells):
    summed = None
    for part, window in enumerate((even[0:cells], odd[0:cells], even[16 : 16 + cells])):
        term = jnp.dot(
            window, taps[0, part * DEPTH : (part + 1) * DEPTH], preferred_element_type=F32
        )
        summed = term if summed is None else summed + term
    return summed


def conv_back(grad, taps, cells):
    summed = None
    for row_off in range(3):
        term = lax.dot_general(
            grad,
            taps[0, row_off * DEPTH : (row_off + 1) * DEPTH],
            (((1,), (1,)), ((), ())),
            preferred_element_type=F32,
        )
        term = term[8 * (2 - row_off) : 8 * (2 - row_off) + cells]
        summed = term if summed is None else summed + term
    grid = (cells // 8, 8, CHANNELS)
    column = lax.broadcasted_iota(jnp.int32, grid, 1)
    first = summed[:, 0:CHANNELS].reshape(grid)
    last = summed[:, 2 * CHANNELS :].reshape(grid)
    total = jnp.where(column == 7, 0.0, pltpu.roll(first, 7, axis=1))
    total += jnp.where(column == 0, 0.0, pltpu.roll(last, 1, axis=1))
    return summed[:, CHANNELS : 2 * CHANNELS] + total.reshape(cells, CHANNELS)


def quarters(value):
    tiles = [value[:, 128 * part : 128 * (part + 1)] for part in range(3)]
    lane = lax.broadcasted_iota(jnp.int32, tiles[0].shape, 1)
    one = jnp.where(lane < 32, pltpu.roll(tiles[0], 32, axis=1), pltpu.roll(tiles[1], 32, axis=1))
    two = jnp.where(lane < 64, pltpu.roll(tiles[1], 64, axis=1), pltpu.roll(tiles[2], 64, axis=1))
    return tiles[0], one, two, pltpu.roll(tiles[2], 96, axis=1)


def joined(parts):
    lane = lax.broadcasted_iota(jnp.int32, parts[0].shape, 1)
    one = pltpu.roll(parts[1], 96, axis=1)
    two = pltpu.roll(parts[2], 64, axis=1)
    three = pltpu.roll(parts[3], 32, axis=1)
    tiles = (
        jnp.where(lane < 96, parts[0], one),
        jnp.where(lane < 64, one, two),
        jnp.where(lane < 32, two, three),
    )
    return jnp.concatenate(tiles, axis=1)


def normed(conv_out):
    center = conv_out - jnp.mean(conv_out, axis=-1, keepdims=True)
    scale = lax.rsqrt(jnp.mean(center * center, axis=-1, keepdims=True) + 1e-05)
    return center * scale, scale


def pull_back(unit, scale, gradient):
    slope = half_erf(unit) + unit * (PDF_SCALE * jnp.exp(-0.5 * unit * unit))
    grad = gradient * slope
    mean = jnp.mean(grad, axis=-1, keepdims=True)
    along = jnp.mean(grad * unit, axis=-1, keepdims=True)
    return scale * (grad - mean - unit * along)


def rows_valid(cells, before):
    row = lax.shift_right_logical(lax.broadcasted_iota(jnp.int32, (cells, 1), 0), 3)
    row = row + lax.axis_index(TM) * ROWS - before
    return (row >= 0) & (row < lax.axis_size(TM) * ROWS)


def pack_kernel(tokens, placement, in_weight, packed, where_out):
    count = tokens.shape[0]
    rows = placement[0:1, :].astype(F32)
    cols = placement[1:2, :].astype(F32)
    tile_row = jnp.floor((rows + 0.5) * (1.0 / ROWS))
    tile = tile_row * 2.0 + jnp.where(cols >= 4.0, 1.0, 0.0)
    down = lax.broadcasted_iota(jnp.int32, (count, count), 0)
    across = lax.broadcasted_iota(jnp.int32, (count, count), 1)

    def column(value):
        return jnp.sum(jnp.where(down == across, value, 0.0), axis=1, keepdims=True)

    earlier = jnp.where((column(tile) == tile) & (down < across), 1.0, 0.0)
    where_to = tile * 2.0 + jnp.sum(earlier, axis=0, keepdims=True)
    where_out[...] = jnp.broadcast_to(column(where_to), where_out.shape)
    index = lax.broadcasted_iota(jnp.int32, (packed.shape[0], 1), 0)
    wanted = lax.shift_right_logical(index, 4) * 4 + (index & 3)
    match = jnp.where(wanted.astype(F32) == where_to, 1.0, 0.0).astype(BF16)
    proj = jnp.dot(tokens[...], in_weight[...], preferred_element_type=F32).astype(BF16)
    lane = lax.broadcasted_iota(jnp.int32, (count, 128), 1)
    notes = jnp.where(lane == 1, column(cols), jnp.where(lane == 2, 1.0, 0.0))
    notes = jnp.where(lane == 0, column(rows - tile_row * ROWS), notes).astype(BF16)
    low = jnp.dot(match, proj[:, 0:256], preferred_element_type=F32)
    rest = jnp.concatenate([proj[:, 256:384], notes], axis=1)
    high = jnp.dot(match, rest, preferred_element_type=F32)
    packed[...] = jnp.where((index & 4) == 0, low, high).astype(BF16)


def place_kernel(arrived, own_aim, other_aim, token, x_out, aim_out, down_out, up_out, chosen_out):
    core = lax.axis_index("freq")
    slots = arrived.shape[0]
    notes = arrived[:, 128:256].astype(F32).reshape(slots // 8, 8, 128)
    within = lax.broadcasted_iota(jnp.int32, notes.shape, 1)
    notes = jnp.where(within >= 4, notes, pltpu.roll(notes, 4, axis=1)).reshape(slots, 128)
    cell = jnp.where(notes[:, 2:3] == 1.0, notes[:, 0:1] * 8.0 + notes[:, 1:2], -1.0)
    lane = lax.broadcasted_iota(jnp.int32, (slots, CELLS), 1)
    index = lax.broadcasted_iota(jnp.int32, (slots, CELLS), 0)
    hit = lane == cell.astype(jnp.int32)

    def pick(flag):
        return lax.dot_general(
            jnp.where(hit & flag, 1.0, 0.0).astype(BF16),
            arrived[...],
            (((0,), (0,)), ((), ())),
            preferred_element_type=F32,
        )

    placed = jnp.concatenate([pick((index & 4) == 0), pick((index & 4) == 4)[:, 0:128]], axis=1)
    number = lax.broadcasted_iota(jnp.int32, (CELLS, 1), 0)
    far = (lax.shift_right_logical(number, 2) & 1) != core
    source = lax.shift_right_logical(number, 3) * 4 + (number & 3) + jnp.where(far, CELLS // 2, 0)
    order = lax.broadcasted_iota(jnp.int32, (CELLS, CELLS), 1) == source
    aim = jnp.dot(
        jnp.where(order, 1.0, 0.0).astype(BF16),
        jnp.concatenate([own_aim[...].astype(F32), other_aim[...].astype(F32)], axis=0).astype(BF16),
        preferred_element_type=F32,
    )
    x = jnp.where(aim[:, PIX : PIX + 1] == 1.0, token[...].astype(F32), placed)
    x_out[...] = x.astype(BF16)
    aim_out[...] = aim.astype(BF16)
    down_out[...] = jnp.concatenate([x[CELLS - 32 :], aim[CELLS - 16 :]], axis=0).astype(BF16)
    up_out[...] = jnp.concatenate([x[0:32], aim[0:16]], axis=0).astype(BF16)
    spread = jnp.broadcast_to(cell, (slots, 128)).reshape(slots // 8, 8, 128)
    first = jnp.sum(jnp.where(within == 4 + 2 * core, spread, 0.0), axis=1, keepdims=True)
    second = jnp.sum(jnp.where(within == 5 + 2 * core, spread, 0.0), axis=1, keepdims=True)
    spread = jnp.where(within == 6, first, jnp.where(within == 7, second, -1.0))
    spread = spread.reshape(slots, 128)
    chosen_out[...] = jnp.where(lane == spread[:, 0:1].astype(jnp.int32), 1.0, 0.0).astype(BF16)


def first_kernel(
    above, own, below, weight, active_out, unit_out, scale_out, share_out, even, odd
):
    source = jnp.concatenate(
        [above[0:32].astype(F32), own[...].astype(F32), below[0:32].astype(F32)], axis=0
    )
    store_columns(source, even, odd)
    unit, scale = normed(conv_taps(even, odd, weight, 448))
    unit_out[...] = unit[16:432]
    scale_out[...] = jnp.broadcast_to(scale[16:432], (416, 128))
    active = source[8:456] + unit * half_erf(unit)
    active = jnp.where(rows_valid(448, 3), active, 0.0)
    active_out[...] = active.astype(BF16)
    share_out[...] = jnp.where(
        lax.axis_index("freq") == 1, active[16:432], source[24:440]
    ).astype(BF16)


def second_kernel(
    active_ref, unit_ref, scale_ref, weight, head, above, aim_ref, below,
    pred, share_own, share_one, share_two, share_three, mid_out, grad_out, even, odd,
):
    active = active_ref[...].astype(F32)
    store_columns(active, even, odd)
    unit, scale = normed(conv_taps(even, odd, weight, 432))
    top = (active[8:440] + unit * half_erf(unit)).astype(BF16)
    guess = jnp.dot(top, head[...], preferred_element_type=F32)
    pred[...] = guess[16:416].astype(BF16)
    aim = jnp.concatenate([above[32:48], aim_ref[...], below[32:48]], axis=0)
    misfit = jnp.where(
        aim[:, PIX : PIX + 1] == 1.0, (guess - aim[:, 0:PIX].astype(F32)) * 0.0625, 0.0
    ).astype(BF16)
    grad_top = lax.dot_general(
        misfit, head[...], (((1,), (1,)), ((), ())), preferred_element_type=F32
    )
    grad_two = pull_back(unit, scale, grad_top).astype(BF16)
    grad_mid = grad_top[8:424] + conv_back(grad_two, weight, 416)
    grad_one = pull_back(unit_ref[...], scale_ref[:, 0:1], grad_mid)
    grad_one = jnp.where(rows_valid(416, 1), grad_one, 0.0)
    grad_out[...] = grad_one.astype(BF16)
    mid_out[...] = grad_mid[8:408]
    share = jnp.where(lax.axis_index("freq") == 1, grad_two.astype(F32)[16:416], grad_one[8:408])
    pieces = quarters(share)
    lane = lax.broadcasted_iota(jnp.int32, (CELLS, 128), 1)
    for step, share_out in enumerate((share_own, share_one, share_two, share_three)):
        quarter = (lax.axis_index("tm_0") + step) & 3
        piece = jnp.where(quarter == 0, pieces[0], pieces[1])
        piece = jnp.where(quarter >= 2, jnp.where(quarter == 2, pieces[2], pieces[3]), piece)
        share_out[...] = jnp.where(lane < 96, piece, 0.0).astype(BF16)


def tail_kernel(grad_ref, mid_ref, weight, chosen, out):
    grad_cells = mid_ref[...] + conv_back(grad_ref[...], weight, CELLS)
    out[...] = jnp.dot(chosen[...], grad_cells.astype(BF16), preferred_element_type=F32)


def turn_kernel(*refs):
    for part in range(4):
        refs[4][part] = refs[part][...].astype(F32).T.astype(BF16)


def weight_kernel(turned, *refs):
    outers, picked = refs[0:4], refs[4]
    out, moved, total = refs[5:]
    summed = None
    for part in range(4):
        low, middle, high = column_shifted(outers[part][...].astype(F32))
        for row_off in range(3):
            for col_off, piece in enumerate((high, middle, low)):
                rows = [piece]
                if row_off:
                    rows.insert(0, jnp.zeros((8 * row_off, 128), F32))
                if row_off < 2:
                    rows.append(jnp.zeros((16 - 8 * row_off, 128), F32))
                tap = 3 * row_off + col_off
                moved[part, :, tap * 128 : (tap + 1) * 128] = jnp.concatenate(
                    rows, axis=0
                ).astype(BF16)
        term = jnp.dot(turned[part], moved[part], preferred_element_type=F32)
        summed = term if summed is None else summed + term
    for tap in range(9):
        total[tap * CHANNELS : (tap + 1) * CHANNELS] = summed[:, tap * 128 : (tap + 1) * 128]
    total[9 * CHANNELS :] = jnp.zeros((8, 128), F32)
    row = lax.broadcasted_iota(jnp.int32, (16, CHANNELS), 0)
    for shard in range(64):
        start = 54 * shard
        packed = joined([total[start + 14 * part : start + 14 * part + 16] for part in range(4)])
        back = picked[8 * shard : 8 * shard + 8]
        packed = jnp.where(row >= 14, jnp.concatenate([back, back], axis=0), packed)
        out[shard] = packed.astype(BF16)


def finish_kernel(arrived, where_ref, in_weight, token_out, conv_out):
    count = where_ref.shape[0]
    rows = arrived.shape[0] * 16
    index = lax.broadcasted_iota(jnp.int32, (count, rows), 1)
    within = index & 15
    slot = lax.shift_right_logical(index, 4) * 2 + within - 14
    hit = (where_ref[:, 0:1].astype(jnp.int32) == slot) & (within >= 14)
    grad_proj = jnp.dot(
        jnp.where(hit, 1.0, 0.0).astype(BF16),
        arrived[...].reshape(rows, CHANNELS),
        preferred_element_type=F32,
    ).astype(BF16)
    token_out[...] = lax.dot_general(
        grad_proj, in_weight[...], (((1,), (1,)), ((), ())), preferred_element_type=F32
    )
    for layer in range(2):
        parts = []
        for peer in range(4):
            summed = None
            for near in range(8):
                term = arrived[16 * peer + 2 * near + layer].astype(F32)
                summed = term if summed is None else summed + term
            parts.append(quarters(summed))
        for group in range(4):
            height = min(14, 54 - 14 * group)
            wide = joined([parts[peer][group] for peer in range(4)])
            conv_out[layer, 14 * group : 14 * group + height] = wide[0:height]


VMEM = pl.BlockSpec(memory_space=pltpu.VMEM)


def call(kernel, shapes, scratch, cost, limit, *operands):
    return pl.pallas_call(
        kernel,
        out_shape=shapes,
        in_specs=[VMEM] * len(operands),
        out_specs=jax.tree.map(lambda _: VMEM, shapes),
        scratch_shapes=scratch,
        compiler_params=pltpu.CompilerParams(vmem_limit_bytes=limit << 20),
        cost_estimate=pl.CostEstimate(
            flops=cost, bytes_accessed=cost // 400, transcendentals=0
        ),
    )(*operands)


def shape(dims, dtype=BF16):
    return jax.ShapeDtypeStruct(dims, dtype)


def send(value, axis, step, wrap):
    count = lax.axis_size(axis)
    pairs = [(i, (i + step) % count) for i in range(count)]
    if not wrap:
        pairs = [(i, i + step) for i in range(count) if 0 <= i + step < count]
    return lax.ppermute(value, axis, pairs)


def per_device(
    tokens, placement, patch_mask, targets, in_weight, mask_token, conv_weight, head_weight
):
    shards = lax.axis_size(TM_FREQ)
    core = lax.axis_index("freq")
    visible = tokens.shape[0]
    half = patch_mask.shape[1]

    packed, where_to = call(
        pack_kernel,
        (shape((shards * 8, 256)), shape((visible, 128), F32)),
        [],
        80_000_000,
        62,
        tokens,
        placement,
        in_weight,
    )
    arrived = lax.all_to_all(packed, TM_FREQ, split_axis=0, concat_axis=0, tiled=True)
    flags = jnp.broadcast_to((patch_mask == 1)[:, :, None], (*patch_mask.shape, 128))
    aim = jnp.concatenate([targets, flags.astype(BF16)], axis=2).reshape(-1, PIX + 128)

    other = send(aim, "freq", 1, True)
    weights = [conv_weight[layer : layer + 1] for layer in range(2)]

    own, aim, down, up, chosen = call(
        place_kernel,
        (
            shape((CELLS, CHANNELS)),
            shape((CELLS, PIX + 128)),
            shape((48, CHANNELS)),
            shape((48, CHANNELS)),
            shape((shards * 8, CELLS)),
        ),
        [],
        300_000_000,
        8,
        arrived,
        aim,
        other,
        mask_token[None, :],
    )
    above = send(down, TM, 1, False)
    below = send(up, TM, -1, False)
    columns = [pltpu.VMEM((464, DEPTH), BF16), pltpu.VMEM((464, DEPTH), BF16)]
    active, unit, scale, inner = call(
        first_kernel,
        (
            shape((448, CHANNELS)),
            shape((416, CHANNELS), F32),
            shape((416, 128), F32),
            shape((416, CHANNELS)),
        ),
        columns,
        1_500_000_000,
        12,
        above,
        own,
        below,
        weights[0],
    )
    inners = [inner] + [send(inner, "tm_0", step, True) for step in (1, 2, 3)]
    pred, *outers, mid, grad = call(
        second_kernel,
        (
            shape((CELLS, PIX)),
            *[shape((CELLS, 128))] * 4,
            shape((CELLS, CHANNELS), F32),
            shape((416, CHANNELS)),
        ),
        columns,
        3_500_000_000,
        18,
        active,
        unit,
        scale,
        weights[1],
        head_weight,
        above,
        aim,
        below,
    )
    outers[1:] = [send(outers[step], "tm_0", step, True) for step in (1, 2, 3)]
    picked = call(
        tail_kernel,
        shape((shards * 8, CHANNELS), F32),
        [],
        1_200_000_000,
        12,
        grad,
        mid,
        weights[0],
        chosen,
    )
    turned = call(turn_kernel, shape((4, CHANNELS, 416)), [], 400_000_000, 8, *inners)
    terms = call(
        weight_kernel,
        shape((shards, 16, CHANNELS)),
        [pltpu.VMEM((4, 416, 9 * 128), BF16), pltpu.VMEM((9 * CHANNELS + 8, 128), F32)],
        1_500_000_000,
        16,
        turned,
        *outers,
        picked,
    )
    terms = lax.all_to_all(terms, TM_FREQ, split_axis=0, concat_axis=0, tiled=True)
    token_grad, conv_grad = call(
        finish_kernel,
        (shape((visible, in_weight.shape[0]), F32), shape((2, 54, CHANNELS), F32)),
        [],
        80_000_000,
        6,
        terms,
        where_to,
        in_weight,
    )
    pred = lax.dynamic_slice_in_dim(pred.reshape(ROWS, COLS, PIX), core * half, half, axis=1)
    return (pred, token_grad, conv_grad)


def solution(mesh):
    split = Mesh(
        mesh.devices.reshape(4, 8, mesh.shape["freq"], mesh.shape["rec"]),
        ("tm_0", "tm_1", "freq", "rec"),
    )
    placed = (
        P(REC_TM_FREQ, None),
        P(None, REC_TM_FREQ),
        P(REC_TM, "freq"),
        P(REC_TM, "freq", None),
        P(),
        P(),
        P(),
        P(),
    )
    return jax.shard_map(
        per_device,
        mesh=split,
        in_specs=placed,
        out_specs=(P(REC_TM, "freq", None), P(REC_TM_FREQ, None), P("rec", TM_FREQ, None)),
        check_vma=False,
    )
```

```python
import jax
import jax.numpy as jnp
from jax import lax
from jax.experimental import pallas as pl
from jax.experimental.pallas import tpu as pltpu
from jax.sharding import Mesh
from jax.sharding import PartitionSpec as P


TM = ("tm_0", "tm_1")
TM_FREQ = ("tm_0", "tm_1", "freq")
REC_TM_FREQ = ("rec", "tm_0", "tm_1", "freq")
REC_TM = ("rec", "tm_0", "tm_1")

F32 = jnp.float32
BF16 = jnp.bfloat16
ROWS = 50
COLS = 8
CELLS = ROWS * COLS
CHANNELS = 384
DEPTH = 3 * CHANNELS
PIX = 256
ERF_SCALE = 0.7071067811865476
PDF_SCALE = 0.3989422804014327
ERF_TOP = (
    0.00022905065861350646,
    0.0034082910107109506,
    0.050955695062380861,
    0.18520832239976145,
    1.128379143519084,
)
ERF_BOTTOM = (
    -1.1791602954361697e-7,
    0.000023547966471313185,
    0.0010179625278914885,
    0.014070470171167667,
    0.11098505178285362,
    0.49746925110067538,
    1.0,
)


def horner(value, factors):
    total = jnp.full_like(value, factors[0])
    for factor in factors[1:]:
        total = total * value + factor
    return total


def erf(value):
    bounded = jnp.clip(value, -3.7439211627767994, 3.7439211627767994)
    square = bounded * bounded
    return bounded * horner(square, ERF_TOP) / horner(square, ERF_BOTTOM)


def half_erf(unit):
    return 0.5 * (1.0 + erf(unit * ERF_SCALE))


def column_shifted(value):
    cells, channels = value.shape
    grid = value.reshape(cells // 8, 8, channels)
    column = lax.broadcasted_iota(jnp.int32, grid.shape, 1)
    lower = jnp.where(column == 0, 0.0, pltpu.roll(grid, 1, axis=1))
    upper = jnp.where(column == 7, 0.0, pltpu.roll(grid, 7, axis=1))
    return lower.reshape(value.shape), value, upper.reshape(value.shape)


def store_columns(value, even, odd):
    cells, channels = value.shape
    for part, shifted in enumerate(column_shifted(value)):
        lanes = slice(part * channels, (part + 1) * channels)
        even[0:cells, lanes] = shifted.astype(BF16)
        odd[0 : cells - 8, lanes] = shifted[8:].astype(BF16)


def conv_taps(even, odd, taps, cells):
    summed = None
    for part, window in enumerate((even[0:cells], odd[0:cells], even[16 : 16 + cells])):
        term = jnp.dot(
            window, taps[0, part * DEPTH : (part + 1) * DEPTH], preferred_element_type=F32
        )
        summed = term if summed is None else summed + term
    return summed


def conv_back(grad, taps, cells):
    summed = None
    for row_off in range(3):
        term = lax.dot_general(
            grad,
            taps[0, row_off * DEPTH : (row_off + 1) * DEPTH],
            (((1,), (1,)), ((), ())),
            preferred_element_type=F32,
        )
        term = term[8 * (2 - row_off) : 8 * (2 - row_off) + cells]
        summed = term if summed is None else summed + term
    grid = (cells // 8, 8, CHANNELS)
    column = lax.broadcasted_iota(jnp.int32, grid, 1)
    first = summed[:, 0:CHANNELS].reshape(grid)
    last = summed[:, 2 * CHANNELS :].reshape(grid)
    total = jnp.where(column == 7, 0.0, pltpu.roll(first, 7, axis=1))
    total += jnp.where(column == 0, 0.0, pltpu.roll(last, 1, axis=1))
    return summed[:, CHANNELS : 2 * CHANNELS] + total.reshape(cells, CHANNELS)


def quarters(value):
    tiles = [value[:, 128 * part : 128 * (part + 1)] for part in range(3)]
    lane = lax.broadcasted_iota(jnp.int32, tiles[0].shape, 1)
    one = jnp.where(lane < 32, pltpu.roll(tiles[0], 32, axis=1), pltpu.roll(tiles[1], 32, axis=1))
    two = jnp.where(lane < 64, pltpu.roll(tiles[1], 64, axis=1), pltpu.roll(tiles[2], 64, axis=1))
    return tiles[0], one, two, pltpu.roll(tiles[2], 96, axis=1)


def joined(parts):
    lane = lax.broadcasted_iota(jnp.int32, parts[0].shape, 1)
    one = pltpu.roll(parts[1], 96, axis=1)
    two = pltpu.roll(parts[2], 64, axis=1)
    three = pltpu.roll(parts[3], 32, axis=1)
    tiles = (
        jnp.where(lane < 96, parts[0], one),
        jnp.where(lane < 64, one, two),
        jnp.where(lane < 32, two, three),
    )
    return jnp.concatenate(tiles, axis=1)


def normed(conv_out):
    center = conv_out - jnp.mean(conv_out, axis=-1, keepdims=True)
    scale = lax.rsqrt(jnp.mean(center * center, axis=-1, keepdims=True) + 1e-05)
    return center * scale, scale


def pull_back(unit, scale, gradient):
    slope = half_erf(unit) + unit * (PDF_SCALE * jnp.exp(-0.5 * unit * unit))
    grad = gradient * slope
    mean = jnp.mean(grad, axis=-1, keepdims=True)
    along = jnp.mean(grad * unit, axis=-1, keepdims=True)
    return scale * (grad - mean - unit * along)


def rows_valid(cells, before):
    row = lax.shift_right_logical(lax.broadcasted_iota(jnp.int32, (cells, 1), 0), 3)
    row = row + lax.axis_index(TM) * ROWS - before
    return (row >= 0) & (row < lax.axis_size(TM) * ROWS)


def pack_kernel(tokens, placement, weight_ref, packed, where_out, in_weight, arrival):
    load = pltpu.make_async_copy(weight_ref, in_weight, arrival)
    load.start()
    count = tokens.shape[0]
    rows = placement[0:1, :].astype(F32)
    cols = placement[1:2, :].astype(F32)
    tile_row = jnp.floor((rows + 0.5) * (1.0 / ROWS))
    tile = tile_row * 2.0 + jnp.where(cols >= 4.0, 1.0, 0.0)
    down = lax.broadcasted_iota(jnp.int32, (count, count), 0)
    across = lax.broadcasted_iota(jnp.int32, (count, count), 1)

    def column(value):
        return jnp.sum(jnp.where(down == across, value, 0.0), axis=1, keepdims=True)

    earlier = jnp.where((column(tile) == tile) & (down < across), 1.0, 0.0)
    where_to = tile * 2.0 + jnp.sum(earlier, axis=0, keepdims=True)
    where_out[...] = jnp.broadcast_to(column(where_to), where_out.shape)
    index = lax.broadcasted_iota(jnp.int32, (packed.shape[0], 1), 0)
    wanted = lax.shift_right_logical(index, 4) * 4 + (index & 3)
    match = jnp.where(wanted.astype(F32) == where_to, 1.0, 0.0).astype(BF16)
    load.wait()
    proj = jnp.dot(tokens[...], in_weight[...], preferred_element_type=F32).astype(BF16)
    lane = lax.broadcasted_iota(jnp.int32, (count, 128), 1)
    notes = jnp.where(lane == 1, column(cols), jnp.where(lane == 2, 1.0, 0.0))
    notes = jnp.where(lane == 0, column(rows - tile_row * ROWS), notes).astype(BF16)
    low = jnp.dot(match, proj[:, 0:256], preferred_element_type=F32)
    rest = jnp.concatenate([proj[:, 256:384], notes], axis=1)
    high = jnp.dot(match, rest, preferred_element_type=F32)
    packed[...] = jnp.where((index & 4) == 0, low, high).astype(BF16)


def order_kernel(own_aim, other_aim, aim_out):
    core = lax.axis_index("freq")
    number = lax.broadcasted_iota(jnp.int32, (CELLS, 1), 0)
    far = (lax.shift_right_logical(number, 2) & 1) != core
    source = lax.shift_right_logical(number, 3) * 4 + (number & 3) + jnp.where(far, CELLS // 2, 0)
    order = lax.broadcasted_iota(jnp.int32, (CELLS, CELLS), 1) == source
    aim_out[...] = jnp.dot(
        jnp.where(order, 1.0, 0.0).astype(BF16),
        jnp.concatenate([own_aim[...].astype(F32), other_aim[...].astype(F32)], axis=0).astype(BF16),
        preferred_element_type=F32,
    ).astype(BF16)


def place_kernel(arrived, aim, token, x_out, down_out, up_out, chosen_out):
    core = lax.axis_index("freq")
    slots = arrived.shape[0]
    notes = arrived[:, 128:256].astype(F32).reshape(slots // 8, 8, 128)
    within = lax.broadcasted_iota(jnp.int32, notes.shape, 1)
    notes = jnp.where(within >= 4, notes, pltpu.roll(notes, 4, axis=1)).reshape(slots, 128)
    cell = jnp.where(notes[:, 2:3] == 1.0, notes[:, 0:1] * 8.0 + notes[:, 1:2], -1.0)
    lane = lax.broadcasted_iota(jnp.int32, (slots, CELLS), 1)
    index = lax.broadcasted_iota(jnp.int32, (slots, CELLS), 0)
    hit = lane == cell.astype(jnp.int32)

    def pick(flag):
        return lax.dot_general(
            jnp.where(hit & flag, 1.0, 0.0).astype(BF16),
            arrived[...],
            (((0,), (0,)), ((), ())),
            preferred_element_type=F32,
        )

    placed = jnp.concatenate([pick((index & 4) == 0), pick((index & 4) == 4)[:, 0:128]], axis=1)
    masked = aim[:, PIX : PIX + 1] == 1.0
    x = jnp.where(masked, token[...].astype(F32), placed).astype(BF16)
    x_out[...] = x
    down_out[0:32] = x[CELLS - 32 :]
    down_out[32:48] = aim[CELLS - 16 :]
    up_out[0:32] = x[0:32]
    up_out[32:48] = aim[0:16]
    spread = jnp.broadcast_to(cell, (slots, 128)).reshape(slots // 8, 8, 128)
    first = jnp.sum(jnp.where(within == 4 + 2 * core, spread, 0.0), axis=1, keepdims=True)
    second = jnp.sum(jnp.where(within == 5 + 2 * core, spread, 0.0), axis=1, keepdims=True)
    spread = jnp.where(within == 6, first, jnp.where(within == 7, second, -1.0))
    spread = spread.reshape(slots, 128)
    chosen_out[...] = jnp.where(lane == spread[:, 0:1].astype(jnp.int32), 1.0, 0.0).astype(BF16)


def first_kernel(
    above, own, below, weight, active_out, unit_out, scale_out, share_out, even, odd
):
    source = jnp.concatenate(
        [above[0:32].astype(F32), own[...].astype(F32), below[0:32].astype(F32)], axis=0
    )
    store_columns(source, even, odd)
    unit, scale = normed(conv_taps(even, odd, weight, 448))
    unit_out[...] = unit[16:432]
    scale_out[...] = jnp.broadcast_to(scale[16:432], (416, 128))
    active = source[8:456] + unit * half_erf(unit)
    active = jnp.where(rows_valid(448, 3), active, 0.0)
    active_out[...] = active.astype(BF16)
    share_out[...] = jnp.where(
        lax.axis_index("freq") == 1, active[16:432], source[24:440]
    ).astype(BF16)


def second_kernel(
    active_ref, unit_ref, scale_ref, weight, head, above, aim_ref, below,
    pred, share_own, share_one, share_two, share_three, mid_out, grad_out, even, odd,
):
    active = active_ref[...].astype(F32)
    store_columns(active, even, odd)
    unit, scale = normed(conv_taps(even, odd, weight, 432))
    top = (active[8:440] + unit * half_erf(unit)).astype(BF16)
    guess = jnp.dot(top, head[...], preferred_element_type=F32)
    pred[...] = guess[16:416].astype(BF16)
    aim = jnp.concatenate([above[32:48], aim_ref[...], below[32:48]], axis=0)
    misfit = jnp.where(
        aim[:, PIX : PIX + 1] == 1.0, (guess - aim[:, 0:PIX].astype(F32)) * 0.0625, 0.0
    ).astype(BF16)
    grad_top = lax.dot_general(
        misfit, head[...], (((1,), (1,)), ((), ())), preferred_element_type=F32
    )
    grad_two = pull_back(unit, scale, grad_top).astype(BF16)
    grad_mid = grad_top[8:424] + conv_back(grad_two, weight, 416)
    grad_one = pull_back(unit_ref[...], scale_ref[:, 0:1], grad_mid)
    grad_one = jnp.where(rows_valid(416, 1), grad_one, 0.0)
    grad_out[...] = grad_one.astype(BF16)
    mid_out[...] = grad_mid[8:408]
    share = jnp.where(lax.axis_index("freq") == 1, grad_two.astype(F32)[16:416], grad_one[8:408])
    pieces = quarters(share)
    lane = lax.broadcasted_iota(jnp.int32, (CELLS, 128), 1)
    for step, share_out in enumerate((share_own, share_one, share_two, share_three)):
        quarter = (lax.axis_index("tm_0") + step) & 3
        piece = jnp.where(quarter == 0, pieces[0], pieces[1])
        piece = jnp.where(quarter >= 2, jnp.where(quarter == 2, pieces[2], pieces[3]), piece)
        share_out[...] = jnp.where(lane < 96, piece, 0.0).astype(BF16)


def tail_kernel(grad_ref, mid_ref, weight, chosen, out):
    grad_cells = mid_ref[...] + conv_back(grad_ref[...], weight, CELLS)
    out[...] = jnp.dot(chosen[...], grad_cells.astype(BF16), preferred_element_type=F32)


def turn_kernel(*refs):
    for part in range(4):
        refs[4][part] = refs[part][...].astype(F32).T.astype(BF16)


def weight_kernel(turned, *refs):
    outers, picked = refs[0:4], refs[4]
    out, moved, total = refs[5:]
    summed = None
    for part in range(4):
        low, middle, high = column_shifted(outers[part][...].astype(F32))
        for row_off in range(3):
            for col_off, piece in enumerate((high, middle, low)):
                rows = [piece]
                if row_off:
                    rows.insert(0, jnp.zeros((8 * row_off, 128), F32))
                if row_off < 2:
                    rows.append(jnp.zeros((16 - 8 * row_off, 128), F32))
                tap = 3 * row_off + col_off
                moved[part, :, tap * 128 : (tap + 1) * 128] = jnp.concatenate(
                    rows, axis=0
                ).astype(BF16)
        term = jnp.dot(turned[part], moved[part], preferred_element_type=F32)
        summed = term if summed is None else summed + term
    for tap in range(9):
        total[tap * CHANNELS : (tap + 1) * CHANNELS] = summed[:, tap * 128 : (tap + 1) * 128]
    total[9 * CHANNELS :] = jnp.zeros((8, 128), F32)
    row = lax.broadcasted_iota(jnp.int32, (16, CHANNELS), 0)
    for shard in range(64):
        start = 54 * shard
        packed = joined([total[start + 14 * part : start + 14 * part + 16] for part in range(4)])
        back = picked[8 * shard : 8 * shard + 8]
        packed = jnp.where(row >= 14, jnp.concatenate([back, back], axis=0), packed)
        out[shard] = packed.astype(BF16)


def finish_kernel(arrived, where_ref, in_weight, token_out, conv_out):
    count = where_ref.shape[0]
    rows = arrived.shape[0] * 16
    index = lax.broadcasted_iota(jnp.int32, (count, rows), 1)
    within = index & 15
    slot = lax.shift_right_logical(index, 4) * 2 + within - 14
    hit = (where_ref[:, 0:1].astype(jnp.int32) == slot) & (within >= 14)
    grad_proj = jnp.dot(
        jnp.where(hit, 1.0, 0.0).astype(BF16),
        arrived[...].reshape(rows, CHANNELS),
        preferred_element_type=F32,
    ).astype(BF16)
    token_out[...] = lax.dot_general(
        grad_proj, in_weight[...], (((1,), (1,)), ((), ())), preferred_element_type=F32
    )
    for layer in range(2):
        parts = []
        for peer in range(4):
            summed = None
            for near in range(8):
                term = arrived[16 * peer + 2 * near + layer].astype(F32)
                summed = term if summed is None else summed + term
            parts.append(quarters(summed))
        for group in range(4):
            height = min(14, 54 - 14 * group)
            wide = joined([parts[peer][group] for peer in range(4)])
            conv_out[14 * group : 14 * group + height, layer] = wide[0:height]


VMEM = pl.BlockSpec(memory_space=pltpu.VMEM)
ANY = pl.BlockSpec(memory_space=pl.ANY)


def call(kernel, shapes, scratch, cost, limit, *operands, far=-1):
    return pl.pallas_call(
        kernel,
        out_shape=shapes,
        in_specs=[ANY if i == far else VMEM for i in range(len(operands))],
        out_specs=jax.tree.map(lambda _: VMEM, shapes),
        scratch_shapes=scratch,
        compiler_params=pltpu.CompilerParams(vmem_limit_bytes=limit << 20),
        cost_estimate=pl.CostEstimate(
            flops=cost, bytes_accessed=cost // 400, transcendentals=0
        ),
    )(*operands)


def shape(dims, dtype=BF16):
    return jax.ShapeDtypeStruct(dims, dtype)


def send(value, axis, step, wrap):
    count = lax.axis_size(axis)
    pairs = [(i, (i + step) % count) for i in range(count)]
    if not wrap:
        pairs = [(i, i + step) for i in range(count) if 0 <= i + step < count]
    return lax.ppermute(value, axis, pairs)


def per_device(
    tokens, placement, patch_mask, targets, in_weight, mask_token, conv_weight, head_weight
):
    shards = lax.axis_size(TM_FREQ)
    core = lax.axis_index("freq")
    visible = tokens.shape[0]
    half = patch_mask.shape[1]

    packed, where_to = call(
        pack_kernel,
        (shape((shards * 8, 256)), shape((visible, 128), F32)),
        [pltpu.VMEM(in_weight.shape, BF16), pltpu.SemaphoreType.DMA],
        80_000_000,
        62,
        tokens,
        placement,
        in_weight,
        far=2,
    )
    arrived = lax.all_to_all(packed, TM_FREQ, split_axis=0, concat_axis=0, tiled=True)
    flags = jnp.broadcast_to((patch_mask == 1)[:, :, None], (*patch_mask.shape, 128))
    aim = jnp.concatenate([targets, flags.astype(BF16)], axis=2).reshape(-1, PIX + 128)

    other = send(aim, "freq", 1, True)
    aim = call(order_kernel, shape((CELLS, PIX + 128)), [], 200_000_000, 8, aim, other)
    weights = [conv_weight[layer : layer + 1] for layer in range(2)]

    own, down, up, chosen = call(
        place_kernel,
        (
            shape((CELLS, CHANNELS)),
            shape((48, CHANNELS)),
            shape((48, CHANNELS)),
            shape((shards * 8, CELLS)),
        ),
        [],
        300_000_000,
        8,
        arrived,
        aim,
        mask_token[None, :],
    )
    above = send(down, TM, 1, False)
    below = send(up, TM, -1, False)
    columns = [pltpu.VMEM((464, DEPTH), BF16), pltpu.VMEM((464, DEPTH), BF16)]
    active, unit, scale, inner = call(
        first_kernel,
        (
            shape((448, CHANNELS)),
            shape((416, CHANNELS), F32),
            shape((416, 128), F32),
            shape((416, CHANNELS)),
        ),
        columns,
        1_500_000_000,
        12,
        above,
        own,
        below,
        weights[0],
    )
    inners = [inner] + [send(inner, "tm_0", step, True) for step in (1, 2, 3)]
    pred, *outers, mid, grad = call(
        second_kernel,
        (
            shape((CELLS, PIX)),
            *[shape((CELLS, 128))] * 4,
            shape((CELLS, CHANNELS), F32),
            shape((416, CHANNELS)),
        ),
        columns,
        3_500_000_000,
        18,
        active,
        unit,
        scale,
        weights[1],
        head_weight,
        above,
        aim,
        below,
    )
    outers[1:] = [send(outers[step], "tm_0", step, True) for step in (1, 2, 3)]
    picked = call(
        tail_kernel,
        shape((shards * 8, CHANNELS), F32),
        [],
        1_200_000_000,
        12,
        grad,
        mid,
        weights[0],
        chosen,
    )
    turned = call(turn_kernel, shape((4, CHANNELS, 416)), [], 400_000_000, 8, *inners)
    terms = call(
        weight_kernel,
        shape((shards, 16, CHANNELS)),
        [pltpu.VMEM((4, 416, 9 * 128), BF16), pltpu.VMEM((9 * CHANNELS + 8, 128), F32)],
        1_500_000_000,
        16,
        turned,
        *outers,
        picked,
    )
    terms = lax.all_to_all(terms, TM_FREQ, split_axis=0, concat_axis=0, tiled=True)
    token_grad, conv_grad = call(
        finish_kernel,
        (shape((visible, in_weight.shape[0]), F32), shape((54, 2, CHANNELS), F32)),
        [],
        80_000_000,
        6,
        terms,
        where_to,
        in_weight,
    )
    conv_grad = conv_grad.transpose(1, 0, 2)
    pred = lax.dynamic_slice_in_dim(pred.reshape(ROWS, COLS, PIX), core * half, half, axis=1)
    return (pred, token_grad, conv_grad)


def solution(mesh):
    split = Mesh(
        mesh.devices.reshape(4, 8, mesh.shape["freq"], mesh.shape["rec"]),
        ("tm_0", "tm_1", "freq", "rec"),
    )
    placed = (
        P(REC_TM_FREQ, None),
        P(None, REC_TM_FREQ),
        P(REC_TM, "freq"),
        P(REC_TM, "freq", None),
        P(),
        P(),
        P(),
        P(),
    )
    return jax.shard_map(
        per_device,
        mesh=split,
        in_specs=placed,
        out_specs=(P(REC_TM, "freq", None), P(REC_TM_FREQ, None), P("rec", TM_FREQ, None)),
        check_vma=False,
    )
```

```python
import jax
import jax.numpy as jnp
from jax import lax
from jax.experimental import pallas as pl
from jax.experimental.pallas import tpu as pltpu
from jax.sharding import Mesh
from jax.sharding import PartitionSpec as P


TM = ("tm_0", "tm_1")
TM_FREQ = ("tm_0", "tm_1", "freq")
REC_TM_FREQ = ("rec", "tm_0", "tm_1", "freq")
REC_TM = ("rec", "tm_0", "tm_1")

F32 = jnp.float32
BF16 = jnp.bfloat16
ROWS = 50
COLS = 8
CELLS = ROWS * COLS
CHANNELS = 384
DEPTH = 3 * CHANNELS
PIX = 256
ERF_SCALE = 0.7071067811865476
PDF_SCALE = 0.3989422804014327
ERF_TOP = (
    0.00022905065861350646,
    0.0034082910107109506,
    0.050955695062380861,
    0.18520832239976145,
    1.128379143519084,
)
ERF_BOTTOM = (
    -1.1791602954361697e-7,
    0.000023547966471313185,
    0.0010179625278914885,
    0.014070470171167667,
    0.11098505178285362,
    0.49746925110067538,
    1.0,
)


def horner(value, factors):
    total = jnp.full_like(value, factors[0])
    for factor in factors[1:]:
        total = total * value + factor
    return total


def erf(value):
    bounded = jnp.clip(value, -3.7439211627767994, 3.7439211627767994)
    square = bounded * bounded
    return bounded * horner(square, ERF_TOP) / horner(square, ERF_BOTTOM)


def half_erf(unit):
    return 0.5 * (1.0 + erf(unit * ERF_SCALE))


def column_shifted(value):
    cells, channels = value.shape
    grid = value.reshape(cells // 8, 8, channels)
    column = lax.broadcasted_iota(jnp.int32, grid.shape, 1)
    lower = jnp.where(column == 0, 0.0, pltpu.roll(grid, 1, axis=1))
    upper = jnp.where(column == 7, 0.0, pltpu.roll(grid, 7, axis=1))
    return lower.reshape(value.shape), value, upper.reshape(value.shape)


def store_columns(value, even, odd):
    cells, channels = value.shape
    for part, shifted in enumerate(column_shifted(value)):
        lanes = slice(part * channels, (part + 1) * channels)
        even[0:cells, lanes] = shifted.astype(BF16)
        odd[0 : cells - 8, lanes] = shifted[8:].astype(BF16)


def conv_taps(windows, taps):
    summed = None
    for part, window in enumerate(windows):
        term = jnp.dot(
            window, taps[0, part * DEPTH : (part + 1) * DEPTH], preferred_element_type=F32
        )
        summed = term if summed is None else summed + term
    return summed


def conv_back(grad, taps, cells):
    summed = None
    for row_off in range(3):
        term = lax.dot_general(
            grad,
            taps[0, row_off * DEPTH : (row_off + 1) * DEPTH],
            (((1,), (1,)), ((), ())),
            preferred_element_type=F32,
        )
        term = term[8 * (2 - row_off) : 8 * (2 - row_off) + cells]
        summed = term if summed is None else summed + term
    grid = (cells // 8, 8, CHANNELS)
    column = lax.broadcasted_iota(jnp.int32, grid, 1)
    first = summed[:, 0:CHANNELS].reshape(grid)
    last = summed[:, 2 * CHANNELS :].reshape(grid)
    total = jnp.where(column == 7, 0.0, pltpu.roll(first, 7, axis=1))
    total += jnp.where(column == 0, 0.0, pltpu.roll(last, 1, axis=1))
    return summed[:, CHANNELS : 2 * CHANNELS] + total.reshape(cells, CHANNELS)


def quarters(value):
    tiles = [value[:, 128 * part : 128 * (part + 1)] for part in range(3)]
    lane = lax.broadcasted_iota(jnp.int32, tiles[0].shape, 1)
    one = jnp.where(lane < 32, pltpu.roll(tiles[0], 32, axis=1), pltpu.roll(tiles[1], 32, axis=1))
    two = jnp.where(lane < 64, pltpu.roll(tiles[1], 64, axis=1), pltpu.roll(tiles[2], 64, axis=1))
    return tiles[0], one, two, pltpu.roll(tiles[2], 96, axis=1)


def joined(parts):
    lane = lax.broadcasted_iota(jnp.int32, parts[0].shape, 1)
    one = pltpu.roll(parts[1], 96, axis=1)
    two = pltpu.roll(parts[2], 64, axis=1)
    three = pltpu.roll(parts[3], 32, axis=1)
    tiles = (
        jnp.where(lane < 96, parts[0], one),
        jnp.where(lane < 64, one, two),
        jnp.where(lane < 32, two, three),
    )
    return jnp.concatenate(tiles, axis=1)


def normed(conv_out):
    center = conv_out - jnp.mean(conv_out, axis=-1, keepdims=True)
    scale = lax.rsqrt(jnp.mean(center * center, axis=-1, keepdims=True) + 1e-05)
    return center * scale, scale


def pull_back(unit, scale, gradient):
    slope = half_erf(unit) + unit * (PDF_SCALE * jnp.exp(-0.5 * unit * unit))
    grad = gradient * slope
    mean = jnp.mean(grad, axis=-1, keepdims=True)
    along = jnp.mean(grad * unit, axis=-1, keepdims=True)
    return scale * (grad - mean - unit * along)


def rows_valid(row):
    row = row + lax.axis_index(TM) * ROWS
    return (row >= 0) & (row < lax.axis_size(TM) * ROWS)


def row_number(cells):
    return lax.shift_right_logical(lax.broadcasted_iota(jnp.int32, (cells, 1), 0), 3)


def pack_kernel(tokens, placement, in_weight, packed, where_out):
    count = tokens.shape[0]
    rows = placement[0:1, :].astype(F32)
    cols = placement[1:2, :].astype(F32)
    tile_row = jnp.floor((rows + 0.5) * (1.0 / ROWS))
    tile = tile_row * 2.0 + jnp.where(cols >= 4.0, 1.0, 0.0)
    down = lax.broadcasted_iota(jnp.int32, (count, count), 0)
    across = lax.broadcasted_iota(jnp.int32, (count, count), 1)

    def column(value):
        return jnp.sum(jnp.where(down == across, value, 0.0), axis=1, keepdims=True)

    earlier = jnp.where((column(tile) == tile) & (down < across), 1.0, 0.0)
    where_to = tile * 2.0 + jnp.sum(earlier, axis=0, keepdims=True)
    where_out[...] = jnp.broadcast_to(column(where_to), where_out.shape)
    index = lax.broadcasted_iota(jnp.int32, (packed.shape[0], 1), 0)
    wanted = lax.shift_right_logical(index, 4) * 4 + (index & 3)
    match = jnp.where(wanted.astype(F32) == where_to, 1.0, 0.0).astype(BF16)
    proj = jnp.dot(tokens[...], in_weight[...], preferred_element_type=F32).astype(BF16)
    lane = lax.broadcasted_iota(jnp.int32, (count, 128), 1)
    notes = jnp.where(lane == 1, column(cols), jnp.where(lane == 2, 1.0, 0.0))
    notes = jnp.where(lane == 0, column(rows - tile_row * ROWS), notes).astype(BF16)
    low = jnp.dot(match, proj[:, 0:256], preferred_element_type=F32)
    rest = jnp.concatenate([proj[:, 256:384], notes], axis=1)
    high = jnp.dot(match, rest, preferred_element_type=F32)
    packed[...] = jnp.where((index & 4) == 0, low, high).astype(BF16)


def order_kernel(own_aim, other_aim, aim_out):
    core = lax.axis_index("freq")
    number = lax.broadcasted_iota(jnp.int32, (CELLS, 1), 0)
    far = (lax.shift_right_logical(number, 2) & 1) != core
    source = lax.shift_right_logical(number, 3) * 4 + (number & 3) + jnp.where(far, CELLS // 2, 0)
    order = lax.broadcasted_iota(jnp.int32, (CELLS, CELLS), 1) == source
    aim_out[...] = jnp.dot(
        jnp.where(order, 1.0, 0.0).astype(BF16),
        jnp.concatenate([own_aim[...].astype(F32), other_aim[...].astype(F32)], axis=0).astype(BF16),
        preferred_element_type=F32,
    ).astype(BF16)


def place_kernel(arrived, aim, token, x_out, down_out, up_out, chosen_out):
    core = lax.axis_index("freq")
    slots = arrived.shape[0]
    notes = arrived[:, 128:256].astype(F32).reshape(slots // 8, 8, 128)
    within = lax.broadcasted_iota(jnp.int32, notes.shape, 1)
    notes = jnp.where(within >= 4, notes, pltpu.roll(notes, 4, axis=1)).reshape(slots, 128)
    cell = jnp.where(notes[:, 2:3] == 1.0, notes[:, 0:1] * 8.0 + notes[:, 1:2], -1.0)
    lane = lax.broadcasted_iota(jnp.int32, (slots, CELLS), 1)
    index = lax.broadcasted_iota(jnp.int32, (slots, CELLS), 0)
    hit = lane == cell.astype(jnp.int32)

    def pick(flag):
        return lax.dot_general(
            jnp.where(hit & flag, 1.0, 0.0).astype(BF16),
            arrived[...],
            (((0,), (0,)), ((), ())),
            preferred_element_type=F32,
        )

    placed = jnp.concatenate([pick((index & 4) == 0), pick((index & 4) == 4)[:, 0:128]], axis=1)
    masked = aim[:, PIX : PIX + 1] == 1.0
    x = jnp.where(masked, token[...].astype(F32), placed).astype(BF16)
    x_out[...] = x
    down_out[0:32] = x[CELLS - 32 :]
    down_out[32:48] = aim[CELLS - 16 :]
    up_out[0:32] = x[0:32]
    up_out[32:48] = aim[0:16]
    spread = jnp.broadcast_to(cell, (slots, 128)).reshape(slots // 8, 8, 128)
    first = jnp.sum(jnp.where(within == 4 + 2 * core, spread, 0.0), axis=1, keepdims=True)
    second = jnp.sum(jnp.where(within == 5 + 2 * core, spread, 0.0), axis=1, keepdims=True)
    spread = jnp.where(within == 6, first, jnp.where(within == 7, second, -1.0))
    spread = spread.reshape(slots, 128)
    chosen_out[...] = jnp.where(lane == spread[:, 0:1].astype(jnp.int32), 1.0, 0.0).astype(BF16)


def inside_kernel(own, weight, active_out, unit_out, scale_out, even, odd):
    source = own[...].astype(F32)
    store_columns(source, even, odd)
    unit, scale = normed(conv_taps((even[0:384], odd[0:384], even[16:400]), weight))
    unit_out[...] = unit
    scale_out[...] = jnp.broadcast_to(scale, scale_out.shape)
    active_out[...] = (source[8:392] + unit * half_erf(unit)).astype(BF16)


def first_kernel(
    above, own, below, weight, active_in, unit_in, scale_in,
    active_out, unit_out, scale_out, share_out, even, odd,
):
    upper, lower = above[0:32].astype(F32), below[0:32].astype(F32)
    border = jnp.concatenate(
        [upper, own[0:16].astype(F32), own[384:400].astype(F32), lower], axis=0
    )
    store_columns(border, even, odd)
    windows = (
        jnp.concatenate([even[0:32], even[48:80]], axis=0),
        jnp.concatenate([odd[0:32], odd[48:80]], axis=0),
        jnp.concatenate([even[16:48], even[64:96]], axis=0),
    )
    unit, scale = normed(conv_taps(windows, weight))
    edge = jnp.concatenate([border[8:40], border[56:88]], axis=0) + unit * half_erf(unit)
    number = row_number(64)
    number = jnp.where(number < 4, number - 3, number + 45)
    edge = jnp.where(rows_valid(number), edge, 0.0)
    active_out[0:32] = edge[0:32].astype(BF16)
    active_out[32:416] = active_in[...]
    active_out[416:448] = edge[32:64].astype(BF16)
    unit_out[0:16] = unit[16:32]
    unit_out[16:400] = unit_in[...]
    unit_out[400:416] = unit[32:48]
    scale = jnp.broadcast_to(scale, (64, 128))
    scale_out[0:16] = scale[16:32]
    scale_out[16:400] = scale_in[...]
    scale_out[400:416] = scale[32:48]
    source = jnp.concatenate([upper[24:32], own[...].astype(F32), lower[0:8]], axis=0)
    active = jnp.concatenate([edge[16:32], active_in[...].astype(F32), edge[32:48]], axis=0)
    share_out[...] = jnp.where(lax.axis_index("freq") == 1, active, source).astype(BF16)


def second_kernel(
    active_ref, unit_ref, scale_ref, weight, head, above, aim_ref, below,
    pred, share_own, share_one, share_two, share_three, mid_out, grad_out, even, odd,
):
    active = active_ref[...].astype(F32)
    store_columns(active, even, odd)
    unit, scale = normed(conv_taps((even[0:432], odd[0:432], even[16:448]), weight))
    top = (active[8:440] + unit * half_erf(unit)).astype(BF16)
    guess = jnp.dot(top, head[...], preferred_element_type=F32)
    pred[...] = guess[16:416].astype(BF16)
    aim = jnp.concatenate([above[32:48], aim_ref[...], below[32:48]], axis=0)
    misfit = jnp.where(
        aim[:, PIX : PIX + 1] == 1.0, (guess - aim[:, 0:PIX].astype(F32)) * 0.0625, 0.0
    ).astype(BF16)
    grad_top = lax.dot_general(
        misfit, head[...], (((1,), (1,)), ((), ())), preferred_element_type=F32
    )
    grad_two = pull_back(unit, scale, grad_top).astype(BF16)
    grad_mid = grad_top[8:424] + conv_back(grad_two, weight, 416)
    grad_one = pull_back(unit_ref[...], scale_ref[:, 0:1], grad_mid)
    grad_one = jnp.where(rows_valid(row_number(416) - 1), grad_one, 0.0)
    grad_out[...] = grad_one.astype(BF16)
    mid_out[...] = grad_mid[8:408]
    share = jnp.where(lax.axis_index("freq") == 1, grad_two.astype(F32)[16:416], grad_one[8:408])
    pieces = quarters(share)
    lane = lax.broadcasted_iota(jnp.int32, (CELLS, 128), 1)
    for step, share_out in enumerate((share_own, share_one, share_two, share_three)):
        quarter = (lax.axis_index("tm_0") + step) & 3
        piece = jnp.where(quarter == 0, pieces[0], pieces[1])
        piece = jnp.where(quarter >= 2, jnp.where(quarter == 2, pieces[2], pieces[3]), piece)
        share_out[...] = jnp.where(lane < 96, piece, 0.0).astype(BF16)


def tail_kernel(grad_ref, mid_ref, weight, chosen, out):
    grad_cells = mid_ref[...] + conv_back(grad_ref[...], weight, CELLS)
    out[...] = jnp.dot(chosen[...], grad_cells.astype(BF16), preferred_element_type=F32)


def turn_kernel(*refs):
    for part in range(4):
        refs[4][part] = refs[part][...].astype(F32).T.astype(BF16)


def weight_kernel(turned, *refs):
    outers, picked = refs[0:4], refs[4]
    out, moved, total = refs[5:]
    summed = None
    for part in range(4):
        low, middle, high = column_shifted(outers[part][...].astype(F32))
        for row_off in range(3):
            for col_off, piece in enumerate((high, middle, low)):
                rows = [piece]
                if row_off:
                    rows.insert(0, jnp.zeros((8 * row_off, 128), F32))
                if row_off < 2:
                    rows.append(jnp.zeros((16 - 8 * row_off, 128), F32))
                tap = 3 * row_off + col_off
                moved[part, :, tap * 128 : (tap + 1) * 128] = jnp.concatenate(
                    rows, axis=0
                ).astype(BF16)
        term = jnp.dot(turned[part], moved[part], preferred_element_type=F32)
        summed = term if summed is None else summed + term
    for tap in range(9):
        total[tap * CHANNELS : (tap + 1) * CHANNELS] = summed[:, tap * 128 : (tap + 1) * 128]
    total[9 * CHANNELS :] = jnp.zeros((8, 128), F32)
    row = lax.broadcasted_iota(jnp.int32, (16, CHANNELS), 0)
    for shard in range(64):
        start = 54 * shard
        packed = joined([total[start + 14 * part : start + 14 * part + 16] for part in range(4)])
        back = picked[8 * shard : 8 * shard + 8]
        packed = jnp.where(row >= 14, jnp.concatenate([back, back], axis=0), packed)
        out[shard] = packed.astype(BF16)


def finish_kernel(arrived, where_ref, in_weight, token_out, conv_out):
    count = where_ref.shape[0]
    rows = arrived.shape[0] * 16
    index = lax.broadcasted_iota(jnp.int32, (count, rows), 1)
    within = index & 15
    slot = lax.shift_right_logical(index, 4) * 2 + within - 14
    hit = (where_ref[:, 0:1].astype(jnp.int32) == slot) & (within >= 14)
    grad_proj = jnp.dot(
        jnp.where(hit, 1.0, 0.0).astype(BF16),
        arrived[...].reshape(rows, CHANNELS),
        preferred_element_type=F32,
    ).astype(BF16)
    token_out[...] = lax.dot_general(
        grad_proj, in_weight[...], (((1,), (1,)), ((), ())), preferred_element_type=F32
    )
    for layer in range(2):
        parts = []
        for peer in range(4):
            summed = None
            for near in range(8):
                term = arrived[16 * peer + 2 * near + layer].astype(F32)
                summed = term if summed is None else summed + term
            parts.append(quarters(summed))
        for group in range(4):
            height = min(14, 54 - 14 * group)
            wide = joined([parts[peer][group] for peer in range(4)])
            conv_out[14 * group : 14 * group + height, layer] = wide[0:height]


VMEM = pl.BlockSpec(memory_space=pltpu.VMEM)


def call(kernel, shapes, scratch, cost, limit, *operands):
    return pl.pallas_call(
        kernel,
        out_shape=shapes,
        in_specs=[VMEM] * len(operands),
        out_specs=jax.tree.map(lambda _: VMEM, shapes),
        scratch_shapes=scratch,
        compiler_params=pltpu.CompilerParams(vmem_limit_bytes=limit << 20),
        cost_estimate=pl.CostEstimate(
            flops=cost, bytes_accessed=cost // 400, transcendentals=0
        ),
    )(*operands)


def shape(dims, dtype=BF16):
    return jax.ShapeDtypeStruct(dims, dtype)


def send(value, axis, step, wrap):
    count = lax.axis_size(axis)
    pairs = [(i, (i + step) % count) for i in range(count)]
    if not wrap:
        pairs = [(i, i + step) for i in range(count) if 0 <= i + step < count]
    return lax.ppermute(value, axis, pairs)


def per_device(
    tokens, placement, patch_mask, targets, in_weight, mask_token, conv_weight, head_weight
):
    shards = lax.axis_size(TM_FREQ)
    core = lax.axis_index("freq")
    visible = tokens.shape[0]
    half = patch_mask.shape[1]

    packed, where_to = call(
        pack_kernel,
        (shape((shards * 8, 256)), shape((visible, 128), F32)),
        [],
        80_000_000,
        62,
        tokens,
        placement,
        in_weight,
    )
    arrived = lax.all_to_all(packed, TM_FREQ, split_axis=0, concat_axis=0, tiled=True)
    flags = jnp.broadcast_to((patch_mask == 1)[:, :, None], (*patch_mask.shape, 128))
    aim = jnp.concatenate([targets, flags.astype(BF16)], axis=2).reshape(-1, PIX + 128)

    other = send(aim, "freq", 1, True)
    aim = call(order_kernel, shape((CELLS, PIX + 128)), [], 200_000_000, 8, aim, other)
    weights = [conv_weight[layer : layer + 1] for layer in range(2)]

    own, down, up, chosen = call(
        place_kernel,
        (
            shape((CELLS, CHANNELS)),
            shape((48, CHANNELS)),
            shape((48, CHANNELS)),
            shape((shards * 8, CELLS)),
        ),
        [],
        300_000_000,
        8,
        arrived,
        aim,
        mask_token[None, :],
    )
    columns = [pltpu.VMEM((464, DEPTH), BF16), pltpu.VMEM((464, DEPTH), BF16)]
    above = send(down, TM, 1, False)
    below = send(up, TM, -1, False)
    inside = call(
        inside_kernel,
        (shape((384, CHANNELS)), shape((384, CHANNELS), F32), shape((384, 128), F32)),
        columns,
        1_200_000_000,
        12,
        own,
        weights[0],
    )
    active, unit, scale, inner = call(
        first_kernel,
        (
            shape((448, CHANNELS)),
            shape((416, CHANNELS), F32),
            shape((416, 128), F32),
            shape((416, CHANNELS)),
        ),
        columns,
        1_500_000_000,
        12,
        above,
        own,
        below,
        weights[0],
        *inside,
    )
    inners = [inner] + [send(inner, "tm_0", step, True) for step in (1, 2, 3)]
    pred, *outers, mid, grad = call(
        second_kernel,
        (
            shape((CELLS, PIX)),
            *[shape((CELLS, 128))] * 4,
            shape((CELLS, CHANNELS), F32),
            shape((416, CHANNELS)),
        ),
        columns,
        3_500_000_000,
        18,
        active,
        unit,
        scale,
        weights[1],
        head_weight,
        above,
        aim,
        below,
    )
    outers[1:] = [send(outers[step], "tm_0", step, True) for step in (1, 2, 3)]
    picked = call(
        tail_kernel,
        shape((shards * 8, CHANNELS), F32),
        [],
        1_200_000_000,
        12,
        grad,
        mid,
        weights[0],
        chosen,
    )
    turned = call(turn_kernel, shape((4, CHANNELS, 416)), [], 400_000_000, 8, *inners)
    terms = call(
        weight_kernel,
        shape((shards, 16, CHANNELS)),
        [pltpu.VMEM((4, 416, 9 * 128), BF16), pltpu.VMEM((9 * CHANNELS + 8, 128), F32)],
        1_500_000_000,
        16,
        turned,
        *outers,
        picked,
    )
    terms = lax.all_to_all(terms, TM_FREQ, split_axis=0, concat_axis=0, tiled=True)
    token_grad, conv_grad = call(
        finish_kernel,
        (shape((visible, in_weight.shape[0]), F32), shape((54, 2, CHANNELS), F32)),
        [],
        80_000_000,
        6,
        terms,
        where_to,
        in_weight,
    )
    conv_grad = conv_grad.transpose(1, 0, 2)
    pred = lax.dynamic_slice_in_dim(pred.reshape(ROWS, COLS, PIX), core * half, half, axis=1)
    return (pred, token_grad, conv_grad)


def solution(mesh):
    split = Mesh(
        mesh.devices.reshape(4, 8, mesh.shape["freq"], mesh.shape["rec"]),
        ("tm_0", "tm_1", "freq", "rec"),
    )
    placed = (
        P(REC_TM_FREQ, None),
        P(None, REC_TM_FREQ),
        P(REC_TM, "freq"),
        P(REC_TM, "freq", None),
        P(),
        P(),
        P(),
        P(),
    )
    return jax.shard_map(
        per_device,
        mesh=split,
        in_specs=placed,
        out_specs=(P(REC_TM, "freq", None), P(REC_TM_FREQ, None), P("rec", TM_FREQ, None)),
        check_vma=False,
    )
```

```python
import jax
import jax.numpy as jnp
from jax import lax
from jax.experimental import pallas as pl
from jax.experimental.pallas import tpu as pltpu
from jax.sharding import Mesh
from jax.sharding import PartitionSpec as P


TM = ("tm_0", "tm_1")
TM_FREQ = ("tm_0", "tm_1", "freq")
REC_TM_FREQ = ("rec", "tm_0", "tm_1", "freq")
REC_TM = ("rec", "tm_0", "tm_1")

F32 = jnp.float32
BF16 = jnp.bfloat16
ROWS = 50
COLS = 8
CELLS = ROWS * COLS
CHANNELS = 384
DEPTH = 3 * CHANNELS
PIX = 256
ERF_SCALE = 0.7071067811865476
PDF_SCALE = 0.3989422804014327
ERF_TOP = (
    0.00022905065861350646,
    0.0034082910107109506,
    0.050955695062380861,
    0.18520832239976145,
    1.128379143519084,
)
ERF_BOTTOM = (
    -1.1791602954361697e-7,
    0.000023547966471313185,
    0.0010179625278914885,
    0.014070470171167667,
    0.11098505178285362,
    0.49746925110067538,
    1.0,
)


def horner(value, factors):
    total = jnp.full_like(value, factors[0])
    for factor in factors[1:]:
        total = total * value + factor
    return total


def erf(value):
    bounded = jnp.clip(value, -3.7439211627767994, 3.7439211627767994)
    square = bounded * bounded
    return bounded * horner(square, ERF_TOP) / horner(square, ERF_BOTTOM)


def half_erf(unit):
    return 0.5 * (1.0 + erf(unit * ERF_SCALE))


def column_shifted(value):
    cells, channels = value.shape
    grid = value.reshape(cells // 8, 8, channels)
    column = lax.broadcasted_iota(jnp.int32, grid.shape, 1)
    lower = jnp.where(column == 0, 0.0, pltpu.roll(grid, 1, axis=1))
    upper = jnp.where(column == 7, 0.0, pltpu.roll(grid, 7, axis=1))
    return lower.reshape(value.shape), value, upper.reshape(value.shape)


def store_columns(value, even, odd):
    cells, channels = value.shape
    for part, shifted in enumerate(column_shifted(value)):
        lanes = slice(part * channels, (part + 1) * channels)
        even[0:cells, lanes] = shifted.astype(BF16)
        odd[0 : cells - 8, lanes] = shifted[8:].astype(BF16)


def conv_taps(windows, taps):
    summed = None
    for part, window in enumerate(windows):
        term = jnp.dot(
            window, taps[0, part * DEPTH : (part + 1) * DEPTH], preferred_element_type=F32
        )
        summed = term if summed is None else summed + term
    return summed


def conv_back(grad, taps, cells):
    summed = None
    for row_off in range(3):
        term = lax.dot_general(
            grad,
            taps[0, row_off * DEPTH : (row_off + 1) * DEPTH],
            (((1,), (1,)), ((), ())),
            preferred_element_type=F32,
        )
        term = term[8 * (2 - row_off) : 8 * (2 - row_off) + cells]
        summed = term if summed is None else summed + term
    grid = (cells // 8, 8, CHANNELS)
    column = lax.broadcasted_iota(jnp.int32, grid, 1)
    first = summed[:, 0:CHANNELS].reshape(grid)
    last = summed[:, 2 * CHANNELS :].reshape(grid)
    total = jnp.where(column == 7, 0.0, pltpu.roll(first, 7, axis=1))
    total += jnp.where(column == 0, 0.0, pltpu.roll(last, 1, axis=1))
    return summed[:, CHANNELS : 2 * CHANNELS] + total.reshape(cells, CHANNELS)


def quarters(value):
    tiles = [value[:, 128 * part : 128 * (part + 1)] for part in range(3)]
    lane = lax.broadcasted_iota(jnp.int32, tiles[0].shape, 1)
    one = jnp.where(lane < 32, pltpu.roll(tiles[0], 32, axis=1), pltpu.roll(tiles[1], 32, axis=1))
    two = jnp.where(lane < 64, pltpu.roll(tiles[1], 64, axis=1), pltpu.roll(tiles[2], 64, axis=1))
    return tiles[0], one, two, pltpu.roll(tiles[2], 96, axis=1)


def joined(parts):
    lane = lax.broadcasted_iota(jnp.int32, parts[0].shape, 1)
    one = pltpu.roll(parts[1], 96, axis=1)
    two = pltpu.roll(parts[2], 64, axis=1)
    three = pltpu.roll(parts[3], 32, axis=1)
    tiles = (
        jnp.where(lane < 96, parts[0], one),
        jnp.where(lane < 64, one, two),
        jnp.where(lane < 32, two, three),
    )
    return jnp.concatenate(tiles, axis=1)


def normed(conv_out):
    center = conv_out - jnp.mean(conv_out, axis=-1, keepdims=True)
    scale = lax.rsqrt(jnp.mean(center * center, axis=-1, keepdims=True) + 1e-05)
    return center * scale, scale


def pull_back(unit, scale, gradient):
    slope = half_erf(unit) + unit * (PDF_SCALE * jnp.exp(-0.5 * unit * unit))
    grad = gradient * slope
    mean = jnp.mean(grad, axis=-1, keepdims=True)
    along = jnp.mean(grad * unit, axis=-1, keepdims=True)
    return scale * (grad - mean - unit * along)


def rows_valid(row):
    row = row + lax.axis_index(TM) * ROWS
    return (row >= 0) & (row < lax.axis_size(TM) * ROWS)


def row_number(cells):
    return lax.shift_right_logical(lax.broadcasted_iota(jnp.int32, (cells, 1), 0), 3)


def pack_kernel(tokens, placement, in_weight, packed, where_out):
    count = tokens.shape[0]
    rows = placement[0:1, :].astype(F32)
    cols = placement[1:2, :].astype(F32)
    tile_row = jnp.floor((rows + 0.5) * (1.0 / ROWS))
    tile = tile_row * 2.0 + jnp.where(cols >= 4.0, 1.0, 0.0)
    down = lax.broadcasted_iota(jnp.int32, (count, count), 0)
    across = lax.broadcasted_iota(jnp.int32, (count, count), 1)

    def column(value):
        return jnp.sum(jnp.where(down == across, value, 0.0), axis=1, keepdims=True)

    earlier = jnp.where((column(tile) == tile) & (down < across), 1.0, 0.0)
    where_to = tile * 2.0 + jnp.sum(earlier, axis=0, keepdims=True)
    where_out[...] = jnp.broadcast_to(column(where_to), where_out.shape)
    index = lax.broadcasted_iota(jnp.int32, (packed.shape[0], 1), 0)
    wanted = lax.shift_right_logical(index, 4) * 4 + (index & 3)
    match = jnp.where(wanted.astype(F32) == where_to, 1.0, 0.0).astype(BF16)
    proj = jnp.dot(tokens[...], in_weight[...], preferred_element_type=F32).astype(BF16)
    lane = lax.broadcasted_iota(jnp.int32, (count, 128), 1)
    notes = jnp.where(lane == 1, column(cols), jnp.where(lane == 2, 1.0, 0.0))
    notes = jnp.where(lane == 0, column(rows - tile_row * ROWS), notes).astype(BF16)
    low = jnp.dot(match, proj[:, 0:256], preferred_element_type=F32)
    rest = jnp.concatenate([proj[:, 256:384], notes], axis=1)
    high = jnp.dot(match, rest, preferred_element_type=F32)
    packed[...] = jnp.where((index & 4) == 0, low, high).astype(BF16)


def order_kernel(own_aim, other_aim, aim_out):
    core = lax.axis_index("freq")
    number = lax.broadcasted_iota(jnp.int32, (CELLS, 1), 0)
    far = (lax.shift_right_logical(number, 2) & 1) != core
    source = lax.shift_right_logical(number, 3) * 4 + (number & 3) + jnp.where(far, CELLS // 2, 0)
    order = lax.broadcasted_iota(jnp.int32, (CELLS, CELLS), 1) == source
    aim_out[...] = jnp.dot(
        jnp.where(order, 1.0, 0.0).astype(BF16),
        jnp.concatenate([own_aim[...].astype(F32), other_aim[...].astype(F32)], axis=0).astype(BF16),
        preferred_element_type=F32,
    ).astype(BF16)


def place_kernel(arrived, aim, token, x_out, down_out, up_out, chosen_out):
    core = lax.axis_index("freq")
    slots = arrived.shape[0]
    notes = arrived[:, 128:256].astype(F32).reshape(slots // 8, 8, 128)
    within = lax.broadcasted_iota(jnp.int32, notes.shape, 1)
    notes = jnp.where(within >= 4, notes, pltpu.roll(notes, 4, axis=1)).reshape(slots, 128)
    cell = jnp.where(notes[:, 2:3] == 1.0, notes[:, 0:1] * 8.0 + notes[:, 1:2], -1.0)
    lane = lax.broadcasted_iota(jnp.int32, (slots, CELLS), 1)
    index = lax.broadcasted_iota(jnp.int32, (slots, CELLS), 0)
    hit = lane == cell.astype(jnp.int32)

    def pick(flag):
        return lax.dot_general(
            jnp.where(hit & flag, 1.0, 0.0).astype(BF16),
            arrived[...],
            (((0,), (0,)), ((), ())),
            preferred_element_type=F32,
        )

    placed = jnp.concatenate([pick((index & 4) == 0), pick((index & 4) == 4)[:, 0:128]], axis=1)
    masked = aim[:, PIX : PIX + 1] == 1.0
    x = jnp.where(masked, token[...].astype(F32), placed).astype(BF16)
    x_out[...] = x
    down_out[0:32] = x[CELLS - 32 :]
    down_out[32:48] = aim[CELLS - 16 :]
    up_out[0:32] = x[0:32]
    up_out[32:48] = aim[0:16]
    spread = jnp.broadcast_to(cell, (slots, 128)).reshape(slots // 8, 8, 128)
    first = jnp.sum(jnp.where(within == 4 + 2 * core, spread, 0.0), axis=1, keepdims=True)
    second = jnp.sum(jnp.where(within == 5 + 2 * core, spread, 0.0), axis=1, keepdims=True)
    spread = jnp.where(within == 6, first, jnp.where(within == 7, second, -1.0))
    spread = spread.reshape(slots, 128)
    chosen_out[...] = jnp.where(lane == spread[:, 0:1].astype(jnp.int32), 1.0, 0.0).astype(BF16)


def inside_kernel(own, weight, active_out, unit_out, scale_out, share_out, even, odd):
    source = own[...].astype(F32)
    store_columns(source, even, odd)
    unit, scale = normed(conv_taps((even[0:384], odd[0:384], even[16:400]), weight))
    unit_out[...] = unit
    scale_out[...] = jnp.broadcast_to(scale, scale_out.shape)
    active = source[8:392] + unit * half_erf(unit)
    active_out[...] = active.astype(BF16)
    share_out[...] = jnp.where(lax.axis_index("freq") == 1, active, source[8:392]).astype(BF16)


def first_kernel(
    above, own, below, weight, active_in, unit_in, scale_in,
    active_out, unit_out, scale_out, share_out, even, odd,
):
    upper, lower = above[0:32].astype(F32), below[0:32].astype(F32)
    border = jnp.concatenate(
        [upper, own[0:16].astype(F32), own[384:400].astype(F32), lower], axis=0
    )
    store_columns(border, even, odd)
    windows = (
        jnp.concatenate([even[0:32], even[48:80]], axis=0),
        jnp.concatenate([odd[0:32], odd[48:80]], axis=0),
        jnp.concatenate([even[16:48], even[64:96]], axis=0),
    )
    unit, scale = normed(conv_taps(windows, weight))
    edge = jnp.concatenate([border[8:40], border[56:88]], axis=0) + unit * half_erf(unit)
    number = row_number(64)
    number = jnp.where(number < 4, number - 3, number + 45)
    edge = jnp.where(rows_valid(number), edge, 0.0)
    active_out[0:32] = edge[0:32].astype(BF16)
    active_out[32:416] = active_in[...]
    active_out[416:448] = edge[32:64].astype(BF16)
    unit_out[0:16] = unit[16:32]
    unit_out[16:400] = unit_in[...]
    unit_out[400:416] = unit[32:48]
    scale = jnp.broadcast_to(scale, (64, 128))
    scale_out[0:16] = scale[16:32]
    scale_out[16:400] = scale_in[...]
    scale_out[400:416] = scale[32:48]
    source = jnp.concatenate(
        [upper[24:32], own[0:8].astype(F32), own[392:400].astype(F32), lower[0:8]], axis=0
    )
    share_out[...] = jnp.where(lax.axis_index("freq") == 1, edge[16:48], source).astype(BF16)


def second_kernel(
    active_ref, unit_ref, scale_ref, border, weight, head, above, aim_ref, below,
    pred, share_own, share_one, share_two, share_three, mid_out, grad_out, even, odd,
):
    active = active_ref[...].astype(F32)
    store_columns(active, even, odd)
    unit, scale = normed(conv_taps((even[0:432], odd[0:432], even[16:448]), weight))
    top = (active[8:440] + unit * half_erf(unit)).astype(BF16)
    guess = jnp.dot(top, head[...], preferred_element_type=F32)
    pred[...] = guess[16:416].astype(BF16)
    aim = jnp.concatenate([above[32:48], aim_ref[...], below[32:48]], axis=0)
    misfit = jnp.where(
        aim[:, PIX : PIX + 1] == 1.0, (guess - aim[:, 0:PIX].astype(F32)) * 0.0625, 0.0
    ).astype(BF16)
    grad_top = lax.dot_general(
        misfit, head[...], (((1,), (1,)), ((), ())), preferred_element_type=F32
    )
    grad_two = pull_back(unit, scale, grad_top).astype(BF16)
    grad_mid = grad_top[8:424] + conv_back(grad_two, weight, 416)
    grad_one = pull_back(unit_ref[...], scale_ref[:, 0:1], grad_mid)
    grad_one = jnp.where(rows_valid(row_number(416) - 1), grad_one, 0.0)
    grad_out[...] = grad_one.astype(BF16)
    mid_out[...] = grad_mid[8:408]
    share = jnp.where(lax.axis_index("freq") == 1, grad_two.astype(F32)[16:416], grad_one[8:408])
    pieces = quarters(share)
    lane = lax.broadcasted_iota(jnp.int32, (CELLS, 128), 1)
    for step, share_out in enumerate((share_own, share_one, share_two, share_three)):
        quarter = (lax.axis_index("tm_0") + step) & 3
        piece = jnp.where(quarter == 0, pieces[0], pieces[1])
        piece = jnp.where(quarter >= 2, jnp.where(quarter == 2, pieces[2], pieces[3]), piece)
        share_out[0:CELLS] = jnp.where(lane < 96, piece, 0.0).astype(BF16)
        for part in range(3):
            share_out[CELLS + 32 * part : CELLS + 32 * (part + 1)] = border[
                :, 128 * part : 128 * (part + 1)
            ]


def tail_kernel(grad_ref, mid_ref, weight, chosen, out):
    grad_cells = mid_ref[...] + conv_back(grad_ref[...], weight, CELLS)
    out[...] = jnp.dot(chosen[...], grad_cells.astype(BF16), preferred_element_type=F32)


def turn_kernel(*refs):
    for part in range(4):
        refs[4][part] = refs[part][...].astype(F32).T.astype(BF16)


def weight_kernel(turned, *refs):
    outers, picked = refs[0:4], refs[4]
    out, moved, total = refs[5:]
    summed = None
    for part in range(4):
        low, middle, high = column_shifted(outers[part][0:CELLS].astype(F32))
        for row_off in range(3):
            for col_off, piece in enumerate((high, middle, low)):
                rows = [piece]
                if row_off:
                    rows.insert(0, jnp.zeros((8 * row_off, 128), F32))
                if row_off < 2:
                    rows.append(jnp.zeros((16 - 8 * row_off, 128), F32))
                rows = jnp.concatenate(rows, axis=0).astype(BF16)
                tap = 3 * row_off + col_off
                lanes = slice(tap * 128, (tap + 1) * 128)
                moved[part, 0:384, lanes] = rows[16:400]
                moved[part, 384:400, lanes] = rows[0:16]
                moved[part, 400:416, lanes] = rows[400:416]
        border = jnp.concatenate(
            [outers[part][CELLS + 32 * k : CELLS + 32 * (k + 1)] for k in range(3)], axis=1
        )
        inner = jnp.concatenate([turned[part], border.astype(F32).T.astype(BF16)], axis=1)
        term = jnp.dot(inner, moved[part], preferred_element_type=F32)
        summed = term if summed is None else summed + term
    for tap in range(9):
        total[tap * CHANNELS : (tap + 1) * CHANNELS] = summed[:, tap * 128 : (tap + 1) * 128]
    total[9 * CHANNELS :] = jnp.zeros((8, 128), F32)
    row = lax.broadcasted_iota(jnp.int32, (16, CHANNELS), 0)
    for shard in range(64):
        start = 54 * shard
        packed = joined([total[start + 14 * part : start + 14 * part + 16] for part in range(4)])
        back = picked[8 * shard : 8 * shard + 8]
        packed = jnp.where(row >= 14, jnp.concatenate([back, back], axis=0), packed)
        out[shard] = packed.astype(BF16)


def finish_kernel(arrived, where_ref, in_weight, token_out, conv_out):
    count = where_ref.shape[0]
    rows = arrived.shape[0] * 16
    index = lax.broadcasted_iota(jnp.int32, (count, rows), 1)
    within = index & 15
    slot = lax.shift_right_logical(index, 4) * 2 + within - 14
    hit = (where_ref[:, 0:1].astype(jnp.int32) == slot) & (within >= 14)
    grad_proj = jnp.dot(
        jnp.where(hit, 1.0, 0.0).astype(BF16),
        arrived[...].reshape(rows, CHANNELS),
        preferred_element_type=F32,
    ).astype(BF16)
    token_out[...] = lax.dot_general(
        grad_proj, in_weight[...], (((1,), (1,)), ((), ())), preferred_element_type=F32
    )
    for layer in range(2):
        parts = []
        for peer in range(4):
            summed = None
            for near in range(8):
                term = arrived[16 * peer + 2 * near + layer].astype(F32)
                summed = term if summed is None else summed + term
            parts.append(quarters(summed))
        for group in range(4):
            height = min(14, 54 - 14 * group)
            wide = joined([parts[peer][group] for peer in range(4)])
            conv_out[14 * group : 14 * group + height, layer] = wide[0:height]


VMEM = pl.BlockSpec(memory_space=pltpu.VMEM)


def call(kernel, shapes, scratch, cost, limit, *operands):
    return pl.pallas_call(
        kernel,
        out_shape=shapes,
        in_specs=[VMEM] * len(operands),
        out_specs=jax.tree.map(lambda _: VMEM, shapes),
        scratch_shapes=scratch,
        compiler_params=pltpu.CompilerParams(vmem_limit_bytes=limit << 20),
        cost_estimate=pl.CostEstimate(
            flops=cost, bytes_accessed=cost // 400, transcendentals=0
        ),
    )(*operands)


def shape(dims, dtype=BF16):
    return jax.ShapeDtypeStruct(dims, dtype)


def send(value, axis, step, wrap):
    count = lax.axis_size(axis)
    pairs = [(i, (i + step) % count) for i in range(count)]
    if not wrap:
        pairs = [(i, i + step) for i in range(count) if 0 <= i + step < count]
    return lax.ppermute(value, axis, pairs)


def per_device(
    tokens, placement, patch_mask, targets, in_weight, mask_token, conv_weight, head_weight
):
    shards = lax.axis_size(TM_FREQ)
    core = lax.axis_index("freq")
    visible = tokens.shape[0]
    half = patch_mask.shape[1]

    packed, where_to = call(
        pack_kernel,
        (shape((shards * 8, 256)), shape((visible, 128), F32)),
        [],
        80_000_000,
        62,
        tokens,
        placement,
        in_weight,
    )
    arrived = lax.all_to_all(packed, TM_FREQ, split_axis=0, concat_axis=0, tiled=True)
    flags = jnp.broadcast_to((patch_mask == 1)[:, :, None], (*patch_mask.shape, 128))
    aim = jnp.concatenate([targets, flags.astype(BF16)], axis=2).reshape(-1, PIX + 128)

    other = send(aim, "freq", 1, True)
    aim = call(order_kernel, shape((CELLS, PIX + 128)), [], 200_000_000, 8, aim, other)
    weights = [conv_weight[layer : layer + 1] for layer in range(2)]

    own, down, up, chosen = call(
        place_kernel,
        (
            shape((CELLS, CHANNELS)),
            shape((48, CHANNELS)),
            shape((48, CHANNELS)),
            shape((shards * 8, CELLS)),
        ),
        [],
        300_000_000,
        8,
        arrived,
        aim,
        mask_token[None, :],
    )
    columns = [pltpu.VMEM((464, DEPTH), BF16), pltpu.VMEM((464, DEPTH), BF16)]
    columns = [pltpu.VMEM((464, DEPTH), BF16), pltpu.VMEM((464, DEPTH), BF16)]
    above = send(down, TM, 1, False)
    below = send(up, TM, -1, False)
    *inside, inner = call(
        inside_kernel,
        (
            shape((384, CHANNELS)),
            shape((384, CHANNELS), F32),
            shape((384, 128), F32),
            shape((384, CHANNELS)),
        ),
        columns,
        1_200_000_000,
        12,
        own,
        weights[0],
    )
    inners = [inner] + [send(inner, "tm_0", step, True) for step in (1, 2, 3)]
    active, unit, scale, border = call(
        first_kernel,
        (
            shape((448, CHANNELS)),
            shape((416, CHANNELS), F32),
            shape((416, 128), F32),
            shape((32, CHANNELS)),
        ),
        columns,
        500_000_000,
        12,
        above,
        own,
        below,
        weights[0],
        *inside,
    )
    pred, *outers, mid, grad = call(
        second_kernel,
        (
            shape((CELLS, PIX)),
            *[shape((CELLS + 96, 128))] * 4,
            shape((CELLS, CHANNELS), F32),
            shape((416, CHANNELS)),
        ),
        columns,
        3_500_000_000,
        18,
        active,
        unit,
        scale,
        border,
        weights[1],
        head_weight,
        above,
        aim,
        below,
    )
    outers[1:] = [send(outers[step], "tm_0", step, True) for step in (1, 2, 3)]
    picked = call(
        tail_kernel,
        shape((shards * 8, CHANNELS), F32),
        [],
        1_200_000_000,
        12,
        grad,
        mid,
        weights[0],
        chosen,
    )
    turned = call(turn_kernel, shape((4, CHANNELS, 384)), [], 400_000_000, 8, *inners)
    terms = call(
        weight_kernel,
        shape((shards, 16, CHANNELS)),
        [pltpu.VMEM((4, 416, 9 * 128), BF16), pltpu.VMEM((9 * CHANNELS + 8, 128), F32)],
        1_500_000_000,
        16,
        turned,
        *outers,
        picked,
    )
    terms = lax.all_to_all(terms, TM_FREQ, split_axis=0, concat_axis=0, tiled=True)
    token_grad, conv_grad = call(
        finish_kernel,
        (shape((visible, in_weight.shape[0]), F32), shape((54, 2, CHANNELS), F32)),
        [],
        80_000_000,
        6,
        terms,
        where_to,
        in_weight,
    )
    conv_grad = conv_grad.transpose(1, 0, 2)
    pred = lax.dynamic_slice_in_dim(pred.reshape(ROWS, COLS, PIX), core * half, half, axis=1)
    return (pred, token_grad, conv_grad)


def solution(mesh):
    split = Mesh(
        mesh.devices.reshape(4, 8, mesh.shape["freq"], mesh.shape["rec"]),
        ("tm_0", "tm_1", "freq", "rec"),
    )
    placed = (
        P(REC_TM_FREQ, None),
        P(None, REC_TM_FREQ),
        P(REC_TM, "freq"),
        P(REC_TM, "freq", None),
        P(),
        P(),
        P(),
        P(),
    )
    return jax.shard_map(
        per_device,
        mesh=split,
        in_specs=placed,
        out_specs=(P(REC_TM, "freq", None), P(REC_TM_FREQ, None), P("rec", TM_FREQ, None)),
        check_vma=False,
    )
```

```python
import jax
import jax.numpy as jnp
from jax import lax
from jax.experimental import pallas as pl
from jax.experimental.pallas import tpu as pltpu
from jax.sharding import Mesh
from jax.sharding import PartitionSpec as P


TM = ("tm_0", "tm_1")
TM_FREQ = ("tm_0", "tm_1", "freq")
REC_TM_FREQ = ("rec", "tm_0", "tm_1", "freq")
REC_TM = ("rec", "tm_0", "tm_1")

F32 = jnp.float32
BF16 = jnp.bfloat16
ROWS = 50
COLS = 8
CELLS = ROWS * COLS
CHANNELS = 384
DEPTH = 3 * CHANNELS
PIX = 256
ERF_SCALE = 0.7071067811865476
PDF_SCALE = 0.3989422804014327
ERF_TOP = (
    0.00022905065861350646,
    0.0034082910107109506,
    0.050955695062380861,
    0.18520832239976145,
    1.128379143519084,
)
ERF_BOTTOM = (
    -1.1791602954361697e-7,
    0.000023547966471313185,
    0.0010179625278914885,
    0.014070470171167667,
    0.11098505178285362,
    0.49746925110067538,
    1.0,
)


def horner(value, factors):
    total = jnp.full_like(value, factors[0])
    for factor in factors[1:]:
        total = total * value + factor
    return total


def erf(value):
    bounded = jnp.clip(value, -3.7439211627767994, 3.7439211627767994)
    square = bounded * bounded
    return bounded * horner(square, ERF_TOP) / horner(square, ERF_BOTTOM)


def half_erf(unit):
    return 0.5 * (1.0 + erf(unit * ERF_SCALE))


def column_shifted(value):
    cells, channels = value.shape
    grid = value.reshape(cells // 8, 8, channels)
    column = lax.broadcasted_iota(jnp.int32, grid.shape, 1)
    lower = jnp.where(column == 0, 0.0, pltpu.roll(grid, 1, axis=1))
    upper = jnp.where(column == 7, 0.0, pltpu.roll(grid, 7, axis=1))
    return lower.reshape(value.shape), value, upper.reshape(value.shape)


def store_columns(value, even, odd):
    cells, channels = value.shape
    for part, shifted in enumerate(column_shifted(value)):
        lanes = slice(part * channels, (part + 1) * channels)
        even[0:cells, lanes] = shifted.astype(BF16)
        odd[0 : cells - 8, lanes] = shifted[8:].astype(BF16)


def conv_taps(windows, taps):
    summed = None
    for part, window in enumerate(windows):
        term = jnp.dot(
            window, taps[0, part * DEPTH : (part + 1) * DEPTH], preferred_element_type=F32
        )
        summed = term if summed is None else summed + term
    return summed


def conv_back(grad, taps, cells):
    summed = None
    for row_off in range(3):
        term = lax.dot_general(
            grad,
            taps[0, row_off * DEPTH : (row_off + 1) * DEPTH],
            (((1,), (1,)), ((), ())),
            preferred_element_type=F32,
        )
        term = term[8 * (2 - row_off) : 8 * (2 - row_off) + cells]
        summed = term if summed is None else summed + term
    grid = (cells // 8, 8, CHANNELS)
    column = lax.broadcasted_iota(jnp.int32, grid, 1)
    first = summed[:, 0:CHANNELS].reshape(grid)
    last = summed[:, 2 * CHANNELS :].reshape(grid)
    total = jnp.where(column == 7, 0.0, pltpu.roll(first, 7, axis=1))
    total += jnp.where(column == 0, 0.0, pltpu.roll(last, 1, axis=1))
    return summed[:, CHANNELS : 2 * CHANNELS] + total.reshape(cells, CHANNELS)


def quarters(value):
    tiles = [value[:, 128 * part : 128 * (part + 1)] for part in range(3)]
    lane = lax.broadcasted_iota(jnp.int32, tiles[0].shape, 1)
    one = jnp.where(lane < 32, pltpu.roll(tiles[0], 32, axis=1), pltpu.roll(tiles[1], 32, axis=1))
    two = jnp.where(lane < 64, pltpu.roll(tiles[1], 64, axis=1), pltpu.roll(tiles[2], 64, axis=1))
    return tiles[0], one, two, pltpu.roll(tiles[2], 96, axis=1)


def joined(parts):
    lane = lax.broadcasted_iota(jnp.int32, parts[0].shape, 1)
    one = pltpu.roll(parts[1], 96, axis=1)
    two = pltpu.roll(parts[2], 64, axis=1)
    three = pltpu.roll(parts[3], 32, axis=1)
    tiles = (
        jnp.where(lane < 96, parts[0], one),
        jnp.where(lane < 64, one, two),
        jnp.where(lane < 32, two, three),
    )
    return jnp.concatenate(tiles, axis=1)


def normed(conv_out):
    center = conv_out - jnp.mean(conv_out, axis=-1, keepdims=True)
    scale = lax.rsqrt(jnp.mean(center * center, axis=-1, keepdims=True) + 1e-05)
    return center * scale, scale


def pull_back(unit, scale, gradient):
    slope = half_erf(unit) + unit * (PDF_SCALE * jnp.exp(-0.5 * unit * unit))
    grad = gradient * slope
    mean = jnp.mean(grad, axis=-1, keepdims=True)
    along = jnp.mean(grad * unit, axis=-1, keepdims=True)
    return scale * (grad - mean - unit * along)


def rows_valid(row):
    row = row + lax.axis_index(TM) * ROWS
    return (row >= 0) & (row < lax.axis_size(TM) * ROWS)


def row_number(cells):
    return lax.shift_right_logical(lax.broadcasted_iota(jnp.int32, (cells, 1), 0), 3)


def pack_kernel(tokens, placement, in_weight, packed, where_out):
    count = tokens.shape[0]
    rows = placement[0:1, :].astype(F32)
    cols = placement[1:2, :].astype(F32)
    tile_row = jnp.floor((rows + 0.5) * (1.0 / ROWS))
    tile = tile_row * 2.0 + jnp.where(cols >= 4.0, 1.0, 0.0)
    down = lax.broadcasted_iota(jnp.int32, (count, count), 0)
    across = lax.broadcasted_iota(jnp.int32, (count, count), 1)

    def column(value):
        return jnp.sum(jnp.where(down == across, value, 0.0), axis=1, keepdims=True)

    earlier = jnp.where((column(tile) == tile) & (down < across), 1.0, 0.0)
    where_to = tile * 2.0 + jnp.sum(earlier, axis=0, keepdims=True)
    where_out[...] = jnp.broadcast_to(column(where_to), where_out.shape)
    index = lax.broadcasted_iota(jnp.int32, (packed.shape[0], 1), 0)
    wanted = lax.shift_right_logical(index, 4) * 4 + (index & 3)
    match = jnp.where(wanted.astype(F32) == where_to, 1.0, 0.0).astype(BF16)
    proj = jnp.dot(tokens[...], in_weight[...], preferred_element_type=F32).astype(BF16)
    lane = lax.broadcasted_iota(jnp.int32, (count, 128), 1)
    notes = jnp.where(lane == 1, column(cols), jnp.where(lane == 2, 1.0, 0.0))
    notes = jnp.where(lane == 0, column(rows - tile_row * ROWS), notes).astype(BF16)
    low = jnp.dot(match, proj[:, 0:256], preferred_element_type=F32)
    rest = jnp.concatenate([proj[:, 256:384], notes], axis=1)
    high = jnp.dot(match, rest, preferred_element_type=F32)
    packed[...] = jnp.where((index & 4) == 0, low, high).astype(BF16)


def order_kernel(own_aim, other_aim, aim_out):
    core = lax.axis_index("freq")
    number = lax.broadcasted_iota(jnp.int32, (CELLS, 1), 0)
    far = (lax.shift_right_logical(number, 2) & 1) != core
    source = lax.shift_right_logical(number, 3) * 4 + (number & 3) + jnp.where(far, CELLS // 2, 0)
    order = lax.broadcasted_iota(jnp.int32, (CELLS, CELLS), 1) == source
    aim_out[...] = jnp.dot(
        jnp.where(order, 1.0, 0.0).astype(BF16),
        jnp.concatenate([own_aim[...].astype(F32), other_aim[...].astype(F32)], axis=0).astype(BF16),
        preferred_element_type=F32,
    ).astype(BF16)


def place_kernel(arrived, aim, token, x_out, down_out, up_out, chosen_out):
    core = lax.axis_index("freq")
    slots = arrived.shape[0]
    notes = arrived[:, 128:256].astype(F32).reshape(slots // 8, 8, 128)
    within = lax.broadcasted_iota(jnp.int32, notes.shape, 1)
    notes = jnp.where(within >= 4, notes, pltpu.roll(notes, 4, axis=1)).reshape(slots, 128)
    cell = jnp.where(notes[:, 2:3] == 1.0, notes[:, 0:1] * 8.0 + notes[:, 1:2], -1.0)
    lane = lax.broadcasted_iota(jnp.int32, (slots, CELLS), 1)
    index = lax.broadcasted_iota(jnp.int32, (slots, CELLS), 0)
    hit = lane == cell.astype(jnp.int32)

    def pick(flag):
        return lax.dot_general(
            jnp.where(hit & flag, 1.0, 0.0).astype(BF16),
            arrived[...],
            (((0,), (0,)), ((), ())),
            preferred_element_type=F32,
        )

    placed = jnp.concatenate([pick((index & 4) == 0), pick((index & 4) == 4)[:, 0:128]], axis=1)
    masked = aim[:, PIX : PIX + 1] == 1.0
    x = jnp.where(masked, token[...].astype(F32), placed).astype(BF16)
    x_out[...] = x
    down_out[0:32] = x[CELLS - 32 :]
    down_out[32:48] = aim[CELLS - 16 :]
    up_out[0:32] = x[0:32]
    up_out[32:48] = aim[0:16]
    spread = jnp.broadcast_to(cell, (slots, 128)).reshape(slots // 8, 8, 128)
    first = jnp.sum(jnp.where(within == 4 + 2 * core, spread, 0.0), axis=1, keepdims=True)
    second = jnp.sum(jnp.where(within == 5 + 2 * core, spread, 0.0), axis=1, keepdims=True)
    spread = jnp.where(within == 6, first, jnp.where(within == 7, second, -1.0))
    spread = spread.reshape(slots, 128)
    chosen_out[...] = jnp.where(lane == spread[:, 0:1].astype(jnp.int32), 1.0, 0.0).astype(BF16)


def inside_kernel(own, weight, active_out, unit_out, scale_out, share_out, even, odd):
    source = own[...].astype(F32)
    store_columns(source, even, odd)
    unit, scale = normed(conv_taps((even[0:384], odd[0:384], even[16:400]), weight))
    unit_out[...] = unit
    scale_out[...] = jnp.broadcast_to(scale, scale_out.shape)
    active = source[8:392] + unit * half_erf(unit)
    active_out[...] = active.astype(BF16)
    share_out[...] = jnp.where(lax.axis_index("freq") == 1, active, source[8:392]).astype(BF16)


def border_rows(
    above, own, below, weight, active_in, unit_in, scale_in,
    active_out, unit_out, scale_out, share_out, even, odd,
):
    upper, lower = above[0:32].astype(F32), below[0:32].astype(F32)
    border = jnp.concatenate(
        [upper, own[0:16].astype(F32), own[384:400].astype(F32), lower], axis=0
    )
    store_columns(border, even, odd)
    windows = (
        jnp.concatenate([even[0:32], even[48:80]], axis=0),
        jnp.concatenate([odd[0:32], odd[48:80]], axis=0),
        jnp.concatenate([even[16:48], even[64:96]], axis=0),
    )
    unit, scale = normed(conv_taps(windows, weight))
    edge = jnp.concatenate([border[8:40], border[56:88]], axis=0) + unit * half_erf(unit)
    number = row_number(64)
    number = jnp.where(number < 4, number - 3, number + 45)
    edge = jnp.where(rows_valid(number), edge, 0.0)
    active_out[0:32] = edge[0:32].astype(BF16)
    active_out[32:416] = active_in[...]
    active_out[416:448] = edge[32:64].astype(BF16)
    unit_out[0:16] = unit[16:32]
    unit_out[16:400] = unit_in[...]
    unit_out[400:416] = unit[32:48]
    scale = jnp.broadcast_to(scale, (64, 128))
    scale_out[0:16] = scale[16:32]
    scale_out[16:400] = scale_in[...]
    scale_out[400:416] = scale[32:48]
    source = jnp.concatenate(
        [upper[24:32], own[0:8].astype(F32), own[392:400].astype(F32), lower[0:8]], axis=0
    )
    share_out[...] = jnp.where(lax.axis_index("freq") == 1, edge[16:48], source).astype(BF16)


def second_kernel(
    above, own, below, first_weight, active_in, unit_in, scale_in, weight, head, aim_ref,
    pred, share_own, share_one, share_two, share_three, mid_out, grad_out,
    even, odd, active_ref, unit_ref, scale_ref, border,
):
    border_rows(
        above, own, below, first_weight, active_in, unit_in, scale_in,
        active_ref, unit_ref, scale_ref, border, even, odd,
    )
    active = active_ref[...].astype(F32)
    store_columns(active, even, odd)
    unit, scale = normed(conv_taps((even[0:432], odd[0:432], even[16:448]), weight))
    top = (active[8:440] + unit * half_erf(unit)).astype(BF16)
    guess = jnp.dot(top, head[...], preferred_element_type=F32)
    pred[...] = guess[16:416].astype(BF16)
    aim = jnp.concatenate([above[32:48], aim_ref[...], below[32:48]], axis=0)
    misfit = jnp.where(
        aim[:, PIX : PIX + 1] == 1.0, (guess - aim[:, 0:PIX].astype(F32)) * 0.0625, 0.0
    ).astype(BF16)
    grad_top = lax.dot_general(
        misfit, head[...], (((1,), (1,)), ((), ())), preferred_element_type=F32
    )
    grad_two = pull_back(unit, scale, grad_top).astype(BF16)
    grad_mid = grad_top[8:424] + conv_back(grad_two, weight, 416)
    grad_one = pull_back(unit_ref[...], scale_ref[:, 0:1], grad_mid)
    grad_one = jnp.where(rows_valid(row_number(416) - 1), grad_one, 0.0)
    grad_out[...] = grad_one.astype(BF16)
    mid_out[...] = grad_mid[8:408]
    share = jnp.where(lax.axis_index("freq") == 1, grad_two.astype(F32)[16:416], grad_one[8:408])
    pieces = quarters(share)
    lane = lax.broadcasted_iota(jnp.int32, (CELLS, 128), 1)
    for step, share_out in enumerate((share_own, share_one, share_two, share_three)):
        quarter = (lax.axis_index("tm_0") + step) & 3
        piece = jnp.where(quarter == 0, pieces[0], pieces[1])
        piece = jnp.where(quarter >= 2, jnp.where(quarter == 2, pieces[2], pieces[3]), piece)
        rest = piece[304:400]
        side = [pltpu.roll(rest, 96 - 32 * part, axis=1) for part in range(3)]
        side = jnp.concatenate([*side, jnp.zeros((16, 128), F32)], axis=0)
        share_out[0:304] = jnp.where(lane[0:304] < 96, piece[0:304], side).astype(BF16)
        for part in range(3):
            share_out[304 + 32 * part : 304 + 32 * (part + 1)] = border[
                :, 128 * part : 128 * (part + 1)
            ]


def tail_kernel(grad_ref, mid_ref, weight, chosen, out):
    grad_cells = mid_ref[...] + conv_back(grad_ref[...], weight, CELLS)
    out[...] = jnp.dot(chosen[...], grad_cells.astype(BF16), preferred_element_type=F32)


def turn_kernel(*refs):
    for part in range(3):
        refs[3][part] = refs[part][...].astype(F32).T.astype(BF16)


def chip_term(turned, outer, moved):
    packed = outer[0:304].astype(F32)
    lane = lax.broadcasted_iota(jnp.int32, (96, 128), 1)
    rest = jnp.where(lane < 96, pltpu.roll(packed[192:288], 96, axis=1), 0.0)
    rest = jnp.where(lane < 64, pltpu.roll(packed[96:192], 64, axis=1), rest)
    rest = jnp.where(lane < 32, pltpu.roll(packed[0:96], 32, axis=1), rest)
    lane = lax.broadcasted_iota(jnp.int32, (304, 128), 1)
    gradient = jnp.concatenate([jnp.where(lane < 96, packed, 0.0), rest], axis=0)
    low, middle, high = column_shifted(gradient)
    for row_off in range(3):
        for col_off, piece in enumerate((high, middle, low)):
            rows = [piece]
            if row_off:
                rows.insert(0, jnp.zeros((8 * row_off, 128), F32))
            if row_off < 2:
                rows.append(jnp.zeros((16 - 8 * row_off, 128), F32))
            rows = jnp.concatenate(rows, axis=0).astype(BF16)
            tap = 3 * row_off + col_off
            lanes = slice(tap * 128, (tap + 1) * 128)
            moved[0:384, lanes] = rows[16:400]
            moved[384:400, lanes] = rows[0:16]
            moved[400:416, lanes] = rows[400:416]
    border = jnp.concatenate([outer[304 + 32 * k : 336 + 32 * k] for k in range(3)], axis=1)
    inner = jnp.concatenate([turned, border.astype(F32).T.astype(BF16)], axis=1)
    return jnp.dot(inner, moved[...], preferred_element_type=F32)


def own_kernel(inner, outer, out, moved):
    out[...] = chip_term(inner[...].astype(F32).T.astype(BF16), outer, moved)


def weight_kernel(summed_ref, turned, *refs):
    outers, picked = refs[0:3], refs[3]
    out, moved, total = refs[4:]
    summed = summed_ref[...]
    for part in range(3):
        summed = summed + chip_term(turned[part], outers[part], moved.at[part])
    for tap in range(9):
        total[tap * CHANNELS : (tap + 1) * CHANNELS] = summed[:, tap * 128 : (tap + 1) * 128]
    total[9 * CHANNELS :] = jnp.zeros((8, 128), F32)
    row = lax.broadcasted_iota(jnp.int32, (16, CHANNELS), 0)
    for shard in range(64):
        start = 54 * shard
        packed = joined([total[start + 14 * part : start + 14 * part + 16] for part in range(4)])
        back = picked[8 * shard : 8 * shard + 8]
        packed = jnp.where(row >= 14, jnp.concatenate([back, back], axis=0), packed)
        out[shard] = packed.astype(BF16)


def finish_kernel(arrived, where_ref, in_weight, token_out, conv_out):
    count = where_ref.shape[0]
    rows = arrived.shape[0] * 16
    index = lax.broadcasted_iota(jnp.int32, (count, rows), 1)
    within = index & 15
    slot = lax.shift_right_logical(index, 4) * 2 + within - 14
    hit = (where_ref[:, 0:1].astype(jnp.int32) == slot) & (within >= 14)
    grad_proj = jnp.dot(
        jnp.where(hit, 1.0, 0.0).astype(BF16),
        arrived[...].reshape(rows, CHANNELS),
        preferred_element_type=F32,
    ).astype(BF16)
    token_out[...] = lax.dot_general(
        grad_proj, in_weight[...], (((1,), (1,)), ((), ())), preferred_element_type=F32
    )
    for layer in range(2):
        parts = []
        for peer in range(4):
            summed = None
            for near in range(8):
                term = arrived[16 * peer + 2 * near + layer].astype(F32)
                summed = term if summed is None else summed + term
            parts.append(quarters(summed))
        for group in range(4):
            height = min(14, 54 - 14 * group)
            wide = joined([parts[peer][group] for peer in range(4)])
            conv_out[14 * group : 14 * group + height, layer] = wide[0:height]


VMEM = pl.BlockSpec(memory_space=pltpu.VMEM)


def call(kernel, shapes, scratch, cost, limit, *operands):
    return pl.pallas_call(
        kernel,
        out_shape=shapes,
        in_specs=[VMEM] * len(operands),
        out_specs=jax.tree.map(lambda _: VMEM, shapes),
        scratch_shapes=scratch,
        compiler_params=pltpu.CompilerParams(vmem_limit_bytes=limit << 20),
        cost_estimate=pl.CostEstimate(
            flops=cost, bytes_accessed=cost // 400, transcendentals=0
        ),
    )(*operands)


def shape(dims, dtype=BF16):
    return jax.ShapeDtypeStruct(dims, dtype)


def send(value, axis, step, wrap):
    count = lax.axis_size(axis)
    pairs = [(i, (i + step) % count) for i in range(count)]
    if not wrap:
        pairs = [(i, i + step) for i in range(count) if 0 <= i + step < count]
    return lax.ppermute(value, axis, pairs)


def per_device(
    tokens, placement, patch_mask, targets, in_weight, mask_token, conv_weight, head_weight
):
    shards = lax.axis_size(TM_FREQ)
    core = lax.axis_index("freq")
    visible = tokens.shape[0]
    half = patch_mask.shape[1]

    packed, where_to = call(
        pack_kernel,
        (shape((shards * 8, 256)), shape((visible, 128), F32)),
        [],
        80_000_000,
        62,
        tokens,
        placement,
        in_weight,
    )
    arrived = lax.all_to_all(packed, TM_FREQ, split_axis=0, concat_axis=0, tiled=True)
    flags = jnp.broadcast_to((patch_mask == 1)[:, :, None], (*patch_mask.shape, 128))
    aim = jnp.concatenate([targets, flags.astype(BF16)], axis=2).reshape(-1, PIX + 128)

    other = send(aim, "freq", 1, True)
    aim = call(order_kernel, shape((CELLS, PIX + 128)), [], 200_000_000, 8, aim, other)
    weights = [conv_weight[layer : layer + 1] for layer in range(2)]

    own, down, up, chosen = call(
        place_kernel,
        (
            shape((CELLS, CHANNELS)),
            shape((48, CHANNELS)),
            shape((48, CHANNELS)),
            shape((shards * 8, CELLS)),
        ),
        [],
        300_000_000,
        8,
        arrived,
        aim,
        mask_token[None, :],
    )
    columns = [pltpu.VMEM((464, DEPTH), BF16), pltpu.VMEM((464, DEPTH), BF16)]
    columns = [pltpu.VMEM((464, DEPTH), BF16), pltpu.VMEM((464, DEPTH), BF16)]
    above = send(down, TM, 1, False)
    below = send(up, TM, -1, False)
    *inside, inner = call(
        inside_kernel,
        (
            shape((384, CHANNELS)),
            shape((384, CHANNELS), F32),
            shape((384, 128), F32),
            shape((384, CHANNELS)),
        ),
        columns,
        1_200_000_000,
        12,
        own,
        weights[0],
    )
    inners = [inner] + [send(inner, "tm_0", step, True) for step in (1, 2, 3)]
    pred, *outers, mid, grad = call(
        second_kernel,
        (
            shape((CELLS, PIX)),
            *[shape((400, 128))] * 4,
            shape((CELLS, CHANNELS), F32),
            shape((416, CHANNELS)),
        ),
        [
            *columns,
            pltpu.VMEM((448, CHANNELS), BF16),
            pltpu.VMEM((416, CHANNELS), F32),
            pltpu.VMEM((416, 128), F32),
            pltpu.VMEM((32, CHANNELS), BF16),
        ],
        3_500_000_000,
        22,
        above,
        own,
        below,
        weights[0],
        *inside,
        weights[1],
        head_weight,
        aim,
    )
    outers[1:] = [send(outers[step], "tm_0", step, True) for step in (1, 2, 3)]
    picked = call(
        tail_kernel,
        shape((shards * 8, CHANNELS), F32),
        [],
        1_200_000_000,
        12,
        grad,
        mid,
        weights[0],
        chosen,
    )
    summed = call(
        own_kernel,
        shape((CHANNELS, 9 * 128), F32),
        [pltpu.VMEM((416, 9 * 128), BF16)],
        400_000_000,
        12,
        inner,
        outers[0],
    )
    turned = call(turn_kernel, shape((3, CHANNELS, 384)), [], 300_000_000, 8, *inners[1:])
    terms = call(
        weight_kernel,
        shape((shards, 16, CHANNELS)),
        [pltpu.VMEM((3, 416, 9 * 128), BF16), pltpu.VMEM((9 * CHANNELS + 8, 128), F32)],
        1_500_000_000,
        16,
        summed,
        turned,
        *outers[1:],
        picked,
    )
    terms = lax.all_to_all(terms, TM_FREQ, split_axis=0, concat_axis=0, tiled=True)
    token_grad, conv_grad = call(
        finish_kernel,
        (shape((visible, in_weight.shape[0]), F32), shape((54, 2, CHANNELS), F32)),
        [],
        80_000_000,
        6,
        terms,
        where_to,
        in_weight,
    )
    conv_grad = conv_grad.transpose(1, 0, 2)
    pred = lax.dynamic_slice_in_dim(pred.reshape(ROWS, COLS, PIX), core * half, half, axis=1)
    return (pred, token_grad, conv_grad)


def solution(mesh):
    split = Mesh(
        mesh.devices.reshape(4, 8, mesh.shape["freq"], mesh.shape["rec"]),
        ("tm_0", "tm_1", "freq", "rec"),
    )
    placed = (
        P(REC_TM_FREQ, None),
        P(None, REC_TM_FREQ),
        P(REC_TM, "freq"),
        P(REC_TM, "freq", None),
        P(),
        P(),
        P(),
        P(),
    )
    return jax.shard_map(
        per_device,
        mesh=split,
        in_specs=placed,
        out_specs=(P(REC_TM, "freq", None), P(REC_TM_FREQ, None), P("rec", TM_FREQ, None)),
        check_vma=False,
    )
```

```python
import jax
import jax.numpy as jnp
from jax import lax
from jax.experimental import pallas as pl
from jax.experimental.pallas import tpu as pltpu
from jax.sharding import Mesh
from jax.sharding import PartitionSpec as P


TM = ("tm_0", "tm_1")
TM_FREQ = ("tm_0", "tm_1", "freq")
REC_TM_FREQ = ("rec", "tm_0", "tm_1", "freq")
REC_TM = ("rec", "tm_0", "tm_1")

F32 = jnp.float32
BF16 = jnp.bfloat16
ROWS = 50
COLS = 8
CELLS = ROWS * COLS
CHANNELS = 384
DEPTH = 3 * CHANNELS
PIX = 256
ERF_SCALE = 0.7071067811865476
PDF_SCALE = 0.3989422804014327
ERF_TOP = (
    0.00022905065861350646,
    0.0034082910107109506,
    0.050955695062380861,
    0.18520832239976145,
    1.128379143519084,
)
ERF_BOTTOM = (
    -1.1791602954361697e-7,
    0.000023547966471313185,
    0.0010179625278914885,
    0.014070470171167667,
    0.11098505178285362,
    0.49746925110067538,
    1.0,
)


def horner(value, factors):
    total = jnp.full_like(value, factors[0])
    for factor in factors[1:]:
        total = total * value + factor
    return total


def erf(value):
    bounded = jnp.clip(value, -3.7439211627767994, 3.7439211627767994)
    square = bounded * bounded
    return bounded * horner(square, ERF_TOP) / horner(square, ERF_BOTTOM)


def half_erf(unit):
    return 0.5 * (1.0 + erf(unit * ERF_SCALE))


def column_shifted(value):
    cells, channels = value.shape
    grid = value.reshape(cells // 8, 8, channels)
    column = lax.broadcasted_iota(jnp.int32, grid.shape, 1)
    lower = jnp.where(column == 0, 0.0, pltpu.roll(grid, 1, axis=1))
    upper = jnp.where(column == 7, 0.0, pltpu.roll(grid, 7, axis=1))
    return lower.reshape(value.shape), value, upper.reshape(value.shape)


def store_columns(value, even, odd):
    cells, channels = value.shape
    for part, shifted in enumerate(column_shifted(value)):
        lanes = slice(part * channels, (part + 1) * channels)
        even[0:cells, lanes] = shifted.astype(BF16)
        odd[0 : cells - 8, lanes] = shifted[8:].astype(BF16)


def conv_taps(windows, taps):
    summed = None
    for part, window in enumerate(windows):
        term = jnp.dot(
            window, taps[0, part * DEPTH : (part + 1) * DEPTH], preferred_element_type=F32
        )
        summed = term if summed is None else summed + term
    return summed


def conv_back(grad, taps, cells):
    summed = None
    for row_off in range(3):
        start = 8 * (2 - row_off)
        term = lax.dot_general(
            grad[start : start + cells].astype(BF16),
            taps[0, row_off * DEPTH : (row_off + 1) * DEPTH],
            (((1,), (1,)), ((), ())),
            preferred_element_type=F32,
        )
        summed = term if summed is None else summed + term
    grid = (cells // 8, 8, CHANNELS)
    column = lax.broadcasted_iota(jnp.int32, grid, 1)
    first = summed[:, 0:CHANNELS].reshape(grid)
    last = summed[:, 2 * CHANNELS :].reshape(grid)
    total = jnp.where(column == 7, 0.0, pltpu.roll(first, 7, axis=1))
    total += jnp.where(column == 0, 0.0, pltpu.roll(last, 1, axis=1))
    return summed[:, CHANNELS : 2 * CHANNELS] + total.reshape(cells, CHANNELS)


def quarters(value):
    tiles = [value[:, 128 * part : 128 * (part + 1)] for part in range(3)]
    lane = lax.broadcasted_iota(jnp.int32, tiles[0].shape, 1)
    one = jnp.where(lane < 32, pltpu.roll(tiles[0], 32, axis=1), pltpu.roll(tiles[1], 32, axis=1))
    two = jnp.where(lane < 64, pltpu.roll(tiles[1], 64, axis=1), pltpu.roll(tiles[2], 64, axis=1))
    return tiles[0], one, two, pltpu.roll(tiles[2], 96, axis=1)


def joined(parts):
    lane = lax.broadcasted_iota(jnp.int32, parts[0].shape, 1)
    one = pltpu.roll(parts[1], 96, axis=1)
    two = pltpu.roll(parts[2], 64, axis=1)
    three = pltpu.roll(parts[3], 32, axis=1)
    tiles = (
        jnp.where(lane < 96, parts[0], one),
        jnp.where(lane < 64, one, two),
        jnp.where(lane < 32, two, three),
    )
    return jnp.concatenate(tiles, axis=1)


def normed(conv_out):
    center = conv_out - jnp.mean(conv_out, axis=-1, keepdims=True)
    scale = lax.rsqrt(jnp.mean(center * center, axis=-1, keepdims=True) + 1e-05)
    return center * scale, scale


def slope_of(unit, half):
    return half + unit * (PDF_SCALE * jnp.exp(-0.5 * unit * unit))


def pull_back(unit, scale, slope, gradient):
    grad = gradient * slope
    mean = jnp.mean(grad, axis=-1, keepdims=True)
    along = jnp.mean(grad * unit, axis=-1, keepdims=True)
    return scale * (grad - mean - unit * along)


def rows_valid(row):
    row = row + lax.axis_index(TM) * ROWS
    return (row >= 0) & (row < lax.axis_size(TM) * ROWS)


def row_number(cells):
    return lax.shift_right_logical(lax.broadcasted_iota(jnp.int32, (cells, 1), 0), 3)


def pack_kernel(tokens, placement, in_weight, packed, where_out):
    count = tokens.shape[0]
    rows = placement[0:1, :].astype(F32)
    cols = placement[1:2, :].astype(F32)
    tile_row = jnp.floor((rows + 0.5) * (1.0 / ROWS))
    tile = tile_row * 2.0 + jnp.where(cols >= 4.0, 1.0, 0.0)
    down = lax.broadcasted_iota(jnp.int32, (count, count), 0)
    across = lax.broadcasted_iota(jnp.int32, (count, count), 1)

    def column(value):
        return jnp.sum(jnp.where(down == across, value, 0.0), axis=1, keepdims=True)

    earlier = jnp.where((column(tile) == tile) & (down < across), 1.0, 0.0)
    where_to = tile * 2.0 + jnp.sum(earlier, axis=0, keepdims=True)
    where_out[...] = jnp.broadcast_to(column(where_to), where_out.shape)
    index = lax.broadcasted_iota(jnp.int32, (packed.shape[0], 1), 0)
    wanted = lax.shift_right_logical(index, 4) * 4 + (index & 3)
    match = jnp.where(wanted.astype(F32) == where_to, 1.0, 0.0).astype(BF16)
    proj = jnp.dot(tokens[...], in_weight[...], preferred_element_type=F32).astype(BF16)
    lane = lax.broadcasted_iota(jnp.int32, (count, 128), 1)
    notes = jnp.where(lane == 1, column(cols), jnp.where(lane == 2, 1.0, 0.0))
    notes = jnp.where(lane == 0, column(rows - tile_row * ROWS), notes).astype(BF16)
    low = jnp.dot(match, proj[:, 0:256], preferred_element_type=F32)
    rest = jnp.concatenate([proj[:, 256:384], notes], axis=1)
    high = jnp.dot(match, rest, preferred_element_type=F32)
    packed[...] = jnp.where((index & 4) == 0, low, high).astype(BF16)


def order_kernel(own_aim, other_aim, aim_out):
    core = lax.axis_index("freq")
    number = lax.broadcasted_iota(jnp.int32, (CELLS, 1), 0)
    far = (lax.shift_right_logical(number, 2) & 1) != core
    source = lax.shift_right_logical(number, 3) * 4 + (number & 3) + jnp.where(far, CELLS // 2, 0)
    order = lax.broadcasted_iota(jnp.int32, (CELLS, CELLS), 1) == source
    aim_out[...] = jnp.dot(
        jnp.where(order, 1.0, 0.0).astype(BF16),
        jnp.concatenate([own_aim[...].astype(F32), other_aim[...].astype(F32)], axis=0).astype(BF16),
        preferred_element_type=F32,
    ).astype(BF16)


def place_kernel(arrived, aim, token, x_out, down_out, up_out, chosen_out):
    core = lax.axis_index("freq")
    slots = arrived.shape[0]
    notes = arrived[:, 128:256].astype(F32).reshape(slots // 8, 8, 128)
    within = lax.broadcasted_iota(jnp.int32, notes.shape, 1)
    notes = jnp.where(within >= 4, notes, pltpu.roll(notes, 4, axis=1)).reshape(slots, 128)
    cell = jnp.where(notes[:, 2:3] == 1.0, notes[:, 0:1] * 8.0 + notes[:, 1:2], -1.0)
    lane = lax.broadcasted_iota(jnp.int32, (slots, CELLS), 1)
    index = lax.broadcasted_iota(jnp.int32, (slots, CELLS), 0)
    hit = lane == cell.astype(jnp.int32)

    def pick(flag):
        return lax.dot_general(
            jnp.where(hit & flag, 1.0, 0.0).astype(BF16),
            arrived[...],
            (((0,), (0,)), ((), ())),
            preferred_element_type=F32,
        )

    placed = jnp.concatenate([pick((index & 4) == 0), pick((index & 4) == 4)[:, 0:128]], axis=1)
    masked = aim[:, PIX : PIX + 1] == 1.0
    x = jnp.where(masked, token[...].astype(F32), placed).astype(BF16)
    x_out[...] = x
    down_out[0:32] = x[CELLS - 32 :]
    down_out[32:48] = aim[CELLS - 16 :]
    up_out[0:32] = x[0:32]
    up_out[32:48] = aim[0:16]
    spread = jnp.broadcast_to(cell, (slots, 128)).reshape(slots // 8, 8, 128)
    first = jnp.sum(jnp.where(within == 4 + 2 * core, spread, 0.0), axis=1, keepdims=True)
    second = jnp.sum(jnp.where(within == 5 + 2 * core, spread, 0.0), axis=1, keepdims=True)
    spread = jnp.where(within == 6, first, jnp.where(within == 7, second, -1.0))
    spread = spread.reshape(slots, 128)
    chosen_out[...] = jnp.where(lane == spread[:, 0:1].astype(jnp.int32), 1.0, 0.0).astype(BF16)


def inside_kernel(
    own, weight, active_out, unit_out, scale_out, slope_out, share_out, even, odd
):
    source = own[...].astype(F32)
    store_columns(source, even, odd)
    unit, scale = normed(conv_taps((even[0:384], odd[0:384], even[16:400]), weight))
    unit_out[...] = unit
    scale_out[...] = jnp.broadcast_to(scale, scale_out.shape)
    half = half_erf(unit)
    slope_out[...] = slope_of(unit, half)
    active = source[8:392] + unit * half
    active_out[...] = active.astype(BF16)
    share_out[...] = jnp.where(lax.axis_index("freq") == 1, active, source[8:392]).astype(BF16)


def border_rows(
    above, own, below, weight, active_in, unit_in, scale_in, slope_in,
    active_out, unit_out, scale_out, slope_out, share_out, even, odd,
):
    upper, lower = above[0:32].astype(F32), below[0:32].astype(F32)
    border = jnp.concatenate(
        [upper, own[0:16].astype(F32), own[384:400].astype(F32), lower], axis=0
    )
    store_columns(border, even, odd)
    windows = (
        jnp.concatenate([even[0:32], even[48:80]], axis=0),
        jnp.concatenate([odd[0:32], odd[48:80]], axis=0),
        jnp.concatenate([even[16:48], even[64:96]], axis=0),
    )
    unit, scale = normed(conv_taps(windows, weight))
    half = half_erf(unit)
    slope = slope_of(unit, half)
    slope_out[0:16] = slope[16:32]
    slope_out[16:400] = slope_in[...]
    slope_out[400:416] = slope[32:48]
    edge = jnp.concatenate([border[8:40], border[56:88]], axis=0) + unit * half
    number = row_number(64)
    number = jnp.where(number < 4, number - 3, number + 45)
    edge = jnp.where(rows_valid(number), edge, 0.0)
    active_out[0:32] = edge[0:32].astype(BF16)
    active_out[32:416] = active_in[...]
    active_out[416:448] = edge[32:64].astype(BF16)
    unit_out[0:16] = unit[16:32]
    unit_out[16:400] = unit_in[...]
    unit_out[400:416] = unit[32:48]
    scale = jnp.broadcast_to(scale, (64, 128))
    scale_out[0:16] = scale[16:32]
    scale_out[16:400] = scale_in[...]
    scale_out[400:416] = scale[32:48]
    source = jnp.concatenate(
        [upper[24:32], own[0:8].astype(F32), own[392:400].astype(F32), lower[0:8]], axis=0
    )
    share_out[...] = jnp.where(lax.axis_index("freq") == 1, edge[16:48], source).astype(BF16)


def second_kernel(
    above, own, below, first_weight, active_in, unit_in, scale_in, slope_in,
    weight, head, aim_ref,
    pred, share_own, share_one, share_two, share_three, mid_out, grad_out,
    even, odd, active_ref, unit_ref, scale_ref, slope_ref, border,
):
    border_rows(
        above, own, below, first_weight, active_in, unit_in, scale_in, slope_in,
        active_ref, unit_ref, scale_ref, slope_ref, border, even, odd,
    )
    active = active_ref[...].astype(F32)
    store_columns(active, even, odd)
    unit, scale = normed(conv_taps((even[0:432], odd[0:432], even[16:448]), weight))
    half = half_erf(unit)
    slope = slope_of(unit, half)
    top = (active[8:440] + unit * half).astype(BF16)
    guess = jnp.dot(top, head[...], preferred_element_type=F32)
    pred[...] = guess[16:416].astype(BF16)
    aim = jnp.concatenate([above[32:48], aim_ref[...], below[32:48]], axis=0)
    misfit = jnp.where(
        aim[:, PIX : PIX + 1] == 1.0, (guess - aim[:, 0:PIX].astype(F32)) * 0.0625, 0.0
    ).astype(BF16)
    grad_top = lax.dot_general(
        misfit, head[...], (((1,), (1,)), ((), ())), preferred_element_type=F32
    )
    grad_two = pull_back(unit, scale, slope, grad_top)
    grad_mid = grad_top[8:424] + conv_back(grad_two, weight, 416)
    grad_one = pull_back(unit_ref[...], scale_ref[:, 0:1], slope_ref[...], grad_mid)
    grad_one = jnp.where(rows_valid(row_number(416) - 1), grad_one, 0.0)
    grad_out[...] = grad_one.astype(BF16)
    mid_out[...] = grad_mid[8:408]
    share = jnp.where(lax.axis_index("freq") == 1, grad_two[16:416], grad_one[8:408])
    pieces = quarters(share)
    lane = lax.broadcasted_iota(jnp.int32, (CELLS, 128), 1)
    for step, share_out in enumerate((share_own, share_one, share_two, share_three)):
        quarter = (lax.axis_index("tm_0") + step) & 3
        piece = jnp.where(quarter == 0, pieces[0], pieces[1])
        piece = jnp.where(quarter >= 2, jnp.where(quarter == 2, pieces[2], pieces[3]), piece)
        rest = piece[304:400]
        side = [pltpu.roll(rest, 96 - 32 * part, axis=1) for part in range(3)]
        side = jnp.concatenate([*side, jnp.zeros((16, 128), F32)], axis=0)
        share_out[0:304] = jnp.where(lane[0:304] < 96, piece[0:304], side).astype(BF16)
        for part in range(3):
            share_out[304 + 32 * part : 304 + 32 * (part + 1)] = border[
                :, 128 * part : 128 * (part + 1)
            ]


def tail_kernel(grad_ref, mid_ref, weight, chosen, out):
    grad_cells = mid_ref[...] + conv_back(grad_ref[...].astype(F32), weight, CELLS)
    out[...] = jnp.dot(chosen[...], grad_cells.astype(BF16), preferred_element_type=F32)


def turn_kernel(*refs):
    for part in range(3):
        refs[3][part] = refs[part][...].astype(F32).T.astype(BF16)


def chip_term(turned, outer, moved):
    packed = outer[0:304].astype(F32)
    lane = lax.broadcasted_iota(jnp.int32, (96, 128), 1)
    rest = jnp.where(lane < 96, pltpu.roll(packed[192:288], 96, axis=1), 0.0)
    rest = jnp.where(lane < 64, pltpu.roll(packed[96:192], 64, axis=1), rest)
    rest = jnp.where(lane < 32, pltpu.roll(packed[0:96], 32, axis=1), rest)
    lane = lax.broadcasted_iota(jnp.int32, (304, 128), 1)
    gradient = jnp.concatenate([jnp.where(lane < 96, packed, 0.0), rest], axis=0)
    low, middle, high = column_shifted(gradient)
    for row_off in range(3):
        for col_off, piece in enumerate((high, middle, low)):
            rows = [piece]
            if row_off:
                rows.insert(0, jnp.zeros((8 * row_off, 128), F32))
            if row_off < 2:
                rows.append(jnp.zeros((16 - 8 * row_off, 128), F32))
            rows = jnp.concatenate(rows, axis=0).astype(BF16)
            tap = 3 * row_off + col_off
            lanes = slice(tap * 128, (tap + 1) * 128)
            moved[0:384, lanes] = rows[16:400]
            moved[384:400, lanes] = rows[0:16]
            moved[400:416, lanes] = rows[400:416]
    border = jnp.concatenate([outer[304 + 32 * k : 336 + 32 * k] for k in range(3)], axis=1)
    inner = jnp.concatenate([turned, border.astype(F32).T.astype(BF16)], axis=1)
    return jnp.dot(inner, moved[...], preferred_element_type=F32)


def own_kernel(inner, outer, out, moved):
    out[...] = chip_term(inner[...].astype(F32).T.astype(BF16), outer, moved)


def weight_kernel(summed_ref, turned, *refs):
    outers, picked = refs[0:3], refs[3]
    out, moved, total = refs[4:]
    summed = summed_ref[...]
    for part in range(3):
        summed = summed + chip_term(turned[part], outers[part], moved.at[part])
    for tap in range(9):
        total[tap * CHANNELS : (tap + 1) * CHANNELS] = summed[:, tap * 128 : (tap + 1) * 128]
    total[9 * CHANNELS :] = jnp.zeros((8, 128), F32)
    row = lax.broadcasted_iota(jnp.int32, (16, CHANNELS), 0)
    for shard in range(64):
        start = 54 * shard
        packed = joined([total[start + 14 * part : start + 14 * part + 16] for part in range(4)])
        back = picked[8 * shard : 8 * shard + 8]
        packed = jnp.where(row >= 14, jnp.concatenate([back, back], axis=0), packed)
        out[shard] = packed.astype(BF16)


def finish_kernel(arrived, where_ref, in_weight, token_out, conv_out):
    count = where_ref.shape[0]
    rows = arrived.shape[0] * 16
    index = lax.broadcasted_iota(jnp.int32, (count, rows), 1)
    within = index & 15
    slot = lax.shift_right_logical(index, 4) * 2 + within - 14
    hit = (where_ref[:, 0:1].astype(jnp.int32) == slot) & (within >= 14)
    grad_proj = jnp.dot(
        jnp.where(hit, 1.0, 0.0).astype(BF16),
        arrived[...].reshape(rows, CHANNELS),
        preferred_element_type=F32,
    ).astype(BF16)
    token_out[...] = lax.dot_general(
        grad_proj, in_weight[...], (((1,), (1,)), ((), ())), preferred_element_type=F32
    )
    for layer in range(2):
        parts = []
        for peer in range(4):
            summed = None
            for near in range(8):
                term = arrived[16 * peer + 2 * near + layer].astype(F32)
                summed = term if summed is None else summed + term
            parts.append(quarters(summed))
        for group in range(4):
            height = min(14, 54 - 14 * group)
            wide = joined([parts[peer][group] for peer in range(4)])
            conv_out[14 * group : 14 * group + height, layer] = wide[0:height]


VMEM = pl.BlockSpec(memory_space=pltpu.VMEM)


def call(kernel, shapes, scratch, cost, limit, *operands):
    return pl.pallas_call(
        kernel,
        out_shape=shapes,
        in_specs=[VMEM] * len(operands),
        out_specs=jax.tree.map(lambda _: VMEM, shapes),
        scratch_shapes=scratch,
        compiler_params=pltpu.CompilerParams(vmem_limit_bytes=limit << 20),
        cost_estimate=pl.CostEstimate(
            flops=cost, bytes_accessed=cost // 400, transcendentals=0
        ),
    )(*operands)


def shape(dims, dtype=BF16):
    return jax.ShapeDtypeStruct(dims, dtype)


def send(value, axis, step, wrap):
    count = lax.axis_size(axis)
    pairs = [(i, (i + step) % count) for i in range(count)]
    if not wrap:
        pairs = [(i, i + step) for i in range(count) if 0 <= i + step < count]
    return lax.ppermute(value, axis, pairs)


def per_device(
    tokens, placement, patch_mask, targets, in_weight, mask_token, conv_weight, head_weight
):
    shards = lax.axis_size(TM_FREQ)
    core = lax.axis_index("freq")
    visible = tokens.shape[0]
    half = patch_mask.shape[1]

    packed, where_to = call(
        pack_kernel,
        (shape((shards * 8, 256)), shape((visible, 128), F32)),
        [],
        80_000_000,
        62,
        tokens,
        placement,
        in_weight,
    )
    arrived = lax.all_to_all(packed, TM_FREQ, split_axis=0, concat_axis=0, tiled=True)
    flags = jnp.broadcast_to((patch_mask == 1)[:, :, None], (*patch_mask.shape, 128))
    aim = jnp.concatenate([targets, flags.astype(BF16)], axis=2).reshape(-1, PIX + 128)

    other = send(aim, "freq", 1, True)
    aim = call(order_kernel, shape((CELLS, PIX + 128)), [], 200_000_000, 8, aim, other)
    weights = [conv_weight[layer : layer + 1] for layer in range(2)]

    own, down, up, chosen = call(
        place_kernel,
        (
            shape((CELLS, CHANNELS)),
            shape((48, CHANNELS)),
            shape((48, CHANNELS)),
            shape((shards * 8, CELLS)),
        ),
        [],
        300_000_000,
        8,
        arrived,
        aim,
        mask_token[None, :],
    )
    columns = [pltpu.VMEM((464, DEPTH), BF16), pltpu.VMEM((464, DEPTH), BF16)]
    columns = [pltpu.VMEM((464, DEPTH), BF16), pltpu.VMEM((464, DEPTH), BF16)]
    above = send(down, TM, 1, False)
    below = send(up, TM, -1, False)
    *inside, inner = call(
        inside_kernel,
        (
            shape((384, CHANNELS)),
            shape((384, CHANNELS), F32),
            shape((384, 128), F32),
            shape((384, CHANNELS), F32),
            shape((384, CHANNELS)),
        ),
        columns,
        1_200_000_000,
        12,
        own,
        weights[0],
    )
    inners = [inner] + [send(inner, "tm_0", step, True) for step in (1, 2, 3)]
    pred, *outers, mid, grad = call(
        second_kernel,
        (
            shape((CELLS, PIX)),
            *[shape((400, 128))] * 4,
            shape((CELLS, CHANNELS), F32),
            shape((416, CHANNELS)),
        ),
        [
            *columns,
            pltpu.VMEM((448, CHANNELS), BF16),
            pltpu.VMEM((416, CHANNELS), F32),
            pltpu.VMEM((416, 128), F32),
            pltpu.VMEM((416, CHANNELS), F32),
            pltpu.VMEM((32, CHANNELS), BF16),
        ],
        3_500_000_000,
        22,
        above,
        own,
        below,
        weights[0],
        *inside,
        weights[1],
        head_weight,
        aim,
    )
    outers[1:] = [send(outers[step], "tm_0", step, True) for step in (1, 2, 3)]
    picked = call(
        tail_kernel,
        shape((shards * 8, CHANNELS), F32),
        [],
        1_200_000_000,
        12,
        grad,
        mid,
        weights[0],
        chosen,
    )
    summed = call(
        own_kernel,
        shape((CHANNELS, 9 * 128), F32),
        [pltpu.VMEM((416, 9 * 128), BF16)],
        400_000_000,
        12,
        inner,
        outers[0],
    )
    turned = call(turn_kernel, shape((3, CHANNELS, 384)), [], 300_000_000, 8, *inners[1:])
    terms = call(
        weight_kernel,
        shape((shards, 16, CHANNELS)),
        [pltpu.VMEM((3, 416, 9 * 128), BF16), pltpu.VMEM((9 * CHANNELS + 8, 128), F32)],
        1_500_000_000,
        16,
        summed,
        turned,
        *outers[1:],
        picked,
    )
    terms = lax.all_to_all(terms, TM_FREQ, split_axis=0, concat_axis=0, tiled=True)
    token_grad, conv_grad = call(
        finish_kernel,
        (shape((visible, in_weight.shape[0]), F32), shape((54, 2, CHANNELS), F32)),
        [],
        80_000_000,
        6,
        terms,
        where_to,
        in_weight,
    )
    conv_grad = conv_grad.transpose(1, 0, 2)
    pred = lax.dynamic_slice_in_dim(pred.reshape(ROWS, COLS, PIX), core * half, half, axis=1)
    return (pred, token_grad, conv_grad)


def solution(mesh):
    split = Mesh(
        mesh.devices.reshape(4, 8, mesh.shape["freq"], mesh.shape["rec"]),
        ("tm_0", "tm_1", "freq", "rec"),
    )
    placed = (
        P(REC_TM_FREQ, None),
        P(None, REC_TM_FREQ),
        P(REC_TM, "freq"),
        P(REC_TM, "freq", None),
        P(),
        P(),
        P(),
        P(),
    )
    return jax.shard_map(
        per_device,
        mesh=split,
        in_specs=placed,
        out_specs=(P(REC_TM, "freq", None), P(REC_TM_FREQ, None), P("rec", TM_FREQ, None)),
        check_vma=False,
    )
```
